32 devices in a mesh: gx: 8 (over z, x), gy: 4 (over y, core).
Axes of the slice: x: 2, y: 2, z: 4, core: 2. Of those that a mesh axis runs over, the one named last changes fastest.
Arguments:
- coarse_state: float32 [5, 256, 1024], P(None, 'gx', 'gy'), may hold values from -6 to 6
- fine_state: float32 [32, 5, 32, 512], P(('gx', 'gy')), may hold values from -6 to 6
- slot_site: int32 [32, 2], P(('gx', 'gy')), may hold values from 0 to 3, as said below
- box_live: int32 [32], P(('gx', 'gy')), may hold values 0 or 1
Outputs:
- coarse_out: float32 [5, 256, 1024], P(None, 'gx', 'gy')
- fine_out: float32 [32, 5, 32, 512], P(('gx', 'gy'))
The draws below stay inside these ranges and needn't reach their ends.
Inputs may be any that keep to these rules, and one draw needn't show every extreme that they name: `slot_site`: within each group of 4 devices that share a gx index, slots of the group and box positions of the group's coarse blocks are matched one to one; column 0 is the gy index of the block, column 1 the position number, 0 to 0.
All inputs are finite; a program needn't handle non-finite values. No bound on the sum of `box_live` on one device may be relied on, other than what follows from the above.
Results may differ from the reference program's by a relative error of at most 0.000088.
Values sent between devices are 32-bit elements; how exact they have to be, the bound alone decides.
No kernel may reach another device: no remote copies, remote signals or barrier semaphores. Data moves between devices by JAX's collectives and lax.ppermute only.
A program may use at most 64 MiB of HBM per device.

```python
import jax
import jax.numpy as jnp
from jax import lax

NVAR = 5
CX = 32
CY = 32
NZ = 8
PATCH = 16
BOXES = 1
NX = 256
NY = 128
N_GX = 8
N_GY = 4


def draw_slot_site(key, part):
    groups = NX // CX
    per_group = NY // CY * BOXES
    scores = jax.random.randint(key, (groups, per_group), 0, 1 << 20) * per_group + jnp.arange(per_group, dtype=jnp.int32)[None, :]
    matched = jnp.argsort(scores, axis=1).astype(jnp.int32)
    parent = matched // BOXES
    position = matched % BOXES
    return jnp.stack([parent, position], axis=-1).reshape(groups * per_group, 2).astype(jnp.int32)


def with_ends(array, rng, least, largest):
    place = [jax.random.randint(jax.random.fold_in(rng, axis), (), 0, length) for axis, length in enumerate(array.shape)]
    widest = array.shape.index(max(array.shape))
    next_to = place[:widest] + [(place[widest] + 1) % array.shape[widest]] + place[widest + 1:]
    return array.at[tuple(place)].set(least).at[tuple(next_to)].set(largest)


def shard_levels(stream_key, extent, cuts, low, high):
    level = 1.0
    for dim, blocks in cuts:
        heights = jax.random.uniform(jax.random.fold_in(jax.random.fold_in(stream_key, 6), dim), (blocks,), jnp.float32, low / len(cuts), high / len(cuts))
        level = level * jnp.repeat(jnp.exp(heights), extent[dim] // blocks).reshape((-1,) + (1,) * (len(extent) - 1 - dim))
    return level


def scatter_about(stream_key, dims, scale, reach, shards=(), kind=jnp.bfloat16):
    entries = scale * jax.random.normal(stream_key, dims, jnp.float32)
    if shards:
        entries = entries * shard_levels(stream_key, dims, shards, -0.22, 0.18)
    return jnp.clip(entries, -reach, reach).astype(kind)


def setup_inputs(seed: int = 0) -> dict:
    seeds = jax.random.split(jax.random.key(seed), 5)
    return {
        "coarse_state": scatter_about(seeds[0], (NVAR, NX, NY * NZ), 1.0, 6.0, ((1, 8), (2, 4)), jnp.float32),
        "fine_state": scatter_about(seeds[1], (N_GX * N_GY * BOXES, NVAR, 2 * PATCH, 4 * PATCH * NZ), 1.0, 6.0, ((0, 32),), jnp.float32),
        "slot_site": draw_slot_site(jax.random.fold_in(seeds[4], 71), 0),
        "box_live": with_ends((jax.random.randint(seeds[3], (N_GX * N_GY * BOXES,), 0, 2) < 1).astype(jnp.int32), jax.random.fold_in(seeds[3], 1), 0, 1),
    }


courant = 0.2
drift = (0.5, 0.3, 0.2)
sound_sq = 1.0
signal = (1.5, 1.3, 1.2)


def minmod(first, second):
    return jnp.maximum(jnp.minimum(first, second), 0.0) + jnp.minimum(jnp.maximum(first, second), 0.0)


def physical(values, direction):
    normal = values[1 + direction]
    pieces = []
    for member in range(5):
        summand = drift[direction] * values[member]
        if member == 0:
            summand = summand + normal
        if member == 1 + direction:
            summand = summand + values[4]
        if member == 4:
            summand = summand + sound_sq * normal
        pieces.append(summand)
    return jnp.stack(pieces)


def face_flux(values, axis_id, direction):
    length = values.shape[axis_id]
    left_cell = lax.slice_in_dim(values, 0, length - 2, axis=axis_id)
    centre = lax.slice_in_dim(values, 1, length - 1, axis=axis_id)
    right_cell = lax.slice_in_dim(values, 2, length, axis=axis_id)
    slopes = minmod(centre - left_cell, right_cell - centre)
    inner_len = length - 2
    left_face = lax.slice_in_dim(centre, 0, inner_len - 1, axis=axis_id) + 0.5 * lax.slice_in_dim(slopes, 0, inner_len - 1, axis=axis_id)
    right_face = lax.slice_in_dim(centre, 1, inner_len, axis=axis_id) - 0.5 * lax.slice_in_dim(slopes, 1, inner_len, axis=axis_id)
    return 0.5 * (physical(left_face, direction) + physical(right_face, direction)) - 0.5 * signal[direction] * (right_face - left_face)


def divergence(fluxes, axis_id):
    length = fluxes.shape[axis_id]
    return lax.slice_in_dim(fluxes, 1, length, axis=axis_id) - lax.slice_in_dim(fluxes, 0, length - 1, axis=axis_id)


def wrap_z(values):
    return jnp.concatenate([values[..., -2:], values, values[..., :2]], axis=-1)


def advance(padded, interior):
    flux_x = face_flux(padded[:, :, 2:-2, :], 1, 0)
    flux_y = face_flux(padded[:, 2:-2, :, :], 2, 1)
    flux_z = face_flux(wrap_z(interior), 3, 2)
    change = divergence(flux_x, 1) + divergence(flux_y, 2) + divergence(flux_z, 3)
    return interior - courant * change, flux_x, flux_y


def inject(fine, window):
    spread = jnp.repeat(jnp.repeat(jnp.repeat(window, 2, axis=1), 2, axis=2), 2, axis=3)
    return spread.at[:, 2:2 + 2 * PATCH, 2:2 + 2 * PATCH, :].set(fine)


def coarsen_face(fluxes):
    shape_now = fluxes.shape
    return fluxes.reshape(shape_now[0], shape_now[1] // 2, 2, shape_now[2] // 2, 2).mean(axis=(2, 4))


def fine_cycle(fine, early, later):
    first, flux_x_one, flux_y_one = advance(inject(fine, early), fine)
    second, flux_x_two, flux_y_two = advance(inject(first, 0.5 * (early + later)), first)
    edge = 2 * PATCH
    registers = [
        0.5 * (coarsen_face(flux_x_one[:, 0]) + coarsen_face(flux_x_two[:, 0])),
        0.5 * (coarsen_face(flux_x_one[:, edge]) + coarsen_face(flux_x_two[:, edge])),
        0.5 * (coarsen_face(flux_y_one[:, :, 0]) + coarsen_face(flux_y_two[:, :, 0])),
        0.5 * (coarsen_face(flux_y_one[:, :, edge]) + coarsen_face(flux_y_two[:, :, edge])),
    ]
    shape_now = second.shape
    average = second.reshape(shape_now[0], shape_now[1] // 2, 2, shape_now[2] // 2, 2, shape_now[3] // 2, 2).mean(axis=(2, 4, 6))
    return second, jnp.concatenate([average, jnp.stack(registers, axis=1)], axis=1)


def reference(coarse_state, fine_state, slot_site, box_live):
    coarse_state = coarse_state.reshape(NVAR, NX, NY, NZ)
    fine_state = fine_state.reshape(fine_state.shape[0], NVAR, 2 * PATCH, 2 * PATCH, 2 * NZ)
    padded = jnp.pad(coarse_state, ((0, 0), (2, 2), (2, 2), (0, 0)), mode="wrap")
    coarse_new, flux_x, flux_y = advance(padded, coarse_state)
    per_row = CY // 32
    per_group = N_GY * BOXES
    slot_ids = jnp.arange(fine_state.shape[0], dtype=jnp.int32)
    group = slot_ids // per_group
    parent = slot_site[:, 0].astype(jnp.int32)
    position = slot_site[:, 1].astype(jnp.int32)
    anchor_x = (group * CX + 32 * (position // per_row) + 8).astype(jnp.int32)
    anchor_y = (parent * CY + 32 * (position % per_row) + 8).astype(jnp.int32)
    live = box_live[((group * N_GY + parent) * BOXES + position).astype(jnp.int32)].astype(coarse_state.dtype)
    nought = jnp.zeros((), jnp.int32)

    def one_box(items):
        fine, start_x, start_y = items
        early = lax.dynamic_slice(coarse_state, (nought, start_x - 1, start_y - 1, nought), (NVAR, PATCH + 2, PATCH + 2, NZ))
        later = lax.dynamic_slice(coarse_new, (nought, start_x - 1, start_y - 1, nought), (NVAR, PATCH + 2, PATCH + 2, NZ))
        return fine_cycle(fine, early, later)

    fine_out, payload = lax.map(one_box, (fine_state, anchor_x, anchor_y))
    offsets = jnp.arange(PATCH, dtype=jnp.int32)
    rows_x = anchor_x[:, None] + offsets[None, :]
    rows_y = anchor_y[:, None] + offsets[None, :]
    present = live > 0
    covered = coarse_new[:, rows_x[:, :, None], rows_y[:, None, :], :]
    average = jnp.moveaxis(payload[:, :, :PATCH], 0, 1)
    result = coarse_new.at[:, rows_x[:, :, None], rows_y[:, None, :], :].set(jnp.where(present[None, :, None, None, None], average, covered))
    weight = courant * live[None, :, None, None]

    def register(index):
        return jnp.moveaxis(payload[:, :, PATCH + index], 0, 1)

    low_x = anchor_x[:, None]
    high_x = low_x + PATCH
    low_y = anchor_y[:, None]
    high_y = low_y + PATCH
    result = result.at[:, low_x - 1, rows_y, :].add(weight * (flux_x[:, low_x, rows_y, :] - register(0)))
    result = result.at[:, high_x, rows_y, :].add(weight * (register(1) - flux_x[:, high_x, rows_y, :]))
    result = result.at[:, rows_x, low_y - 1, :].add(weight * (flux_y[:, rows_x, low_y, :] - register(2)))
    result = result.at[:, rows_x, high_y, :].add(weight * (register(3) - flux_y[:, rows_x, high_y, :]))
    fine_shape = fine_out.shape
    return result.reshape(NVAR, NX, NY * NZ), fine_out.reshape(fine_shape[0], NVAR, 2 * PATCH, fine_shape[3] * fine_shape[4])
```

```python
from functools import partial

import jax
import jax.numpy as jnp
from jax import lax
from jax.experimental import pallas as pl
from jax.experimental.pallas import tpu as pltpu
from jax.sharding import PartitionSpec as P

LANES = 128
SUB = 8
PAD = 8

courant = 0.2
drift = (0.5, 0.3, 0.2)
signal = (1.5, 1.3, 1.2)
PLUS = tuple(0.5 * (a + s) for a, s in zip(drift, signal))
MINUS = tuple(0.5 * (a - s) for a, s in zip(drift, signal))

NVAR = 5
VMEM = pltpu.VMEM


def minmod(first, second):
    return jnp.maximum(jnp.minimum(first, second), jnp.minimum(jnp.maximum(first, second), 0.0))


def lanes_of(rows=SUB):
    return lax.broadcasted_iota(jnp.int32, (rows, LANES), 1)


def roll(values, step):
    step = step % LANES
    return values if step == 0 else pltpu.roll(values, step, 1)


def take(values, index):
    return jnp.take_along_axis(values, index, axis=1, mode="promise_in_bounds")


def coupled(direction):
    return {0: 1 + direction, 1 + direction: 4, 4: 1 + direction}


def add_jumps(acc, direction, jumps):
    couples = coupled(direction)
    for v in range(NVAR):
        left, right = jumps(v)
        for t in range(len(left)):
            term = (courant * PLUS[direction]) * left[t] + (courant * MINUS[direction]) * right[t]
            acc[v][t] = term if acc[v][t] is None else acc[v][t] + term
        targets = [w for w in couples if couples[w] == v]
        if targets:
            for t in range(len(left)):
                shared = (0.5 * courant) * (left[t] + right[t])
                for w in targets:
                    acc[w][t] = shared if acc[w][t] is None else acc[w][t] + shared


def flux_of(left, right, direction):
    couples = coupled(direction)
    out = []
    for v in range(NVAR):
        flux = PLUS[direction] * left[v] + MINUS[direction] * right[v]
        if v in couples:
            w = couples[v]
            flux = flux + 0.5 * (left[w] + right[w])
        out.append(flux)
    return out


class Level:
    def __init__(self, q, slopes, count, rows, depth):
        self.q, self.slopes, self.count, self.rows, self.depth = q, slopes, count, rows, depth
        lane = lanes_of()
        self.first = lane < depth
        self.last = lane >= LANES - depth
        place = lane % depth
        self.behind = jnp.where(place == 0, lane + depth - 1, lane - 1)
        self.ahead = jnp.where(place == depth - 1, lane - depth + 1, lane + 1)

    def x_slopes(self):
        q = self.q
        for v in range(NVAR):
            for t in range(self.count):
                for b in range((self.rows + 2 + SUB - 1) // SUB):
                    row = PAD - 1 + SUB * b
                    here = q[v, t + 1, row : row + SUB]
                    low = here - q[v, t + 1, row - 1 : row - 1 + SUB]
                    high = q[v, t + 1, row + 1 : row + 1 + SUB] - here
                    self.slopes[v, t, SUB * b : SUB * (b + 1)] = 0.5 * minmod(low, high)

    def x_jumps(self, s, v):
        left, right = [], []
        row = PAD + SUB * s
        for t in range(self.count):
            here = self.q[v, t + 1, row : row + SUB]
            low = here - self.q[v, t + 1, row - 1 : row - 1 + SUB]
            high = self.q[v, t + 1, row + 1 : row + 1 + SUB] - here
            before = self.slopes[v, t, SUB * s : SUB * s + SUB]
            slope = self.slopes[v, t, SUB * s + 1 : SUB * s + 1 + SUB]
            after = self.slopes[v, t, SUB * s + 2 : SUB * s + 2 + SUB]
            left.append(low + (slope - before))
            right.append(high - (after - slope))
        return left, right

    def from_low(self, tiles):
        rolled = [roll(tile, self.depth) for tile in tiles]
        return [
            rolled[i] if i == 0 else jnp.where(self.first, rolled[i - 1], rolled[i])
            for i in range(len(tiles))
        ]

    def from_high(self, tiles):
        rolled = [roll(tile, -self.depth) for tile in tiles]
        top = len(tiles) - 1
        return [
            rolled[i] if i == top else jnp.where(self.last, rolled[i + 1], rolled[i])
            for i in range(len(tiles))
        ]

    def y_parts(self, s, v):
        row = PAD + SUB * s
        tiles = [self.q[v, t, row : row + SUB] for t in range(self.count + 2)]
        low = [tile - near for tile, near in zip(tiles, self.from_low(tiles))]
        slopes = [0.5 * minmod(a, b) for a, b in zip(low, self.from_high(low))]
        return tiles, low, slopes

    def y_jumps(self, parts):
        tiles, low, slopes = parts
        rise = [slope - near for slope, near in zip(slopes, self.from_low(slopes))]
        left = [a + b for a, b in zip(low, rise)]
        right = self.from_high([a - b for a, b in zip(low, rise)])
        return left[1:-1], right[1:-1]

    def z_jumps(self, s, v):
        left, right = [], []
        row = PAD + SUB * s
        for t in range(self.count):
            here = self.q[v, t + 1, row : row + SUB]
            low = here - take(here, self.behind)
            slope = 0.5 * minmod(low, take(low, self.ahead))
            rise = slope - take(slope, self.behind)
            left.append(low + rise)
            right.append(take(low - rise, self.ahead))
        return left, right

    def block(self, s, seen=None):
        acc = [[None] * self.count for _ in range(NVAR)]
        add_jumps(acc, 0, partial(self.x_jumps, s))
        parts = {}

        def jumps(v):
            parts[v] = self.y_parts(s, v)
            return self.y_jumps(parts[v])

        add_jumps(acc, 1, jumps)
        if seen is not None:
            seen(parts)
        add_jumps(acc, 2, partial(self.z_jumps, s))
        row = PAD + SUB * s
        return [
            [self.q[v, t + 1, row : row + SUB] - acc[v][t] for t in range(self.count)]
            for v in range(NVAR)
        ]


class Plan:
    def __init__(self, coarse, fine, size):
        self.rows = coarse[1]
        self.depth = 8
        self.count = coarse[2] // LANES
        self.fine_rows = fine[2]
        self.fine_depth = 2 * self.depth
        self.fine_count = fine[3] // LANES
        self.patch = self.fine_rows // 2
        self.start = (self.rows - self.patch) // 2
        self.end = self.start + self.patch
        self.size = size
        self.line_rows = 24
        self.ring_rows = 48
        self.sent_rows = 72
        self.average_rows = NVAR * self.patch
        self.side_at = self.average_rows
        self.face_at = self.side_at + self.patch
        self.owner_at = self.face_at + 10
        self.payload_rows = self.owner_at + 6


def split(plan, c_ref, q):
    for v in range(NVAR):
        for t in range(plan.count):
            q[v, t + 1, PAD : PAD + plan.rows] = c_ref[v, :, LANES * t : LANES * (t + 1)]


def window_row(plan, tiles, lane):
    low, high = (roll(tile, LANES // 2) for tile in tiles)
    return jnp.where(lane < LANES // 2, low, high)


def coarse_kernel(plan, c_ref, up_ref, down_ref, mid_ref, xup_ref, xdown_ref, q, slopes, fresh):
    split(plan, c_ref, q)
    for v in range(NVAR):
        for t in range(plan.count):
            for edge in (0, PAD + plan.rows):
                q[v, t + 1, edge : edge + PAD] = jnp.zeros((PAD, LANES), jnp.float32)
        for t in (0, plan.count + 1):
            q[v, t, PAD : PAD + plan.rows] = jnp.zeros((plan.rows, LANES), jnp.float32)
    level = Level(q, slopes, plan.count, plan.rows, plan.depth)
    level.x_slopes()
    for s in range(plan.rows // SUB):
        new = level.block(s)
        row = PAD + SUB * s
        for v in range(NVAR):
            for t in range(plan.count):
                here = q[v, t + 1, row : row + SUB]
                fresh[v, t, SUB * s : SUB * (s + 1)] = 0.5 * (here + new[v][t])
    lane, single = lanes_of(), lanes_of(1)
    sent = (up_ref, down_ref, mid_ref)
    blank = jnp.zeros((SUB, LANES), jnp.float32)
    for ref in sent:
        ref[16:24] = blank
    for level_id in range(2):
        for side, x in enumerate((plan.start - 1, plan.end)):
            for v in range(NVAR):
                if level_id == 0:
                    tiles = [q[v, t + 1, PAD + x : PAD + x + 1] for t in range(2)]
                else:
                    tiles = [fresh[v, t, x : x + 1] for t in range(2)]
                line = window_row(plan, tiles, single)
                at = 10 * level_id + 5 * side + v
                for ref in sent:
                    ref[at : at + 1] = line
    depth = plan.depth
    low_lane = (plan.start - 1) * depth
    high_lane = plan.end * depth - LANES
    packed = [None] * 3
    for level_id in range(2):
        for side, (t, at) in enumerate(((0, low_lane), (1, high_lane))):
            for v in range(NVAR):
                for half in range(plan.patch // SUB):
                    x = plan.start + SUB * half
                    if level_id == 0:
                        tile = q[v, t + 1, PAD + x : PAD + x + SUB]
                    else:
                        tile = fresh[v, t, x : x + SUB]
                    piece = ((level_id * 2 + side) * NVAR + v) * 2 + half
                    slot = piece % 16
                    moved = roll(tile, slot * depth - at)
                    where, old = piece // 16, packed[piece // 16]
                    packed[where] = moved if old is None else jnp.where(lane // depth == slot, moved, old)
    for index, tile in enumerate(packed):
        for ref in sent:
            ref[plan.line_rows + SUB * index : plan.line_rows + SUB * (index + 1)] = tile
    wide = 2 * depth
    for ref, t, at in ((up_ref, plan.count - 1, LANES - wide), (down_ref, 0, 0)):
        packed = [None] * 3
        for v in range(NVAR):
            for s in range(plan.rows // SUB):
                piece = v * (plan.rows // SUB) + s
                slot = piece % 8
                moved = roll(q[v, t + 1, PAD + SUB * s : PAD + SUB * (s + 1)], slot * wide - at)
                where, old = piece // 8, packed[piece // 8]
                packed[where] = moved if old is None else jnp.where(lane // wide == slot, moved, old)
        for index, tile in enumerate(packed):
            ref[plan.ring_rows + SUB * index : plan.ring_rows + SUB * (index + 1)] = tile
    for ref, x in ((xup_ref, plan.rows - 2), (xdown_ref, 0)):
        ref[16:24] = blank
        for v in range(NVAR):
            for t in range(plan.count):
                at = (v * plan.count + t) * 2
                ref[at : at + 2] = q[v, t + 1, PAD + x : PAD + x + 2]


def fine_kernel(plan, others, site_ref, me_ref, f_ref, *refs):
    rings = refs[: others + 1]
    out_ref, pay_ref, q, slopes, lines, faces, sides = refs[others + 1 :]
    turn = (me_ref[0] - site_ref[0, 0] + plan.size) % plan.size
    count, depth, rows = plan.fine_count, plan.fine_depth, plan.fine_rows
    lane = lanes_of()
    ring = []
    for at in range(0, plan.ring_rows, SUB):
        chosen = rings[0][at : at + SUB]
        for k in range(1, others + 1):
            chosen = jnp.where(turn == k, rings[k][at : at + SUB], chosen)
        ring.append(chosen)
    for t in range(count):
        cells = (lane // depth + t * (LANES // depth)) // 2
        index = cells * plan.depth + (lane % depth) // 2
        for at in range(plan.line_rows // SUB):
            lines[t, SUB * at : SUB * (at + 1)] = take(ring[at], index)
    spread = (lane % depth) // 2

    def ghosts(level_id):
        for v in range(NVAR):
            for side, row in enumerate((PAD - 2, PAD + rows)):
                at = 10 * level_id + 5 * side + v
                for t in range(count):
                    q[v, t + 1, row : row + 2] = jnp.broadcast_to(lines[t, at : at + 1], (2, LANES))
            for side, t in enumerate((0, count + 1)):
                for half in range(plan.patch // SUB):
                    piece = ((level_id * 2 + side) * NVAR + v) * 2 + half
                    tile = ring[plan.line_rows // SUB + piece // 16]
                    column = take(tile, spread + (piece % 16) * plan.depth)
                    row = PAD + 2 * SUB * half
                    q[v, t, pl.ds(row, SUB, stride=2)] = column
                    q[v, t, pl.ds(row + 1, SUB, stride=2)] = column

    for v in range(NVAR):
        for t in range(count):
            q[v, t + 1, PAD : PAD + rows] = f_ref[0, v, :, LANES * t : LANES * (t + 1)]
    level = Level(q, slopes, count, rows, depth)
    for step in range(2):
        ghosts(step)
        level.x_slopes()
        for side in range(2):
            for t in range(count):
                edge = PAD if side == 0 else PAD + rows
                left = [q[v, t + 1, edge - 1 : edge] for v in range(NVAR)]
                right = [q[v, t + 1, edge : edge + 1] for v in range(NVAR)]
                for v in range(NVAR):
                    if side == 0:
                        right[v] = right[v] - slopes[v, t, 1:2]
                    else:
                        left[v] = left[v] + slopes[v, t, rows : rows + 1]
                flux = flux_of(left, right, 0)
                for v in range(NVAR):
                    at = 5 * side + v
                    if step == 0:
                        faces[t, at : at + 1] = flux[v]
                    else:
                        faces[t, at : at + 1] = faces[t, at : at + 1] + flux[v]

        fresh = []
        for s in range(rows // SUB):

            def seen(parts, s=s):
                left = []
                right = []
                second = (lane >= depth) & (lane < 2 * depth)
                for v in range(NVAR):
                    tiles, low, slope = parts[v]
                    ghost_low = roll(tiles[0], depth)
                    inner_high = roll(tiles[count] + slope[count], 2 * depth)
                    left.append(jnp.where(second, inner_high, ghost_low))
                    right.append(jnp.where(second, roll(tiles[count + 1], depth), tiles[1] - slope[1]))
                flux = flux_of(left, right, 1)
                for v in range(NVAR):
                    if step == 0:
                        sides[v, SUB * s : SUB * (s + 1)] = flux[v]
                    else:
                        sides[v, SUB * s : SUB * (s + 1)] = sides[v, SUB * s : SUB * (s + 1)] + flux[v]

            new = level.block(s, seen)
            for v in range(NVAR):
                for t in range(count):
                    if step == 0:
                        q2 = new[v][t]
                        fresh.append((v, t, s, q2))
                    else:
                        out_ref[0, v, SUB * s : SUB * (s + 1), LANES * t : LANES * (t + 1)] = new[v][t]
                        fresh.append((v, t, s, new[v][t]))
        for v, t, s, tile in fresh:
            q[v, t + 1, PAD + SUB * s : PAD + SUB * (s + 1)] = tile

    within = ((lane % 32) // plan.depth) * (2 * depth) + (lane % plan.depth) * 2

    def pack(tiles):
        out = None
        for t, tile in enumerate(tiles):
            tile = tile + roll(tile, -1)
            tile = tile + roll(tile, -depth)
            tile = take(tile, within)
            out = tile if out is None else jnp.where(lane // 32 == t, tile, out)
        return out

    for v in range(NVAR):
        for half in range(plan.patch // SUB):
            row = PAD + 2 * SUB * half
            tiles = [
                q[v, t + 1, pl.ds(row, SUB, stride=2)] + q[v, t + 1, pl.ds(row + 1, SUB, stride=2)]
                for t in range(count)
            ]
            at = v * plan.patch + SUB * half
            pay_ref[at : at + SUB] = 0.125 * pack(tiles)
    pair = ((lane // plan.depth) % 2) * depth + (lane % plan.depth) * 2
    for half in range(plan.patch // SUB):
        out = None
        for v in range(NVAR):
            row = 2 * SUB * half
            tile = sides[v, pl.ds(row, SUB, stride=2)] + sides[v, pl.ds(row + 1, SUB, stride=2)]
            tile = take(tile + roll(tile, -1), pair)
            out = tile if out is None else jnp.where(lane // depth == v, tile, out)
        at = plan.side_at + SUB * half
        pay_ref[at : at + SUB] = 0.125 * out
    owner = jnp.zeros((SUB, LANES), jnp.float32) + site_ref[0, 0].astype(jnp.float32)
    pay_ref[plan.payload_rows - SUB : plan.payload_rows] = owner
    pay_ref[plan.face_at : plan.face_at + SUB] = 0.125 * pack([faces[t, 0:SUB] for t in range(count)])
    tail = pack([faces[t, SUB : 2 * SUB] for t in range(count)])
    pay_ref[plan.face_at + SUB : plan.face_at + SUB + 2] = 0.125 * tail[0:2]


def reflux_kernel(plan, others, live_ref, me_ref, c_ref, low_ref, high_ref, before_ref, after_ref, *refs):
    payloads = refs[: others + 1]
    out_ref, q, slopes, pay = refs[others + 1 :]
    count, depth, rows = plan.count, plan.depth, plan.rows
    lane, single = lanes_of(), lanes_of(1)
    split(plan, c_ref, q)
    wide = 2 * depth
    for v in range(NVAR):
        for t in range(count):
            at = (v * count + t) * 2
            q[v, t + 1, PAD - 2 : PAD] = before_ref[at : at + 2]
            q[v, t + 1, PAD + rows : PAD + rows + 2] = after_ref[at : at + 2]
        for s in range(rows // SUB):
            piece = v * (rows // SUB) + s
            at = plan.ring_rows + SUB * (piece // 8)
            slot = piece % 8
            row = PAD + SUB * s
            q[v, 0, row : row + SUB] = roll(low_ref[at : at + SUB], LANES - wide - slot * wide)
            q[v, count + 1, row : row + SUB] = roll(high_ref[at : at + SUB], -slot * wide)
    mine = me_ref[0].astype(jnp.float32)
    owners = [ref[plan.owner_at : plan.owner_at + 1] == mine for ref in payloads]
    for at in range(0, plan.payload_rows, SUB):
        chosen = payloads[0][at : at + SUB]
        for k in range(1, others + 1):
            chosen = jnp.where(jnp.broadcast_to(owners[k], (SUB, LANES)), payloads[k][at : at + SUB], chosen)
        pay[at : at + SUB] = chosen
    live = live_ref[0]
    weight = courant * live.astype(jnp.float32)
    present = live > 0
    level = Level(q, slopes, count, rows, depth)
    level.x_slopes()
    half = LANES // 2
    low_lane = (plan.start - 1) * depth
    high_lane = plan.end * depth - LANES
    at_low = (lane >= low_lane) & (lane < low_lane + depth)
    at_high = (lane >= high_lane) & (lane < high_lane + depth)
    for s in range(rows // SUB):
        inside = plan.start <= SUB * s < plan.end
        change = {}

        def seen(parts):
            left = [level.from_low([p[0][1] + p[2][1], p[0][2] + p[2][2]]) for p in parts.values()]
            plain = [[p[0][1] + p[2][1], p[0][2] + p[2][2]] for p in parts.values()]
            right = [[p[0][1] - p[2][1], p[0][2] - p[2][2]] for p in parts.values()]
            moved = [level.from_high(r) for r in right]
            low = flux_of([p[0] for p in plain], [m[0] for m in moved], 1)
            high = flux_of([p[1] for p in left], [r[1] for r in right], 1)
            base = plan.side_at + SUB * s - plan.start
            tile = pay[base : base + SUB]
            for v in range(NVAR):
                reg_low = roll(tile, low_lane - v * wide)
                reg_high = roll(tile, high_lane - v * wide - depth)
                change[v] = (
                    jnp.where(at_low, weight * (low[v] - reg_low), 0.0),
                    jnp.where(at_high, weight * (reg_high - high[v]), 0.0),
                )

        new = level.block(s, seen if inside else None)
        for v in range(NVAR):
            if inside:
                base = v * plan.patch + SUB * s - plan.start
                average = roll(pay[base : base + SUB], half)
                new[v][0] = new[v][0] + change[v][0]
                new[v][1] = new[v][1] + change[v][1]
                new[v][0] = jnp.where(present & (lane >= half), average, new[v][0])
                new[v][1] = jnp.where(present & (lane < half), average, new[v][1])
            for t in range(count):
                out_ref[v, SUB * s : SUB * (s + 1), LANES * t : LANES * (t + 1)] = new[v][t]
    for side, x in enumerate((plan.start - 1, plan.end)):
        for t in range(count):
            face = x if side == 0 else x - 1
            left = [q[v, t + 1, PAD + face : PAD + face + 1] + slopes[v, t, face + 1 : face + 2] for v in range(NVAR)]
            right = [
                q[v, t + 1, PAD + face + 1 : PAD + face + 2] - slopes[v, t, face + 2 : face + 3]
                for v in range(NVAR)
            ]
            flux = flux_of(left, right, 0)
            inner = single >= half if t == 0 else single < half
            for v in range(NVAR):
                at = plan.face_at + 5 * side + v
                register = roll(pay[at : at + 1], half)
                gap = flux[v] - register if side == 0 else register - flux[v]
                old = out_ref[v, x : x + 1, LANES * t : LANES * (t + 1)]
                out_ref[v, x : x + 1, LANES * t : LANES * (t + 1)] = old + jnp.where(inner, weight * gap, 0.0)


def call(body, out_shape, scratch, flops, moved, smem=0, operands=0):
    specs = [pl.BlockSpec(memory_space=pltpu.SMEM)] * smem + [pl.BlockSpec(memory_space=VMEM)] * (operands - smem)
    return pl.pallas_call(
        body,
        out_shape=out_shape,
        in_specs=specs,
        out_specs=jax.tree.map(lambda _: pl.BlockSpec(memory_space=VMEM), out_shape),
        scratch_shapes=scratch,
        cost_estimate=pl.CostEstimate(flops=flops, bytes_accessed=moved, transcendentals=0),
        compiler_params=pltpu.CompilerParams(vmem_limit_bytes=16 << 20),
    )


def rotate(array, axis, step):
    size = lax.axis_size(axis)
    return lax.ppermute(array, axis, [(i, (i + step) % size) for i in range(size)])


def shards(coarse_state, fine_state, slot_site, box_live):
    size = lax.axis_size("gy")
    plan = Plan(coarse_state.shape, fine_state.shape, size)
    f32 = jnp.float32
    shape = jax.ShapeDtypeStruct
    coarse_scratch = [
        VMEM((NVAR, plan.count + 2, plan.rows + 2 * PAD, LANES), f32),
        VMEM((NVAR, plan.count, plan.rows + SUB, LANES), f32),
    ]
    sent = shape((plan.sent_rows, LANES), f32)
    edge = shape((24, LANES), f32)
    up, down, mid, xup, xdown = call(
        partial(coarse_kernel, plan),
        (sent, sent, shape((plan.ring_rows, LANES), f32), edge, edge),
        coarse_scratch + [VMEM((NVAR, plan.count, plan.rows, LANES), f32)],
        4_000_000,
        400_000,
        operands=1,
    )(coarse_state)
    others = size - 1
    rings = {0: mid}
    for k in range(1, size):
        rings[k] = rotate(up if k == 1 else down if k == size - 1 else mid, "gy", k)
    before = rotate(xup, "gx", 1)
    after = rotate(xdown, "gx", -1)
    me = lax.axis_index("gy").astype(jnp.int32).reshape(1)
    fine_out, payload = call(
        partial(fine_kernel, plan, others),
        (shape(fine_state.shape, f32), shape((plan.payload_rows, LANES), f32)),
        [
            VMEM((NVAR, plan.fine_count + 2, plan.fine_rows + 2 * PAD, LANES), f32),
            VMEM((NVAR, plan.fine_count, plan.fine_rows + SUB, LANES), f32),
            VMEM((plan.fine_count, plan.line_rows, LANES), f32),
            VMEM((plan.fine_count, 2 * SUB, LANES), f32),
            VMEM((NVAR, plan.fine_rows, LANES), f32),
        ],
        16_000_000,
        1_000_000,
        smem=2,
        operands=3 + size,
    )(slot_site, me, fine_state, *[rings[k] for k in range(size)])
    payloads = [payload] + [rotate(payload, "gy", k) for k in range(1, size)]
    coarse_out = call(
        partial(reflux_kernel, plan, others),
        shape(coarse_state.shape, f32),
        coarse_scratch + [VMEM((plan.payload_rows, LANES), f32)],
        4_000_000,
        400_000,
        smem=2,
        operands=7 + size,
    )(box_live, me, coarse_state, rings[1], rings[size - 1], before, after, *payloads)
    return (coarse_out, fine_out)


def solution(mesh):
    return jax.shard_map(
        shards,
        mesh=mesh,
        in_specs=(
            P(None, "gx", "gy"),
            P(("gx", "gy"), None, None, None),
            P(("gx", "gy"), None),
            P(("gx", "gy")),
        ),
        out_specs=(P(None, "gx", "gy"), P(("gx", "gy"), None, None, None)),
        check_vma=False,
    )
```

```python
from functools import partial

import jax
import jax.numpy as jnp
from jax import lax
from jax.experimental import pallas as pl
from jax.experimental.pallas import tpu as pltpu
from jax.sharding import PartitionSpec as P

LANES = 128
SUB = 8
PAD = 8

courant = 0.2
drift = (0.5, 0.3, 0.2)
signal = (1.5, 1.3, 1.2)
PLUS = tuple(0.5 * (a + s) for a, s in zip(drift, signal))
MINUS = tuple(0.5 * (a - s) for a, s in zip(drift, signal))

NVAR = 5
VMEM = pltpu.VMEM


def minmod(first, second):
    return jnp.maximum(jnp.minimum(first, second), jnp.minimum(jnp.maximum(first, second), 0.0))


def lanes_of(rows=SUB):
    return lax.broadcasted_iota(jnp.int32, (rows, LANES), 1)


def roll(values, step):
    step = step % LANES
    return values if step == 0 else pltpu.roll(values, step, 1)


def take(values, index):
    return jnp.take_along_axis(values, index, axis=1, mode="promise_in_bounds")


def coupled(direction):
    return {0: 1 + direction, 1 + direction: 4, 4: 1 + direction}


def flux_of(left, right, direction):
    couples = coupled(direction)
    out = []
    for v in range(NVAR):
        flux = PLUS[direction] * left[v] + MINUS[direction] * right[v]
        if v in couples:
            w = couples[v]
            flux = flux + 0.5 * (left[w] + right[w])
        out.append(flux)
    return out


class Level:
    def __init__(self, work, count, rows, depth, ghosts):
        self.slopes, self.low, self.slope, self.left, self.right = work[:5]
        self.zlow, self.zslope, self.zleft, self.zright = work[5:]
        self.count, self.rows, self.depth, self.ghosts = count, rows, depth, ghosts
        lane = lanes_of()
        self.first = lane < depth
        self.last = lane >= LANES - depth
        place = lane % depth
        self.behind = jnp.where(place == 0, lane + depth - 1, lane - 1)
        self.ahead = jnp.where(place == depth - 1, lane - depth + 1, lane + 1)

    @staticmethod
    def work(count, rows):
        f32 = jnp.float32
        wide = VMEM((NVAR, count + 2, rows, LANES), f32)
        narrow = VMEM((NVAR, count, rows, LANES), f32)
        return [VMEM((NVAR, count, rows + SUB, LANES), f32)] + [wide] * 4 + [narrow] * 4

    def columns(self):
        for v in range(NVAR):
            for s in range(self.rows // SUB):
                yield v, slice(SUB * s, SUB * (s + 1)), slice(PAD + SUB * s, PAD + SUB * (s + 1))

    def tiles(self):
        for v, here, padded in self.columns():
            for t in range(self.count):
                yield v, t, here, padded

    def prepare(self, q):
        count, depth = self.count, self.depth
        full, flat = self.ghosts == "full", self.ghosts == "flat"
        inner = range(1, count + 1)
        for v, here, padded in self.columns():
            cells = {t: q[v, t, padded] for t in range(count + 2)}
            moved = {t: roll(cells[t], depth) for t in inner}
            moved[0] = roll(cells[0], depth) if full else cells[0] if flat else moved[1]
            for t in inner:
                self.low[v, t, here] = cells[t] - jnp.where(self.first, moved[t - 1], moved[t])
            if full:
                top = roll(cells[count + 1], depth)
                self.low[v, 0, here] = cells[0] - moved[0]
                self.low[v, count + 1, here] = cells[count + 1] - jnp.where(self.first, moved[count], top)
            if flat:
                self.low[v, count + 1, here] = cells[count + 1] - moved[count]
        for v, t, here, padded in self.tiles():
            cell = q[v, t + 1, padded]
            self.zlow[v, t, here] = cell - take(cell, self.behind)
        for v in range(NVAR):
            for t in range(count):
                for b in range((self.rows + 2 + SUB - 1) // SUB):
                    row = PAD - 1 + SUB * b
                    cell = q[v, t + 1, row : row + SUB]
                    low = cell - q[v, t + 1, row - 1 : row - 1 + SUB]
                    high = q[v, t + 1, row + 1 : row + 1 + SUB] - cell
                    self.slopes[v, t, SUB * b : SUB * (b + 1)] = 0.5 * minmod(low, high)
        for v, here, padded in self.columns():
            low = {t: self.low[v, t, here] for t in inner}
            moved = {t: roll(low[t], -depth) for t in inner}
            if full or flat:
                low[count + 1] = self.low[v, count + 1, here]
                moved[count + 1] = roll(low[count + 1], -depth)
            else:
                moved[count + 1] = moved[count]
            for t in inner:
                high = jnp.where(self.last, moved[t + 1], moved[t])
                self.slope[v, t, here] = 0.5 * minmod(low[t], high)
            if full:
                low[0] = self.low[v, 0, here]
                high = jnp.where(self.last, moved[1], roll(low[0], -depth))
                self.slope[v, 0, here] = 0.5 * minmod(low[0], high)
                self.slope[v, count + 1, here] = 0.5 * minmod(low[count + 1], moved[count + 1])
        for v, t, here, padded in self.tiles():
            low = self.zlow[v, t, here]
            self.zslope[v, t, here] = 0.5 * minmod(low, take(low, self.ahead))

    def finish(self, q, store):
        count, depth = self.count, self.depth
        full, flat = self.ghosts == "full", self.ghosts == "flat"
        inner = range(1, count + 1)
        for v, t, here, padded in self.tiles():
            slope = self.zslope[v, t, here]
            rise = slope - take(slope, self.behind)
            low = self.zlow[v, t, here]
            self.zleft[v, t, here] = low + rise
            self.zright[v, t, here] = low - rise
        for v, here, padded in self.columns():
            slope = {t: self.slope[v, t, here] for t in inner}
            moved = {t: roll(slope[t], depth) for t in inner}
            if full:
                moved[0] = roll(self.slope[v, 0, here], depth)
            else:
                moved[0] = jnp.zeros((SUB, LANES), jnp.float32) if flat else moved[1]
            for t in inner:
                rise = slope[t] - jnp.where(self.first, moved[t - 1], moved[t])
                low = self.low[v, t, here]
                self.left[v, t, here] = low + rise
                self.right[v, t, here] = low - rise
            if full:
                rise = self.slope[v, count + 1, here] - moved[count]
                self.right[v, count + 1, here] = self.low[v, count + 1, here] - rise
            if flat:
                self.right[v, count + 1, here] = self.low[v, count + 1, here] + moved[count]
        for v, t, here, padded in self.tiles():
            self.zright[v, t, here] = take(self.zright[v, t, here], self.ahead)
        for v, here, padded in self.columns():
            moved = {t: roll(self.right[v, t, here], -depth) for t in inner}
            if full or flat:
                moved[count + 1] = roll(self.right[v, count + 1, here], -depth)
            else:
                moved[count + 1] = moved[count]
            for t in inner:
                self.right[v, t, here] = jnp.where(self.last, moved[t + 1], moved[t])
        for s in range(self.rows // SUB):
            for t in range(count):
                self.gather(q, s, t, store)

    def gather(self, q, s, t, store):
        here = slice(SUB * s, SUB * (s + 1))
        row = PAD + SUB * s
        cell = [q[v, t + 1, row : row + SUB] for v in range(NVAR)]
        acc = [None] * NVAR

        def add(v, term):
            acc[v] = term if acc[v] is None else acc[v] + term

        for direction in range(3):
            couples = coupled(direction)
            for v in range(NVAR):
                if direction == 0:
                    low = cell[v] - q[v, t + 1, row - 1 : row - 1 + SUB]
                    high = q[v, t + 1, row + 1 : row + 1 + SUB] - cell[v]
                    slope = self.slopes[v, t, SUB * s + 1 : SUB * s + 1 + SUB]
                    left = low + (slope - self.slopes[v, t, SUB * s : SUB * s + SUB])
                    right = high - (self.slopes[v, t, SUB * s + 2 : SUB * s + 2 + SUB] - slope)
                elif direction == 1:
                    left, right = self.left[v, t + 1, here], self.right[v, t + 1, here]
                else:
                    left, right = self.zleft[v, t, here], self.zright[v, t, here]
                add(v, (courant * PLUS[direction]) * left + (courant * MINUS[direction]) * right)
                targets = [w for w in couples if couples[w] == v]
                if targets:
                    shared = (0.5 * courant) * (left + right)
                    for w in targets:
                        add(w, shared)
        for v in range(NVAR):
            store(v, t, s, cell[v] - acc[v])


class Plan:
    def __init__(self, coarse, fine, size):
        self.rows = coarse[1]
        self.depth = 8
        self.count = coarse[2] // LANES
        self.fine_rows = fine[2]
        self.fine_depth = 2 * self.depth
        self.fine_count = fine[3] // LANES
        self.patch = self.fine_rows // 2
        self.start = (self.rows - self.patch) // 2
        self.end = self.start + self.patch
        self.size = size
        self.line_rows = 24
        self.ring_rows = 48
        self.sent_rows = 72
        self.average_rows = NVAR * self.patch
        self.side_at = self.average_rows
        self.face_at = self.side_at + self.patch
        self.owner_at = self.face_at + 10
        self.payload_rows = self.owner_at + 6


def split(plan, c_ref, q):
    for v in range(NVAR):
        for t in range(plan.count):
            q[v, t + 1, PAD : PAD + plan.rows] = c_ref[v, :, LANES * t : LANES * (t + 1)]


def window_row(plan, tiles, lane):
    low, high = (roll(tile, LANES // 2) for tile in tiles)
    return jnp.where(lane < LANES // 2, low, high)


def coarse_kernel(plan, c_ref, f_ref, up_ref, down_ref, mid_ref, xup_ref, xdown_ref, held_ref, q, fresh, sem, *work):
    load = pltpu.make_async_copy(f_ref, held_ref, sem)
    load.start()
    split(plan, c_ref, q)
    for v in range(NVAR):
        for t in range(plan.count):
            for edge in (0, PAD + plan.rows):
                q[v, t + 1, edge : edge + PAD] = jnp.zeros((PAD, LANES), jnp.float32)
        for t in (0, plan.count + 1):
            q[v, t, PAD : PAD + plan.rows] = jnp.zeros((plan.rows, LANES), jnp.float32)
    level = Level(work, plan.count, plan.rows, plan.depth, "none")
    level.prepare(q)

    def store(v, t, s, tile):
        row = PAD + SUB * s
        fresh[v, t, SUB * s : SUB * (s + 1)] = 0.5 * (q[v, t + 1, row : row + SUB] + tile)

    level.finish(q, store)
    lane, single = lanes_of(), lanes_of(1)
    sent = (up_ref, down_ref, mid_ref)
    blank = jnp.zeros((SUB, LANES), jnp.float32)
    for ref in sent:
        ref[16:24] = blank
    for level_id in range(2):
        for side, x in enumerate((plan.start - 1, plan.end)):
            for v in range(NVAR):
                if level_id == 0:
                    tiles = [q[v, t + 1, PAD + x : PAD + x + 1] for t in range(2)]
                else:
                    tiles = [fresh[v, t, x : x + 1] for t in range(2)]
                line = window_row(plan, tiles, single)
                at = 10 * level_id + 5 * side + v
                for ref in sent:
                    ref[at : at + 1] = line
    depth = plan.depth
    low_lane = (plan.start - 1) * depth
    high_lane = plan.end * depth - LANES
    packed = [None] * 3
    for level_id in range(2):
        for side, (t, at) in enumerate(((0, low_lane), (1, high_lane))):
            for v in range(NVAR):
                for half in range(plan.patch // SUB):
                    x = plan.start + SUB * half
                    if level_id == 0:
                        tile = q[v, t + 1, PAD + x : PAD + x + SUB]
                    else:
                        tile = fresh[v, t, x : x + SUB]
                    piece = ((level_id * 2 + side) * NVAR + v) * 2 + half
                    slot = piece % 16
                    moved = roll(tile, slot * depth - at)
                    where, old = piece // 16, packed[piece // 16]
                    packed[where] = moved if old is None else jnp.where(lane // depth == slot, moved, old)
    for index, tile in enumerate(packed):
        for ref in sent:
            ref[plan.line_rows + SUB * index : plan.line_rows + SUB * (index + 1)] = tile
    wide = 2 * depth
    for ref, t, at in ((up_ref, plan.count - 1, LANES - wide), (down_ref, 0, 0)):
        packed = [None] * 3
        for v in range(NVAR):
            for s in range(plan.rows // SUB):
                piece = v * (plan.rows // SUB) + s
                slot = piece % 8
                moved = roll(q[v, t + 1, PAD + SUB * s : PAD + SUB * (s + 1)], slot * wide - at)
                where, old = piece // 8, packed[piece // 8]
                packed[where] = moved if old is None else jnp.where(lane // wide == slot, moved, old)
        for index, tile in enumerate(packed):
            ref[plan.ring_rows + SUB * index : plan.ring_rows + SUB * (index + 1)] = tile
    for ref, x in ((xup_ref, plan.rows - 2), (xdown_ref, 0)):
        ref[16:24] = blank
        for v in range(NVAR):
            for t in range(plan.count):
                at = (v * plan.count + t) * 2
                ref[at : at + 2] = q[v, t + 1, PAD + x : PAD + x + 2]
    load.wait()


def fine_kernel(plan, others, site_ref, me_ref, f_ref, *refs):
    rings = refs[: others + 1]
    out_ref, pay_ref, q, q_later, lines, faces, sides = refs[others + 1 : others + 8]
    work = refs[others + 8 :]
    turn = (me_ref[0] - site_ref[0, 0] + plan.size) % plan.size
    count, depth, rows = plan.fine_count, plan.fine_depth, plan.fine_rows
    lane = lanes_of()
    ring = []
    for at in range(0, plan.ring_rows, SUB):
        chosen = rings[0][at : at + SUB]
        for k in range(1, others + 1):
            chosen = jnp.where(turn == k, rings[k][at : at + SUB], chosen)
        ring.append(chosen)
    for t in range(count):
        cells = (lane // depth + t * (LANES // depth)) // 2
        index = cells * plan.depth + (lane % depth) // 2
        for at in range(plan.line_rows // SUB):
            lines[t, SUB * at : SUB * (at + 1)] = take(ring[at], index)
    spread = (lane % depth) // 2

    def ghosts(q, level_id):
        for v in range(NVAR):
            for side, row in enumerate((PAD - 2, PAD + rows)):
                at = 10 * level_id + 5 * side + v
                for t in range(count):
                    q[v, t + 1, row : row + 2] = jnp.broadcast_to(lines[t, at : at + 1], (2, LANES))
            for side, t in enumerate((0, count + 1)):
                for half in range(plan.patch // SUB):
                    piece = ((level_id * 2 + side) * NVAR + v) * 2 + half
                    tile = ring[plan.line_rows // SUB + piece // 16]
                    column = take(roll(tile, -(piece % 16) * plan.depth), spread)
                    row = PAD + 2 * SUB * half
                    q[v, t, pl.ds(row, SUB, stride=2)] = column
                    q[v, t, pl.ds(row + 1, SUB, stride=2)] = column

    for v in range(NVAR):
        for t in range(count):
            q[v, t + 1, PAD : PAD + rows] = f_ref[0, v, :, LANES * t : LANES * (t + 1)]
    level = Level(work, count, rows, depth, "flat")
    slopes = level.slopes
    second = (lane >= depth) & (lane < 2 * depth)
    ghosts(q, 0)
    ghosts(q_later, 1)
    for step, (now, later) in enumerate(((q, q_later), (q_later, q))):

        def add(ref, index, value, step=step):
            ref[index] = value if step == 0 else ref[index] + value

        level.prepare(now)
        for side in range(2):
            for t in range(count):
                edge = PAD if side == 0 else PAD + rows
                left = [now[v, t + 1, edge - 1 : edge] for v in range(NVAR)]
                right = [now[v, t + 1, edge : edge + 1] for v in range(NVAR)]
                for v in range(NVAR):
                    if side == 0:
                        right[v] = right[v] - slopes[v, t, 1:2]
                    else:
                        left[v] = left[v] + slopes[v, t, rows : rows + 1]
                flux = flux_of(left, right, 0)
                for v in range(NVAR):
                    add(faces, (t, slice(5 * side + v, 5 * side + v + 1)), flux[v])
        for s in range(rows // SUB):
            here = slice(SUB * s, SUB * (s + 1))
            padded = slice(PAD + SUB * s, PAD + SUB * (s + 1))
            left, right = [], []
            for v in range(NVAR):
                inner = roll(now[v, count, padded] + level.slope[v, count, here], 2 * depth)
                left.append(jnp.where(second, inner, now[v, 0, padded]))
                right.append(jnp.where(second, now[v, count + 1, padded], now[v, 1, padded] - level.slope[v, 1, here]))
            flux = flux_of(left, right, 1)
            for v in range(NVAR):
                add(sides, (v, here), flux[v])

        def store(v, t, s, tile, step=step, later=later):
            later[v, t + 1, PAD + SUB * s : PAD + SUB * (s + 1)] = tile
            if step == 1:
                out_ref[0, v, SUB * s : SUB * (s + 1), LANES * t : LANES * (t + 1)] = tile

        level.finish(now, store)

    within = ((lane % 32) // plan.depth) * (2 * depth) + (lane % plan.depth) * 2

    def pack(tiles):
        out = None
        for t, tile in enumerate(tiles):
            tile = tile + roll(tile, -1)
            tile = tile + roll(tile, -depth)
            tile = take(tile, within)
            out = tile if out is None else jnp.where(lane // 32 == t, tile, out)
        return out

    for v in range(NVAR):
        for half in range(plan.patch // SUB):
            row = PAD + 2 * SUB * half
            tiles = [
                q[v, t + 1, pl.ds(row, SUB, stride=2)] + q[v, t + 1, pl.ds(row + 1, SUB, stride=2)]
                for t in range(count)
            ]
            at = v * plan.patch + SUB * half
            pay_ref[at : at + SUB] = 0.125 * pack(tiles)
    pair = ((lane // plan.depth) % 2) * depth + (lane % plan.depth) * 2
    for half in range(plan.patch // SUB):
        out = None
        for v in range(NVAR):
            row = 2 * SUB * half
            tile = sides[v, pl.ds(row, SUB, stride=2)] + sides[v, pl.ds(row + 1, SUB, stride=2)]
            tile = take(tile + roll(tile, -1), pair)
            out = tile if out is None else jnp.where(lane // depth == v, tile, out)
        at = plan.side_at + SUB * half
        pay_ref[at : at + SUB] = 0.125 * out
    owner = jnp.zeros((SUB, LANES), jnp.float32) + site_ref[0, 0].astype(jnp.float32)
    pay_ref[plan.payload_rows - SUB : plan.payload_rows] = owner
    pay_ref[plan.face_at : plan.face_at + SUB] = 0.125 * pack([faces[t, 0:SUB] for t in range(count)])
    tail = pack([faces[t, SUB : 2 * SUB] for t in range(count)])
    pay_ref[plan.face_at + SUB : plan.face_at + SUB + 2] = 0.125 * tail[0:2]


def outer_kernel(plan, live_ref, c_ref, held_ref, low_ref, high_ref, before_ref, after_ref, out_ref, fine_ref, q, sem, *work):
    put = pltpu.make_async_copy(held_ref, fine_ref, sem)
    put.start()
    count, depth, rows = plan.count, plan.depth, plan.rows
    lane, single = lanes_of(), lanes_of(1)
    split(plan, c_ref, q)
    wide = 2 * depth
    blank = jnp.zeros((PAD, LANES), jnp.float32)
    for v in range(NVAR):
        for t in range(count):
            at = (v * count + t) * 2
            q[v, t + 1, 0:PAD] = blank
            q[v, t + 1, PAD + rows : 2 * PAD + rows] = blank
            q[v, t + 1, PAD - 2 : PAD] = before_ref[at : at + 2]
            q[v, t + 1, PAD + rows : PAD + rows + 2] = after_ref[at : at + 2]
        for s in range(rows // SUB):
            piece = v * (rows // SUB) + s
            at = plan.ring_rows + SUB * (piece // 8)
            slot = piece % 8
            row = PAD + SUB * s
            q[v, 0, row : row + SUB] = roll(low_ref[at : at + SUB], LANES - wide - slot * wide)
            q[v, count + 1, row : row + SUB] = roll(high_ref[at : at + SUB], -slot * wide)
    weight = courant * live_ref[0].astype(jnp.float32)
    level = Level(work, count, rows, depth, "full")
    slopes = level.slopes
    level.prepare(q)

    def store(v, t, s, tile):
        out_ref[v, SUB * s : SUB * (s + 1), LANES * t : LANES * (t + 1)] = tile

    level.finish(q, store)
    half = LANES // 2
    low_lane = (plan.start - 1) * depth
    high_lane = plan.end * depth - LANES
    at_low = (lane >= low_lane) & (lane < low_lane + depth)
    at_high = (lane >= high_lane) & (lane < high_lane + depth)
    for x in range(plan.start, plan.end, SUB):
        here, padded = slice(x, x + SUB), slice(PAD + x, PAD + x + SUB)
        cells = [[q[v, t + 1, padded] for v in range(NVAR)] for t in range(2)]
        slope = [[level.slope[v, t + 1, here] for v in range(NVAR)] for t in range(2)]
        left = [[c + d for c, d in zip(cells[t], slope[t])] for t in range(2)]
        right = [[c - d for c, d in zip(cells[t], slope[t])] for t in range(2)]
        last, first = level.last, level.first
        ahead = [
            jnp.where(last, roll(b, -depth), roll(a, -depth)) for a, b in zip(right[0], right[1])
        ]
        behind = [
            jnp.where(first, roll(a, depth), roll(b, depth)) for a, b in zip(left[0], left[1])
        ]
        low = flux_of(left[0], ahead, 1)
        high = flux_of(behind, right[1], 1)
        for v in range(NVAR):
            out_ref[v, here, 0:LANES] = out_ref[v, here, 0:LANES] + jnp.where(at_low, weight * low[v], 0.0)
            out_ref[v, here, LANES : 2 * LANES] = out_ref[v, here, LANES : 2 * LANES] - jnp.where(
                at_high, weight * high[v], 0.0
            )
    for side, x in enumerate((plan.start - 1, plan.end)):
        face = x if side == 0 else x - 1
        for t in range(2):
            left = [q[v, t + 1, PAD + face : PAD + face + 1] + slopes[v, t, face + 1 : face + 2] for v in range(NVAR)]
            right = [
                q[v, t + 1, PAD + face + 1 : PAD + face + 2] - slopes[v, t, face + 2 : face + 3]
                for v in range(NVAR)
            ]
            flux = flux_of(left, right, 0)
            inner = single >= half if t == 0 else single < half
            signed = weight if side == 0 else -weight
            for v in range(NVAR):
                at = (v, slice(x, x + 1), slice(LANES * t, LANES * (t + 1)))
                out_ref[at] = out_ref[at] + jnp.where(inner, signed * flux[v], 0.0)
    put.wait()


def patch_kernel(plan, others, live_ref, me_ref, c_ref, *refs):
    payloads = refs[: others + 1]
    out_ref, pay = refs[others + 1 :]
    depth = plan.depth
    lane, single = lanes_of(), lanes_of(1)
    mine = me_ref[0].astype(jnp.float32)
    owners = [
        jnp.broadcast_to(ref[plan.owner_at : plan.owner_at + 1], (SUB, LANES)) == mine for ref in payloads
    ]
    for at in range(0, plan.payload_rows, SUB):
        chosen = payloads[0][at : at + SUB]
        for k in range(1, others + 1):
            chosen = jnp.where(owners[k], payloads[k][at : at + SUB], chosen)
        pay[at : at + SUB] = chosen
    live = live_ref[0]
    weight = courant * live.astype(jnp.float32)
    present = jnp.full((SUB, LANES), live, jnp.int32) > 0
    half = LANES // 2
    low_lane = (plan.start - 1) * depth
    high_lane = plan.end * depth - LANES
    at_low = (lane >= low_lane) & (lane < low_lane + depth)
    at_high = (lane >= high_lane) & (lane < high_lane + depth)
    under = (present & (lane >= half), present & (lane < half))
    for v in range(NVAR):
        for x in range(0, plan.rows, SUB):
            here = slice(x, x + SUB)
            tiles = [c_ref[v, here, LANES * t : LANES * (t + 1)] for t in range(plan.count)]
            if plan.start <= x < plan.end:
                base = plan.side_at + x - plan.start
                side = pay[base : base + SUB]
                low = roll(side, low_lane - v * 2 * depth)
                high = roll(side, high_lane - v * 2 * depth - depth)
                tiles[0] = tiles[0] - jnp.where(at_low, weight * low, 0.0)
                tiles[1] = tiles[1] + jnp.where(at_high, weight * high, 0.0)
                base = v * plan.patch + x - plan.start
                average = roll(pay[base : base + SUB], half)
                for t in range(2):
                    tiles[t] = jnp.where(under[t], average, tiles[t])
            for t in range(plan.count):
                out_ref[v, here, LANES * t : LANES * (t + 1)] = tiles[t]
        for side, x in enumerate((plan.start - 1, plan.end)):
            at = plan.face_at + 5 * side + v
            register = roll(pay[at : at + 1], half)
            signed = -weight if side == 0 else weight
            for t in range(2):
                inner = single >= half if t == 0 else single < half
                at = (v, slice(x, x + 1), slice(LANES * t, LANES * (t + 1)))
                out_ref[at] = c_ref[at] + jnp.where(inner, signed * register, 0.0)


def call(body, out_shape, scratch, flops, moved, spaces, out_spaces=None):
    if out_spaces is None:
        out_spaces = jax.tree.map(lambda _: VMEM, out_shape)
    return pl.pallas_call(
        body,
        out_shape=out_shape,
        in_specs=[pl.BlockSpec(memory_space=space) for space in spaces],
        out_specs=jax.tree.map(lambda space: pl.BlockSpec(memory_space=space), out_spaces),
        scratch_shapes=scratch,
        cost_estimate=pl.CostEstimate(flops=flops, bytes_accessed=moved, transcendentals=0),
        compiler_params=pltpu.CompilerParams(vmem_limit_bytes=16 << 20),
    )


def rotate(array, axis, step):
    size = lax.axis_size(axis)
    return lax.ppermute(array, axis, [(i, (i + step) % size) for i in range(size)])


def shards(coarse_state, fine_state, slot_site, box_live):
    size = lax.axis_size("gy")
    plan = Plan(coarse_state.shape, fine_state.shape, size)
    f32 = jnp.float32
    shape = jax.ShapeDtypeStruct
    smem, anywhere = pltpu.SMEM, pl.ANY
    cells = VMEM((NVAR, plan.count + 2, plan.rows + 2 * PAD, LANES), f32)
    copying = pltpu.SemaphoreType.DMA
    sent = shape((plan.sent_rows, LANES), f32)
    edge = shape((24, LANES), f32)
    held_shape = shape(fine_state.shape, f32)
    up, down, mid, xup, xdown, held = call(
        partial(coarse_kernel, plan),
        (sent, sent, shape((plan.ring_rows, LANES), f32), edge, edge, held_shape),
        [cells, VMEM((NVAR, plan.count, plan.rows, LANES), f32), copying] + Level.work(plan.count, plan.rows),
        4_000_000,
        400_000,
        [VMEM, anywhere],
    )(coarse_state, fine_state)
    others = size - 1
    rings = {0: mid}
    for k in range(1, size):
        rings[k] = rotate(up if k == 1 else down if k == size - 1 else mid, "gy", k)
    before = rotate(xup, "gx", 1)
    after = rotate(xdown, "gx", -1)
    me = lax.axis_index("gy").astype(jnp.int32).reshape(1)
    fine_cells = VMEM((NVAR, plan.fine_count + 2, plan.fine_rows + 2 * PAD, LANES), f32)
    second, payload = call(
        partial(fine_kernel, plan, others),
        (held_shape, shape((plan.payload_rows, LANES), f32)),
        [
            fine_cells,
            fine_cells,
            VMEM((plan.fine_count, plan.line_rows, LANES), f32),
            VMEM((plan.fine_count, 2 * SUB, LANES), f32),
            VMEM((NVAR, plan.fine_rows, LANES), f32),
        ]
        + Level.work(plan.fine_count, plan.fine_rows),
        16_000_000,
        1_000_000,
        [smem, smem, VMEM] + [VMEM] * size,
    )(slot_site, me, held, *[rings[k] for k in range(size)])
    payloads = [payload] + [rotate(payload, "gy", k) for k in range(1, size)]
    coarse_new, fine_out = call(
        partial(outer_kernel, plan),
        (shape(coarse_state.shape, f32), held_shape),
        [cells, copying] + Level.work(plan.count, plan.rows),
        4_000_000,
        400_000,
        [smem] + [VMEM] * 6,
        (VMEM, anywhere),
    )(box_live, coarse_state, second, rings[1], rings[size - 1], before, after)
    coarse_out = call(
        partial(patch_kernel, plan, others),
        shape(coarse_state.shape, f32),
        [VMEM((plan.payload_rows, LANES), f32)],
        400_000,
        400_000,
        [smem, smem, VMEM] + [VMEM] * size,
    )(box_live, me, coarse_new, *payloads)
    return (coarse_out, fine_out)


def solution(mesh):
    return jax.shard_map(
        shards,
        mesh=mesh,
        in_specs=(
            P(None, "gx", "gy"),
            P(("gx", "gy"), None, None, None),
            P(("gx", "gy"), None),
            P(("gx", "gy")),
        ),
        out_specs=(P(None, "gx", "gy"), P(("gx", "gy"), None, None, None)),
        check_vma=False,
    )
```

```python
from functools import partial

import jax
import jax.numpy as jnp
from jax import lax
from jax.experimental import pallas as pl
from jax.experimental.pallas import tpu as pltpu
from jax.sharding import PartitionSpec as P

LANES = 128
SUB = 8
PAD = 8

courant = 0.2
drift = (0.5, 0.3, 0.2)
signal = (1.5, 1.3, 1.2)
PLUS = tuple(0.5 * (a + s) for a, s in zip(drift, signal))
MINUS = tuple(0.5 * (a - s) for a, s in zip(drift, signal))

NVAR = 5
VMEM = pltpu.VMEM


def minmod(first, second):
    return jnp.maximum(jnp.minimum(first, second), jnp.minimum(jnp.maximum(first, second), 0.0))


def lanes_of(rows=SUB):
    return lax.broadcasted_iota(jnp.int32, (rows, LANES), 1)


def roll(values, step):
    step = step % LANES
    return values if step == 0 else pltpu.roll(values, step, 1)


def take(values, index):
    return jnp.take_along_axis(values, index, axis=1, mode="promise_in_bounds")


def coupled(direction):
    return {0: 1 + direction, 1 + direction: 4, 4: 1 + direction}


def flux_of(left, right, direction):
    couples = coupled(direction)
    out = []
    for v in range(NVAR):
        flux = PLUS[direction] * left[v] + MINUS[direction] * right[v]
        if v in couples:
            w = couples[v]
            flux = flux + 0.5 * (left[w] + right[w])
        out.append(flux)
    return out


class Level:
    def __init__(self, work, count, rows, depth, ghosts):
        self.slopes, self.low, self.slope, self.left, self.right = work[:5]
        self.zlow, self.zslope, self.zleft, self.zright = work[5:]
        self.count, self.rows, self.depth, self.ghosts = count, rows, depth, ghosts
        lane = lanes_of()
        self.first = lane < depth
        self.last = lane >= LANES - depth
        place = lane % depth
        self.behind = jnp.where(place == 0, lane + depth - 1, lane - 1)
        self.ahead = jnp.where(place == depth - 1, lane - depth + 1, lane + 1)

    @staticmethod
    def work(count, rows):
        f32 = jnp.float32
        wide = VMEM((NVAR, count + 2, rows, LANES), f32)
        narrow = VMEM((NVAR, count, rows, LANES), f32)
        return [VMEM((NVAR, count, rows + SUB, LANES), f32)] + [wide] * 4 + [narrow] * 4

    def columns(self):
        for v in range(NVAR):
            for s in range(self.rows // SUB):
                yield v, slice(SUB * s, SUB * (s + 1)), slice(PAD + SUB * s, PAD + SUB * (s + 1))

    def tiles(self):
        for v, here, padded in self.columns():
            for t in range(self.count):
                yield v, t, here, padded

    def prepare(self, q):
        count, depth = self.count, self.depth
        full, flat = self.ghosts == "full", self.ghosts == "flat"
        inner = range(1, count + 1)
        for v, here, padded in self.columns():
            cells = {t: q[v, t, padded] for t in range(count + 2)}
            moved = {t: roll(cells[t], depth) for t in inner}
            moved[0] = roll(cells[0], depth) if full else cells[0] if flat else moved[1]
            for t in inner:
                self.low[v, t, here] = cells[t] - jnp.where(self.first, moved[t - 1], moved[t])
            if full:
                top = roll(cells[count + 1], depth)
                self.low[v, 0, here] = cells[0] - moved[0]
                self.low[v, count + 1, here] = cells[count + 1] - jnp.where(self.first, moved[count], top)
            if flat:
                self.low[v, count + 1, here] = cells[count + 1] - moved[count]
        for v, t, here, padded in self.tiles():
            cell = q[v, t + 1, padded]
            self.zlow[v, t, here] = cell - take(cell, self.behind)
        for v in range(NVAR):
            for t in range(count):
                for b in range((self.rows + 2 + SUB - 1) // SUB):
                    row = PAD - 1 + SUB * b
                    cell = q[v, t + 1, row : row + SUB]
                    low = cell - q[v, t + 1, row - 1 : row - 1 + SUB]
                    high = q[v, t + 1, row + 1 : row + 1 + SUB] - cell
                    self.slopes[v, t, SUB * b : SUB * (b + 1)] = 0.5 * minmod(low, high)
        for v, here, padded in self.columns():
            low = {t: self.low[v, t, here] for t in inner}
            moved = {t: roll(low[t], -depth) for t in inner}
            if full or flat:
                low[count + 1] = self.low[v, count + 1, here]
                moved[count + 1] = roll(low[count + 1], -depth)
            else:
                moved[count + 1] = moved[count]
            for t in inner:
                high = jnp.where(self.last, moved[t + 1], moved[t])
                self.slope[v, t, here] = 0.5 * minmod(low[t], high)
            if full:
                low[0] = self.low[v, 0, here]
                high = jnp.where(self.last, moved[1], roll(low[0], -depth))
                self.slope[v, 0, here] = 0.5 * minmod(low[0], high)
                self.slope[v, count + 1, here] = 0.5 * minmod(low[count + 1], moved[count + 1])
        for v, t, here, padded in self.tiles():
            low = self.zlow[v, t, here]
            self.zslope[v, t, here] = 0.5 * minmod(low, take(low, self.ahead))

    def finish(self, q, store):
        count, depth = self.count, self.depth
        full, flat = self.ghosts == "full", self.ghosts == "flat"
        inner = range(1, count + 1)
        for v, t, here, padded in self.tiles():
            slope = self.zslope[v, t, here]
            rise = slope - take(slope, self.behind)
            low = self.zlow[v, t, here]
            self.zleft[v, t, here] = low + rise
            self.zright[v, t, here] = low - rise
        for v, here, padded in self.columns():
            slope = {t: self.slope[v, t, here] for t in inner}
            moved = {t: roll(slope[t], depth) for t in inner}
            if full:
                moved[0] = roll(self.slope[v, 0, here], depth)
            else:
                moved[0] = jnp.zeros((SUB, LANES), jnp.float32) if flat else moved[1]
            for t in inner:
                rise = slope[t] - jnp.where(self.first, moved[t - 1], moved[t])
                low = self.low[v, t, here]
                self.left[v, t, here] = low + rise
                self.right[v, t, here] = low - rise
            if full:
                rise = self.slope[v, count + 1, here] - moved[count]
                self.right[v, count + 1, here] = self.low[v, count + 1, here] - rise
            if flat:
                self.right[v, count + 1, here] = self.low[v, count + 1, here] + moved[count]
        for v, t, here, padded in self.tiles():
            self.zright[v, t, here] = take(self.zright[v, t, here], self.ahead)
        for v, here, padded in self.columns():
            moved = {t: roll(self.right[v, t, here], -depth) for t in inner}
            if full or flat:
                moved[count + 1] = roll(self.right[v, count + 1, here], -depth)
            else:
                moved[count + 1] = moved[count]
            for t in inner:
                self.right[v, t, here] = jnp.where(self.last, moved[t + 1], moved[t])
        for s in range(self.rows // SUB):
            for t in range(count):
                self.gather(q, s, t, store)

    def gather(self, q, s, t, store):
        here = slice(SUB * s, SUB * (s + 1))
        row = PAD + SUB * s
        cell = [q[v, t + 1, row : row + SUB] for v in range(NVAR)]
        acc = [None] * NVAR

        def add(v, term):
            acc[v] = term if acc[v] is None else acc[v] + term

        for direction in range(3):
            couples = coupled(direction)
            for v in range(NVAR):
                if direction == 0:
                    low = cell[v] - q[v, t + 1, row - 1 : row - 1 + SUB]
                    high = q[v, t + 1, row + 1 : row + 1 + SUB] - cell[v]
                    slope = self.slopes[v, t, SUB * s + 1 : SUB * s + 1 + SUB]
                    left = low + (slope - self.slopes[v, t, SUB * s : SUB * s + SUB])
                    right = high - (self.slopes[v, t, SUB * s + 2 : SUB * s + 2 + SUB] - slope)
                elif direction == 1:
                    left, right = self.left[v, t + 1, here], self.right[v, t + 1, here]
                else:
                    left, right = self.zleft[v, t, here], self.zright[v, t, here]
                add(v, (courant * PLUS[direction]) * left + (courant * MINUS[direction]) * right)
                targets = [w for w in couples if couples[w] == v]
                if targets:
                    shared = (0.5 * courant) * (left + right)
                    for w in targets:
                        add(w, shared)
        for v in range(NVAR):
            store(v, t, s, cell[v] - acc[v])


class Plan:
    def __init__(self, coarse, fine, size):
        self.rows = coarse[1]
        self.depth = 8
        self.count = coarse[2] // LANES
        self.fine_rows = fine[2]
        self.fine_depth = 2 * self.depth
        self.fine_count = fine[3] // LANES
        self.patch = self.fine_rows // 2
        self.start = (self.rows - self.patch) // 2
        self.end = self.start + self.patch
        self.size = size
        self.line_rows = 24
        self.ring_rows = 48
        self.sent_rows = 72
        self.average_rows = NVAR * self.patch
        self.side_at = self.average_rows
        self.face_at = self.side_at + self.patch
        self.owner_at = self.face_at + 10
        self.payload_rows = self.owner_at + 6


def split(plan, c_ref, q):
    for v in range(NVAR):
        for t in range(plan.count):
            q[v, t + 1, PAD : PAD + plan.rows] = c_ref[v, :, LANES * t : LANES * (t + 1)]


def window_row(plan, tiles, lane):
    low, high = (roll(tile, LANES // 2) for tile in tiles)
    return jnp.where(lane < LANES // 2, low, high)


def coarse_kernel(
    plan, site_hbm, c_hbm, f_hbm, up_ref, down_ref, mid_ref, xup_ref, xdown_ref, ids_ref, held_ref, c_ref,
    q, fresh, site_ref, sems, *work
):
    loads = [
        pltpu.make_async_copy(source, target, sems.at[index])
        for index, (source, target) in enumerate(
            ((c_hbm, c_ref), (f_hbm, held_ref), (site_hbm, site_ref))
        )
    ]
    for load in loads:
        load.start()
    loads[0].wait()
    split(plan, c_ref, q)
    for v in range(NVAR):
        for t in range(plan.count):
            for edge in (0, PAD + plan.rows):
                q[v, t + 1, edge : edge + PAD] = jnp.zeros((PAD, LANES), jnp.float32)
        for t in (0, plan.count + 1):
            q[v, t, PAD : PAD + plan.rows] = jnp.zeros((plan.rows, LANES), jnp.float32)
    level = Level(work, plan.count, plan.rows, plan.depth, "none")
    level.prepare(q)

    def store(v, t, s, tile):
        row = PAD + SUB * s
        fresh[v, t, SUB * s : SUB * (s + 1)] = 0.5 * (q[v, t + 1, row : row + SUB] + tile)

    level.finish(q, store)
    lane, single = lanes_of(), lanes_of(1)
    sent = (up_ref, down_ref, mid_ref)
    blank = jnp.zeros((SUB, LANES), jnp.float32)
    for ref in sent:
        ref[16:24] = blank
    for level_id in range(2):
        for side, x in enumerate((plan.start - 1, plan.end)):
            for v in range(NVAR):
                if level_id == 0:
                    tiles = [q[v, t + 1, PAD + x : PAD + x + 1] for t in range(2)]
                else:
                    tiles = [fresh[v, t, x : x + 1] for t in range(2)]
                line = window_row(plan, tiles, single)
                at = 10 * level_id + 5 * side + v
                for ref in sent:
                    ref[at : at + 1] = line
    depth = plan.depth
    low_lane = (plan.start - 1) * depth
    high_lane = plan.end * depth - LANES
    packed = [None] * 3
    for level_id in range(2):
        for side, (t, at) in enumerate(((0, low_lane), (1, high_lane))):
            for v in range(NVAR):
                for half in range(plan.patch // SUB):
                    x = plan.start + SUB * half
                    if level_id == 0:
                        tile = q[v, t + 1, PAD + x : PAD + x + SUB]
                    else:
                        tile = fresh[v, t, x : x + SUB]
                    piece = ((level_id * 2 + side) * NVAR + v) * 2 + half
                    slot = piece % 16
                    moved = roll(tile, slot * depth - at)
                    where, old = piece // 16, packed[piece // 16]
                    packed[where] = moved if old is None else jnp.where(lane // depth == slot, moved, old)
    for index, tile in enumerate(packed):
        for ref in sent:
            ref[plan.line_rows + SUB * index : plan.line_rows + SUB * (index + 1)] = tile
    wide = 2 * depth
    for ref, t, at in ((up_ref, plan.count - 1, LANES - wide), (down_ref, 0, 0)):
        packed = [None] * 3
        for v in range(NVAR):
            for s in range(plan.rows // SUB):
                piece = v * (plan.rows // SUB) + s
                slot = piece % 8
                moved = roll(q[v, t + 1, PAD + SUB * s : PAD + SUB * (s + 1)], slot * wide - at)
                where, old = piece // 8, packed[piece // 8]
                packed[where] = moved if old is None else jnp.where(lane // wide == slot, moved, old)
        for index, tile in enumerate(packed):
            ref[plan.ring_rows + SUB * index : plan.ring_rows + SUB * (index + 1)] = tile
    for ref, x in ((xup_ref, plan.rows - 2), (xdown_ref, 0)):
        ref[16:24] = blank
        for v in range(NVAR):
            for t in range(plan.count):
                at = (v * plan.count + t) * 2
                ref[at : at + 2] = q[v, t + 1, PAD + x : PAD + x + 2]
    for load in loads[1:]:
        load.wait()
    zero = jnp.zeros((SUB, LANES), jnp.float32)
    for index, number in enumerate((site_ref[0, 0], lax.axis_index("gy"))):
        ids_ref[SUB * index : SUB * (index + 1)] = zero + number.astype(jnp.float32)


def fine_kernel(plan, others, ids_ref, f_ref, *refs):
    rings = refs[: others + 1]
    out_ref, pay_ref, q, q_later, lines, faces, sides = refs[others + 1 : others + 8]
    work = refs[others + 8 :]
    owner = ids_ref[0:SUB]
    gap = ids_ref[SUB : 2 * SUB] - owner
    turn = jnp.where(gap < 0, gap + plan.size, gap)
    count, depth, rows = plan.fine_count, plan.fine_depth, plan.fine_rows
    lane = lanes_of()
    ring = []
    for at in range(0, plan.ring_rows, SUB):
        chosen = rings[0][at : at + SUB]
        for k in range(1, others + 1):
            chosen = jnp.where(turn == k, rings[k][at : at + SUB], chosen)
        ring.append(chosen)
    for t in range(count):
        cells = (lane // depth + t * (LANES // depth)) // 2
        index = cells * plan.depth + (lane % depth) // 2
        for at in range(plan.line_rows // SUB):
            lines[t, SUB * at : SUB * (at + 1)] = take(ring[at], index)
    spread = (lane % depth) // 2

    def ghosts(q, level_id):
        for v in range(NVAR):
            for side, row in enumerate((PAD - 2, PAD + rows)):
                at = 10 * level_id + 5 * side + v
                for t in range(count):
                    q[v, t + 1, row : row + 2] = jnp.broadcast_to(lines[t, at : at + 1], (2, LANES))
        places = [
            (v, side, half) for v in range(NVAR) for side in range(2) for half in range(plan.patch // SUB)
        ]
        moved = []
        for v, side, half in places:
            piece = ((level_id * 2 + side) * NVAR + v) * 2 + half
            tile = ring[plan.line_rows // SUB + piece // 16]
            moved.append(roll(tile, -(piece % 16) * plan.depth))
        moved = [take(tile, spread) for tile in moved]
        for (v, side, half), column in zip(places, moved):
            row = PAD + 2 * SUB * half
            q[v, (count + 1) * side, pl.ds(row, SUB, stride=2)] = column
            q[v, (count + 1) * side, pl.ds(row + 1, SUB, stride=2)] = column

    for v in range(NVAR):
        for t in range(count):
            q[v, t + 1, PAD : PAD + rows] = f_ref[0, v, :, LANES * t : LANES * (t + 1)]
    level = Level(work, count, rows, depth, "flat")
    slopes = level.slopes
    second = (lane >= depth) & (lane < 2 * depth)
    ghosts(q, 0)
    ghosts(q_later, 1)
    for step, (now, later) in enumerate(((q, q_later), (q_later, q))):

        def add(ref, index, value, step=step):
            ref[index] = value if step == 0 else ref[index] + value

        level.prepare(now)
        for side in range(2):
            for t in range(count):
                edge = PAD if side == 0 else PAD + rows
                left = [now[v, t + 1, edge - 1 : edge] for v in range(NVAR)]
                right = [now[v, t + 1, edge : edge + 1] for v in range(NVAR)]
                for v in range(NVAR):
                    if side == 0:
                        right[v] = right[v] - slopes[v, t, 1:2]
                    else:
                        left[v] = left[v] + slopes[v, t, rows : rows + 1]
                flux = flux_of(left, right, 0)
                for v in range(NVAR):
                    add(faces, (t, slice(5 * side + v, 5 * side + v + 1)), flux[v])
        for s in range(rows // SUB):
            here = slice(SUB * s, SUB * (s + 1))
            padded = slice(PAD + SUB * s, PAD + SUB * (s + 1))
            left, right = [], []
            for v in range(NVAR):
                inner = roll(now[v, count, padded] + level.slope[v, count, here], 2 * depth)
                left.append(jnp.where(second, inner, now[v, 0, padded]))
                right.append(jnp.where(second, now[v, count + 1, padded], now[v, 1, padded] - level.slope[v, 1, here]))
            flux = flux_of(left, right, 1)
            for v in range(NVAR):
                add(sides, (v, here), flux[v])

        def store(v, t, s, tile, step=step, later=later):
            later[v, t + 1, PAD + SUB * s : PAD + SUB * (s + 1)] = tile
            if step == 1:
                out_ref[0, v, SUB * s : SUB * (s + 1), LANES * t : LANES * (t + 1)] = tile

        level.finish(now, store)

    within = ((lane % 32) // plan.depth) * (2 * depth) + (lane % plan.depth) * 2

    groups = []
    for v in range(NVAR):
        for half in range(plan.patch // SUB):
            row = PAD + 2 * SUB * half
            groups.append(
                [
                    q[v, t + 1, pl.ds(row, SUB, stride=2)] + q[v, t + 1, pl.ds(row + 1, SUB, stride=2)]
                    for t in range(count)
                ]
            )
    for part in range(2):
        groups.append([faces[t, SUB * part : SUB * (part + 1)] for t in range(count)])
    beside = []
    for v in range(NVAR):
        for half in range(plan.patch // SUB):
            row = 2 * SUB * half
            beside.append(sides[v, pl.ds(row, SUB, stride=2)] + sides[v, pl.ds(row + 1, SUB, stride=2)])
    groups = [[tile + roll(tile, -1) for tile in tiles] for tiles in groups]
    beside = [tile + roll(tile, -1) for tile in beside]
    groups = [[tile + roll(tile, -depth) for tile in tiles] for tiles in groups]
    pair = ((lane // plan.depth) % 2) * depth + (lane % plan.depth) * 2
    beside = [take(tile, pair) for tile in beside]
    groups = [[take(tile, within) for tile in tiles] for tiles in groups]
    packed = []
    for tiles in groups:
        out = tiles[0]
        for t in range(1, count):
            out = jnp.where(lane // 32 == t, tiles[t], out)
        packed.append(0.125 * out)
    halves = plan.patch // SUB
    for at in range(NVAR * halves):
        pay_ref[SUB * at : SUB * (at + 1)] = packed[at]
    for half in range(halves):
        out = beside[half]
        for v in range(1, NVAR):
            out = jnp.where(lane // depth == v, beside[v * halves + half], out)
        at = plan.side_at + SUB * half
        pay_ref[at : at + SUB] = 0.125 * out
    pay_ref[plan.payload_rows - SUB : plan.payload_rows] = owner
    pay_ref[plan.face_at : plan.face_at + SUB] = packed[-2]
    pay_ref[plan.face_at + SUB : plan.face_at + SUB + 2] = packed[-1][0:2]


def outer_kernel(plan, live_ref, c_ref, held_ref, low_ref, high_ref, before_ref, after_ref, out_ref, fine_ref, q, sem, *work):
    put = pltpu.make_async_copy(held_ref, fine_ref, sem)
    put.start()
    count, depth, rows = plan.count, plan.depth, plan.rows
    lane, single = lanes_of(), lanes_of(1)
    split(plan, c_ref, q)
    wide = 2 * depth
    blank = jnp.zeros((PAD, LANES), jnp.float32)
    for v in range(NVAR):
        for t in range(count):
            at = (v * count + t) * 2
            q[v, t + 1, 0:PAD] = blank
            q[v, t + 1, PAD + rows : 2 * PAD + rows] = blank
            q[v, t + 1, PAD - 2 : PAD] = before_ref[at : at + 2]
            q[v, t + 1, PAD + rows : PAD + rows + 2] = after_ref[at : at + 2]
        for s in range(rows // SUB):
            piece = v * (rows // SUB) + s
            at = plan.ring_rows + SUB * (piece // 8)
            slot = piece % 8
            row = PAD + SUB * s
            q[v, 0, row : row + SUB] = roll(low_ref[at : at + SUB], LANES - wide - slot * wide)
            q[v, count + 1, row : row + SUB] = roll(high_ref[at : at + SUB], -slot * wide)
    weight = courant * live_ref[0].astype(jnp.float32)
    level = Level(work, count, rows, depth, "full")
    slopes = level.slopes
    level.prepare(q)

    def store(v, t, s, tile):
        out_ref[v, SUB * s : SUB * (s + 1), LANES * t : LANES * (t + 1)] = tile

    level.finish(q, store)
    half = LANES // 2
    low_lane = (plan.start - 1) * depth
    high_lane = plan.end * depth - LANES
    at_low = (lane >= low_lane) & (lane < low_lane + depth)
    at_high = (lane >= high_lane) & (lane < high_lane + depth)
    for x in range(plan.start, plan.end, SUB):
        here, padded = slice(x, x + SUB), slice(PAD + x, PAD + x + SUB)
        cells = [[q[v, t + 1, padded] for v in range(NVAR)] for t in range(2)]
        slope = [[level.slope[v, t + 1, here] for v in range(NVAR)] for t in range(2)]
        left = [[c + d for c, d in zip(cells[t], slope[t])] for t in range(2)]
        right = [[c - d for c, d in zip(cells[t], slope[t])] for t in range(2)]
        last, first = level.last, level.first
        ahead = [
            jnp.where(last, roll(b, -depth), roll(a, -depth)) for a, b in zip(right[0], right[1])
        ]
        behind = [
            jnp.where(first, roll(a, depth), roll(b, depth)) for a, b in zip(left[0], left[1])
        ]
        low = flux_of(left[0], ahead, 1)
        high = flux_of(behind, right[1], 1)
        for v in range(NVAR):
            out_ref[v, here, 0:LANES] = out_ref[v, here, 0:LANES] + jnp.where(at_low, weight * low[v], 0.0)
            out_ref[v, here, LANES : 2 * LANES] = out_ref[v, here, LANES : 2 * LANES] - jnp.where(
                at_high, weight * high[v], 0.0
            )
    for side, x in enumerate((plan.start - 1, plan.end)):
        face = x if side == 0 else x - 1
        for t in range(2):
            left = [q[v, t + 1, PAD + face : PAD + face + 1] + slopes[v, t, face + 1 : face + 2] for v in range(NVAR)]
            right = [
                q[v, t + 1, PAD + face + 1 : PAD + face + 2] - slopes[v, t, face + 2 : face + 3]
                for v in range(NVAR)
            ]
            flux = flux_of(left, right, 0)
            inner = single >= half if t == 0 else single < half
            signed = weight if side == 0 else -weight
            for v in range(NVAR):
                at = (v, slice(x, x + 1), slice(LANES * t, LANES * (t + 1)))
                out_ref[at] = out_ref[at] + jnp.where(inner, signed * flux[v], 0.0)
    put.wait()


def patch_kernel(plan, others, live_ref, ids_ref, c_ref, *refs):
    payloads = refs[: others + 1]
    out_ref, pay = refs[others + 1 :]
    depth = plan.depth
    lane, single = lanes_of(), lanes_of(1)
    mine = ids_ref[SUB : 2 * SUB]
    owners = [
        jnp.broadcast_to(ref[plan.owner_at : plan.owner_at + 1], (SUB, LANES)) == mine for ref in payloads
    ]
    for at in range(0, plan.payload_rows, SUB):
        chosen = payloads[0][at : at + SUB]
        for k in range(1, others + 1):
            chosen = jnp.where(owners[k], payloads[k][at : at + SUB], chosen)
        pay[at : at + SUB] = chosen
    live = jnp.zeros((SUB, LANES), jnp.float32) + live_ref[0].astype(jnp.float32)
    weight = courant * live
    present = live > 0
    half = LANES // 2
    low_lane = (plan.start - 1) * depth
    high_lane = plan.end * depth - LANES
    at_low = (lane >= low_lane) & (lane < low_lane + depth)
    at_high = (lane >= high_lane) & (lane < high_lane + depth)
    under = (present & (lane >= half), present & (lane < half))
    for v in range(NVAR):
        for x in range(0, plan.rows, SUB):
            here = slice(x, x + SUB)
            tiles = [c_ref[v, here, LANES * t : LANES * (t + 1)] for t in range(plan.count)]
            if plan.start <= x < plan.end:
                base = plan.side_at + x - plan.start
                side = pay[base : base + SUB]
                low = roll(side, low_lane - v * 2 * depth)
                high = roll(side, high_lane - v * 2 * depth - depth)
                tiles[0] = tiles[0] - jnp.where(at_low, weight * low, 0.0)
                tiles[1] = tiles[1] + jnp.where(at_high, weight * high, 0.0)
                base = v * plan.patch + x - plan.start
                average = roll(pay[base : base + SUB], half)
                for t in range(2):
                    tiles[t] = jnp.where(under[t], average, tiles[t])
            for t in range(plan.count):
                out_ref[v, here, LANES * t : LANES * (t + 1)] = tiles[t]
        for side, x in enumerate((plan.start - 1, plan.end)):
            at = plan.face_at + 5 * side + v
            register = roll(pay[at : at + 1], half)
            signed = -weight[0:1] if side == 0 else weight[0:1]
            for t in range(2):
                inner = single >= half if t == 0 else single < half
                at = (v, slice(x, x + 1), slice(LANES * t, LANES * (t + 1)))
                out_ref[at] = c_ref[at] + jnp.where(inner, signed * register, 0.0)


def call(body, out_shape, scratch, flops, moved, spaces, out_spaces=None):
    if out_spaces is None:
        out_spaces = jax.tree.map(lambda _: VMEM, out_shape)
    return pl.pallas_call(
        body,
        out_shape=out_shape,
        in_specs=[pl.BlockSpec(memory_space=space) for space in spaces],
        out_specs=jax.tree.map(lambda space: pl.BlockSpec(memory_space=space), out_spaces),
        scratch_shapes=scratch,
        cost_estimate=pl.CostEstimate(flops=flops, bytes_accessed=moved, transcendentals=0),
        compiler_params=pltpu.CompilerParams(vmem_limit_bytes=16 << 20),
    )


def rotate(array, axis, step):
    size = lax.axis_size(axis)
    return lax.ppermute(array, axis, [(i, (i + step) % size) for i in range(size)])


def shards(coarse_state, fine_state, slot_site, box_live):
    size = lax.axis_size("gy")
    plan = Plan(coarse_state.shape, fine_state.shape, size)
    f32 = jnp.float32
    shape = jax.ShapeDtypeStruct
    smem = pltpu.SMEM
    cells = VMEM((NVAR, plan.count + 2, plan.rows + 2 * PAD, LANES), f32)
    copying = pltpu.SemaphoreType.DMA
    sent = shape((plan.sent_rows, LANES), f32)
    edge = shape((24, LANES), f32)
    held_shape = shape(fine_state.shape, f32)
    coarse_shape = shape(coarse_state.shape, f32)
    up, down, mid, xup, xdown, ids, held, coarse = call(
        partial(coarse_kernel, plan),
        (sent, sent, shape((plan.ring_rows, LANES), f32), edge, edge, edge, held_shape, coarse_shape),
        [cells, VMEM((NVAR, plan.count, plan.rows, LANES), f32), smem((1, 2), jnp.int32), copying((3,))]
        + Level.work(plan.count, plan.rows),
        4_000_000,
        400_000,
        [pltpu.HBM] * 3,
    )(*[pltpu.with_memory_space_constraint(x, pltpu.HBM) for x in (slot_site, coarse_state, fine_state)])
    others = size - 1
    rings = {0: mid}
    for k in range(1, size):
        rings[k] = rotate(up if k == 1 else down if k == size - 1 else mid, "gy", k)
    before = rotate(xup, "gx", 1)
    after = rotate(xdown, "gx", -1)
    fine_cells = VMEM((NVAR, plan.fine_count + 2, plan.fine_rows + 2 * PAD, LANES), f32)
    second, payload = call(
        partial(fine_kernel, plan, others),
        (held_shape, shape((plan.payload_rows, LANES), f32)),
        [
            fine_cells,
            fine_cells,
            VMEM((plan.fine_count, plan.line_rows, LANES), f32),
            VMEM((plan.fine_count, 2 * SUB, LANES), f32),
            VMEM((NVAR, plan.fine_rows, LANES), f32),
        ]
        + Level.work(plan.fine_count, plan.fine_rows),
        16_000_000,
        1_000_000,
        [VMEM, VMEM] + [VMEM] * size,
    )(ids, held, *[rings[k] for k in range(size)])
    payloads = [payload] + [rotate(payload, "gy", k) for k in range(1, size)]
    coarse_new, fine_out = call(
        partial(outer_kernel, plan),
        (coarse_shape, held_shape),
        [cells, copying] + Level.work(plan.count, plan.rows),
        4_000_000,
        400_000,
        [smem] + [VMEM] * 6,
        (VMEM, pltpu.HBM),
    )(box_live, coarse, second, rings[1], rings[size - 1], before, after)
    coarse_out = call(
        partial(patch_kernel, plan, others),
        coarse_shape,
        [VMEM((plan.payload_rows, LANES), f32)],
        400_000,
        400_000,
        [smem, VMEM, VMEM] + [VMEM] * size,
    )(box_live, ids, coarse_new, *payloads)
    return (coarse_out, fine_out)


def solution(mesh):
    return jax.shard_map(
        shards,
        mesh=mesh,
        in_specs=(
            P(None, "gx", "gy"),
            P(("gx", "gy"), None, None, None),
            P(("gx", "gy"), None),
            P(("gx", "gy")),
        ),
        out_specs=(P(None, "gx", "gy"), P(("gx", "gy"), None, None, None)),
        check_vma=False,
    )
```

```python
from functools import partial

import jax
import jax.numpy as jnp
from jax import lax
from jax.experimental import pallas as pl
from jax.experimental.pallas import tpu as pltpu
from jax.sharding import PartitionSpec as P


LANES = 128
SUB = 8
PAD = 8

courant = 0.2
drift = (0.5, 0.3, 0.2)
signal = (1.5, 1.3, 1.2)
PLUS = tuple(0.5 * (a + s) for a, s in zip(drift, signal))
MINUS = tuple(0.5 * (a - s) for a, s in zip(drift, signal))

NVAR = 5
VMEM = pltpu.VMEM


def minmod(first, second):
    return jnp.maximum(jnp.minimum(first, second), jnp.minimum(jnp.maximum(first, second), 0.0))


def lanes_of(rows=SUB):
    return lax.broadcasted_iota(jnp.int32, (rows, LANES), 1)


def roll(values, step):
    step = step % LANES
    return values if step == 0 else pltpu.roll(values, step, 1)


def take(values, index):
    return jnp.take_along_axis(values, index, axis=1, mode="promise_in_bounds")


def coupled(direction):
    return {0: 1 + direction, 1 + direction: 4, 4: 1 + direction}


def flux_of(left, right, direction):
    couples = coupled(direction)
    out = []
    for v in range(NVAR):
        flux = PLUS[direction] * left[v] + MINUS[direction] * right[v]
        if v in couples:
            w = couples[v]
            flux = flux + 0.5 * (left[w] + right[w])
        out.append(flux)
    return out


class Level:
    def __init__(self, work, count, rows, depth, ghosts):
        self.slopes, self.low, self.slope, self.left, self.right = work[:5]
        self.zlow, self.zslope, self.zleft, self.zright = work[5:]
        self.count, self.rows, self.depth, self.ghosts = count, rows, depth, ghosts
        lane = lanes_of()
        self.first = lane < depth
        self.last = lane >= LANES - depth
        place = lane % depth
        self.behind = jnp.where(place == 0, lane + depth - 1, lane - 1)
        self.ahead = jnp.where(place == depth - 1, lane - depth + 1, lane + 1)

    @staticmethod
    def work(count, rows):
        f32 = jnp.float32
        wide = VMEM((NVAR, count + 2, rows, LANES), f32)
        narrow = VMEM((NVAR, count, rows, LANES), f32)
        return [VMEM((NVAR, count, rows + SUB, LANES), f32)] + [wide] * 4 + [narrow] * 4

    def columns(self):
        for v in range(NVAR):
            for s in range(self.rows // SUB):
                yield v, slice(SUB * s, SUB * (s + 1)), slice(PAD + SUB * s, PAD + SUB * (s + 1))

    def tiles(self):
        for v, here, padded in self.columns():
            for t in range(self.count):
                yield v, t, here, padded

    def prepare(self, q):
        count, depth = self.count, self.depth
        full, flat = self.ghosts == "full", self.ghosts == "flat"
        inner = range(1, count + 1)
        for v, here, padded in self.columns():
            cells = {t: q[v, t, padded] for t in range(count + 2)}
            moved = {t: roll(cells[t], depth) for t in inner}
            moved[0] = roll(cells[0], depth) if full else cells[0] if flat else moved[1]
            for t in inner:
                self.low[v, t, here] = cells[t] - jnp.where(self.first, moved[t - 1], moved[t])
            if full:
                top = roll(cells[count + 1], depth)
                self.low[v, 0, here] = cells[0] - moved[0]
                self.low[v, count + 1, here] = cells[count + 1] - jnp.where(self.first, moved[count], top)
            if flat:
                self.low[v, count + 1, here] = cells[count + 1] - moved[count]
        for v, t, here, padded in self.tiles():
            cell = q[v, t + 1, padded]
            self.zlow[v, t, here] = cell - take(cell, self.behind)
        for v in range(NVAR):
            for t in range(count):
                for b in range((self.rows + 2 + SUB - 1) // SUB):
                    row = PAD - 1 + SUB * b
                    cell = q[v, t + 1, row : row + SUB]
                    low = cell - q[v, t + 1, row - 1 : row - 1 + SUB]
                    high = q[v, t + 1, row + 1 : row + 1 + SUB] - cell
                    self.slopes[v, t, SUB * b : SUB * (b + 1)] = 0.5 * minmod(low, high)
        for v, here, padded in self.columns():
            low = {t: self.low[v, t, here] for t in inner}
            moved = {t: roll(low[t], -depth) for t in inner}
            if full or flat:
                low[count + 1] = self.low[v, count + 1, here]
                moved[count + 1] = roll(low[count + 1], -depth)
            else:
                moved[count + 1] = moved[count]
            for t in inner:
                high = jnp.where(self.last, moved[t + 1], moved[t])
                self.slope[v, t, here] = 0.5 * minmod(low[t], high)
            if full:
                low[0] = self.low[v, 0, here]
                high = jnp.where(self.last, moved[1], roll(low[0], -depth))
                self.slope[v, 0, here] = 0.5 * minmod(low[0], high)
                self.slope[v, count + 1, here] = 0.5 * minmod(low[count + 1], moved[count + 1])
        for v, t, here, padded in self.tiles():
            low = self.zlow[v, t, here]
            self.zslope[v, t, here] = 0.5 * minmod(low, take(low, self.ahead))

    def finish(self, q, store):
        count, depth = self.count, self.depth
        full, flat = self.ghosts == "full", self.ghosts == "flat"
        inner = range(1, count + 1)
        for v, t, here, padded in self.tiles():
            slope = self.zslope[v, t, here]
            rise = slope - take(slope, self.behind)
            low = self.zlow[v, t, here]
            self.zleft[v, t, here] = low + rise
            self.zright[v, t, here] = low - rise
        for v, here, padded in self.columns():
            slope = {t: self.slope[v, t, here] for t in inner}
            moved = {t: roll(slope[t], depth) for t in inner}
            if full:
                moved[0] = roll(self.slope[v, 0, here], depth)
            else:
                moved[0] = jnp.zeros((SUB, LANES), jnp.float32) if flat else moved[1]
            for t in inner:
                rise = slope[t] - jnp.where(self.first, moved[t - 1], moved[t])
                low = self.low[v, t, here]
                self.left[v, t, here] = low + rise
                self.right[v, t, here] = low - rise
            if full:
                rise = self.slope[v, count + 1, here] - moved[count]
                self.right[v, count + 1, here] = self.low[v, count + 1, here] - rise
            if flat:
                self.right[v, count + 1, here] = self.low[v, count + 1, here] + moved[count]
        for v, t, here, padded in self.tiles():
            self.zright[v, t, here] = take(self.zright[v, t, here], self.ahead)
        for v, here, padded in self.columns():
            moved = {t: roll(self.right[v, t, here], -depth) for t in inner}
            if full or flat:
                moved[count + 1] = roll(self.right[v, count + 1, here], -depth)
            else:
                moved[count + 1] = moved[count]
            for t in inner:
                self.right[v, t, here] = jnp.where(self.last, moved[t + 1], moved[t])
        for s in range(self.rows // SUB):
            for t in range(count):
                self.gather(q, s, t, store)

    def gather(self, q, s, t, store):
        here = slice(SUB * s, SUB * (s + 1))
        row = PAD + SUB * s
        cell = [q[v, t + 1, row : row + SUB] for v in range(NVAR)]
        acc = [None] * NVAR

        def add(v, term):
            acc[v] = term if acc[v] is None else acc[v] + term

        for direction in range(3):
            couples = coupled(direction)
            for v in range(NVAR):
                if direction == 0:
                    low = cell[v] - q[v, t + 1, row - 1 : row - 1 + SUB]
                    high = q[v, t + 1, row + 1 : row + 1 + SUB] - cell[v]
                    slope = self.slopes[v, t, SUB * s + 1 : SUB * s + 1 + SUB]
                    left = low + (slope - self.slopes[v, t, SUB * s : SUB * s + SUB])
                    right = high - (self.slopes[v, t, SUB * s + 2 : SUB * s + 2 + SUB] - slope)
                elif direction == 1:
                    left, right = self.left[v, t + 1, here], self.right[v, t + 1, here]
                else:
                    left, right = self.zleft[v, t, here], self.zright[v, t, here]
                add(v, (courant * PLUS[direction]) * left + (courant * MINUS[direction]) * right)
                targets = [w for w in couples if couples[w] == v]
                if targets:
                    shared = (0.5 * courant) * (left + right)
                    for w in targets:
                        add(w, shared)
        for v in range(NVAR):
            store(v, t, s, cell[v] - acc[v])


class Plan:
    def __init__(self, coarse, fine, size):
        self.rows = coarse[1]
        self.depth = 8
        self.count = coarse[2] // LANES
        self.fine_rows = fine[2]
        self.fine_depth = 2 * self.depth
        self.fine_count = fine[3] // LANES
        self.patch = self.fine_rows // 2
        self.start = (self.rows - self.patch) // 2
        self.end = self.start + self.patch
        self.size = size
        self.paired = size & (size - 1) == 0
        self.exchanges = list(range(size // 2, size)) + list(range(1, size // 2))
        near = {1, size - 1}
        self.near = [k for k in self.exchanges if any((self.target(i, k) - i) % size in near for i in range(size))]
        self.line_rows = 24
        self.source_at = 20
        self.ring_rows = 48
        self.sent_rows = 72
        self.edge_rows = 24
        self.average_rows = NVAR * self.patch
        self.side_at = self.average_rows
        self.face_at = self.side_at + self.patch
        self.owner_at = self.face_at + 10
        self.payload_rows = self.owner_at + 6


    def target(self, i, k):
        return i ^ k if self.paired else (i + k) % self.size


def split(plan, c_ref, q):
    for v in range(NVAR):
        for t in range(plan.count):
            q[v, t + 1, PAD : PAD + plan.rows] = c_ref[v, :, LANES * t : LANES * (t + 1)]


def window_row(tiles, lane):
    low, high = (roll(tile, LANES // 2) for tile in tiles)
    return jnp.where(lane < LANES // 2, low, high)


def coarse_kernel(
    plan, site_hbm, c_hbm, f_hbm, mid_ref, rows_ref, ids_ref, held_ref, c_ref, *refs
):
    near_refs = refs[: len(plan.near)]
    q, fresh, site_ref, sems = refs[len(plan.near) : len(plan.near) + 4]
    work = refs[len(plan.near) + 4 :]
    me = lax.axis_index("gy")
    loads = [
        pltpu.make_async_copy(source, target, sems.at[index])
        for index, (source, target) in enumerate(
            ((c_hbm, c_ref), (f_hbm, held_ref), (site_hbm, site_ref))
        )
    ]
    for load in loads:
        load.start()
    loads[0].wait()
    split(plan, c_ref, q)
    for v in range(NVAR):
        for t in range(plan.count):
            for edge in (0, PAD + plan.rows):
                q[v, t + 1, edge : edge + PAD] = jnp.zeros((PAD, LANES), jnp.float32)
        for t in (0, plan.count + 1):
            q[v, t, PAD : PAD + plan.rows] = jnp.zeros((plan.rows, LANES), jnp.float32)
    level = Level(work, plan.count, plan.rows, plan.depth, "none")
    level.prepare(q)

    def store(v, t, s, tile):
        row = PAD + SUB * s
        fresh[v, t, SUB * s : SUB * (s + 1)] = 0.5 * (q[v, t + 1, row : row + SUB] + tile)

    level.finish(q, store)
    lane, single = lanes_of(), lanes_of(1)
    sent = (mid_ref, *near_refs)
    blank = jnp.zeros((SUB, LANES), jnp.float32)
    mine = blank + me.astype(jnp.float32)
    for ref in sent:
        ref[16:24] = mine
    for level_id in range(2):
        for side, x in enumerate((plan.start - 1, plan.end)):
            for v in range(NVAR):
                if level_id == 0:
                    tiles = [q[v, t + 1, PAD + x : PAD + x + 1] for t in range(2)]
                else:
                    tiles = [fresh[v, t, x : x + 1] for t in range(2)]
                line = window_row(tiles, single)
                at = 10 * level_id + 5 * side + v
                for ref in sent:
                    ref[at : at + 1] = line
    depth = plan.depth
    low_lane = (plan.start - 1) * depth
    high_lane = plan.end * depth - LANES
    packed = [None] * 3
    for level_id in range(2):
        for side, (t, at) in enumerate(((0, low_lane), (1, high_lane))):
            for v in range(NVAR):
                for half in range(plan.patch // SUB):
                    x = plan.start + SUB * half
                    if level_id == 0:
                        tile = q[v, t + 1, PAD + x : PAD + x + SUB]
                    else:
                        tile = fresh[v, t, x : x + SUB]
                    piece = ((level_id * 2 + side) * NVAR + v) * 2 + half
                    slot = piece % 16
                    moved = roll(tile, slot * depth - at)
                    where, old = piece // 16, packed[piece // 16]
                    packed[where] = moved if old is None else jnp.where(lane // depth == slot, moved, old)
    for index, tile in enumerate(packed):
        for ref in sent:
            ref[plan.line_rows + SUB * index : plan.line_rows + SUB * (index + 1)] = tile
    wide = 2 * depth
    edges = []
    for t, at in ((plan.count - 1, LANES - wide), (0, 0)):
        packed = [None] * 3
        for v in range(NVAR):
            for s in range(plan.rows // SUB):
                piece = v * (plan.rows // SUB) + s
                slot = piece % 8
                moved = roll(q[v, t + 1, PAD + SUB * s : PAD + SUB * (s + 1)], slot * wide - at)
                where, old = piece // 8, packed[piece // 8]
                packed[where] = moved if old is None else jnp.where(lane // wide == slot, moved, old)
        edges.append(packed)
    for k, ref in zip(plan.near, near_refs):
        upward = plan.target(me, k) == (me + 1) % plan.size
        for index in range(3):
            ref[plan.ring_rows + SUB * index : plan.ring_rows + SUB * (index + 1)] = jnp.where(
                upward, edges[0][index], edges[1][index]
            )
    for base, x in ((0, plan.rows - 2), (plan.edge_rows, 0)):
        rows_ref[base + 16 : base + 24] = blank
        for v in range(NVAR):
            for t in range(plan.count):
                at = base + (v * plan.count + t) * 2
                rows_ref[at : at + 2] = q[v, t + 1, PAD + x : PAD + x + 2]
    for load in loads[1:]:
        load.wait()
    zero = jnp.zeros((SUB, LANES), jnp.float32)
    for index, number in enumerate((site_ref[0, 0], me, (me + 1) % plan.size, (me + plan.size - 1) % plan.size)):
        ids_ref[SUB * index : SUB * (index + 1)] = zero + number.astype(jnp.float32)


def fine_kernel(plan, others, ids_ref, f_ref, *refs):
    rings = refs[: others + 1]
    out_ref, pay_ref, q, q_later, lines, faces, sides = refs[others + 1 : others + 8]
    work = refs[others + 8 :]
    owner = ids_ref[0:SUB]
    sources = [jnp.broadcast_to(ref[plan.source_at : plan.source_at + 1], (SUB, LANES)) == owner for ref in rings]
    count, depth, rows = plan.fine_count, plan.fine_depth, plan.fine_rows
    lane = lanes_of()
    ring = []
    for at in range(0, plan.ring_rows, SUB):
        chosen = rings[0][at : at + SUB]
        for k in range(1, others + 1):
            chosen = jnp.where(sources[k], rings[k][at : at + SUB], chosen)
        ring.append(chosen)
    for t in range(count):
        cells = (lane // depth + t * (LANES // depth)) // 2
        index = cells * plan.depth + (lane % depth) // 2
        for at in range(plan.line_rows // SUB):
            lines[t, SUB * at : SUB * (at + 1)] = take(ring[at], index)
    spread = (lane % depth) // 2

    def ghosts(q, level_id):
        for v in range(NVAR):
            for side, row in enumerate((PAD - 2, PAD + rows)):
                at = 10 * level_id + 5 * side + v
                for t in range(count):
                    q[v, t + 1, row : row + 2] = jnp.broadcast_to(lines[t, at : at + 1], (2, LANES))
        places = [
            (v, side, half) for v in range(NVAR) for side in range(2) for half in range(plan.patch // SUB)
        ]
        moved = []
        for v, side, half in places:
            piece = ((level_id * 2 + side) * NVAR + v) * 2 + half
            tile = ring[plan.line_rows // SUB + piece // 16]
            moved.append(roll(tile, -(piece % 16) * plan.depth))
        moved = [take(tile, spread) for tile in moved]
        for (v, side, half), column in zip(places, moved):
            row = PAD + 2 * SUB * half
            q[v, (count + 1) * side, pl.ds(row, SUB, stride=2)] = column
            q[v, (count + 1) * side, pl.ds(row + 1, SUB, stride=2)] = column

    for v in range(NVAR):
        for t in range(count):
            q[v, t + 1, PAD : PAD + rows] = f_ref[0, v, :, LANES * t : LANES * (t + 1)]
    level = Level(work, count, rows, depth, "flat")
    slopes = level.slopes
    second = (lane >= depth) & (lane < 2 * depth)
    ghosts(q, 0)
    ghosts(q_later, 1)
    for step, (now, later) in enumerate(((q, q_later), (q_later, q))):

        def add(ref, index, value, step=step):
            ref[index] = value if step == 0 else ref[index] + value

        level.prepare(now)
        for side in range(2):
            for t in range(count):
                edge = PAD if side == 0 else PAD + rows
                left = [now[v, t + 1, edge - 1 : edge] for v in range(NVAR)]
                right = [now[v, t + 1, edge : edge + 1] for v in range(NVAR)]
                for v in range(NVAR):
                    if side == 0:
                        right[v] = right[v] - slopes[v, t, 1:2]
                    else:
                        left[v] = left[v] + slopes[v, t, rows : rows + 1]
                flux = flux_of(left, right, 0)
                for v in range(NVAR):
                    add(faces, (t, slice(5 * side + v, 5 * side + v + 1)), flux[v])
        for s in range(rows // SUB):
            here = slice(SUB * s, SUB * (s + 1))
            padded = slice(PAD + SUB * s, PAD + SUB * (s + 1))
            left, right = [], []
            for v in range(NVAR):
                inner = roll(now[v, count, padded] + level.slope[v, count, here], 2 * depth)
                left.append(jnp.where(second, inner, now[v, 0, padded]))
                right.append(jnp.where(second, now[v, count + 1, padded], now[v, 1, padded] - level.slope[v, 1, here]))
            flux = flux_of(left, right, 1)
            for v in range(NVAR):
                add(sides, (v, here), flux[v])

        def store(v, t, s, tile, step=step, later=later):
            later[v, t + 1, PAD + SUB * s : PAD + SUB * (s + 1)] = tile
            if step == 1:
                out_ref[0, v, SUB * s : SUB * (s + 1), LANES * t : LANES * (t + 1)] = tile

        level.finish(now, store)

    within = ((lane % 32) // plan.depth) * (2 * depth) + (lane % plan.depth) * 2

    groups = []
    for v in range(NVAR):
        for half in range(plan.patch // SUB):
            row = PAD + 2 * SUB * half
            groups.append(
                [
                    q[v, t + 1, pl.ds(row, SUB, stride=2)] + q[v, t + 1, pl.ds(row + 1, SUB, stride=2)]
                    for t in range(count)
                ]
            )
    for part in range(2):
        groups.append([faces[t, SUB * part : SUB * (part + 1)] for t in range(count)])
    beside = []
    for v in range(NVAR):
        for half in range(plan.patch // SUB):
            row = 2 * SUB * half
            beside.append(sides[v, pl.ds(row, SUB, stride=2)] + sides[v, pl.ds(row + 1, SUB, stride=2)])
    groups = [[tile + roll(tile, -1) for tile in tiles] for tiles in groups]
    beside = [tile + roll(tile, -1) for tile in beside]
    groups = [[tile + roll(tile, -depth) for tile in tiles] for tiles in groups]
    pair = ((lane // plan.depth) % 2) * depth + (lane % plan.depth) * 2
    beside = [take(tile, pair) for tile in beside]
    groups = [[take(tile, within) for tile in tiles] for tiles in groups]
    packed = []
    for tiles in groups:
        out = tiles[0]
        for t in range(1, count):
            out = jnp.where(lane // 32 == t, tiles[t], out)
        packed.append(0.125 * out)
    halves = plan.patch // SUB
    for at in range(NVAR * halves):
        pay_ref[SUB * at : SUB * (at + 1)] = packed[at]
    for half in range(halves):
        out = beside[half]
        for v in range(1, NVAR):
            out = jnp.where(lane // depth == v, beside[v * halves + half], out)
        at = plan.side_at + SUB * half
        pay_ref[at : at + SUB] = 0.125 * out
    pay_ref[plan.payload_rows - SUB : plan.payload_rows] = owner
    pay_ref[plan.face_at : plan.face_at + SUB] = packed[-2]
    pay_ref[plan.face_at + SUB : plan.face_at + SUB + 2] = packed[-1][0:2]


def outer_kernel(plan, live_ref, ids_ref, c_ref, held_ref, before_ref, after_ref, *refs):
    near_refs = refs[: len(plan.near)]
    out_ref, fine_ref, q, sem = refs[len(plan.near) : len(plan.near) + 4]
    work = refs[len(plan.near) + 4 :]
    put = pltpu.make_async_copy(held_ref, fine_ref, sem)
    put.start()
    count, depth, rows = plan.count, plan.depth, plan.rows
    lane, single = lanes_of(), lanes_of(1)
    split(plan, c_ref, q)
    wide = 2 * depth
    blank = jnp.zeros((PAD, LANES), jnp.float32)
    for v in range(NVAR):
        for t in range(count):
            at = (v * count + t) * 2
            q[v, t + 1, 0:PAD] = blank
            q[v, t + 1, PAD + rows : 2 * PAD + rows] = blank
            q[v, t + 1, PAD - 2 : PAD] = before_ref[at : at + 2]
            q[v, t + 1, PAD + rows : PAD + rows + 2] = after_ref[plan.edge_rows + at : plan.edge_rows + at + 2]
    columns = []
    for side in range(2):
        wanted = ids_ref[SUB * (3 - side) : SUB * (4 - side)]
        chosen = [blank] * 3
        for ref in near_refs:
            found = jnp.broadcast_to(ref[plan.source_at : plan.source_at + 1], (SUB, LANES)) == wanted
            for index in range(3):
                at = plan.ring_rows + SUB * index
                chosen[index] = jnp.where(found, ref[at : at + SUB], chosen[index])
        columns.append(chosen)
    for v in range(NVAR):
        for s in range(rows // SUB):
            piece = v * (rows // SUB) + s
            slot = piece % 8
            row = PAD + SUB * s
            q[v, 0, row : row + SUB] = roll(columns[0][piece // 8], LANES - wide - slot * wide)
            q[v, count + 1, row : row + SUB] = roll(columns[1][piece // 8], -slot * wide)
    weight = courant * live_ref[0].astype(jnp.float32)
    level = Level(work, count, rows, depth, "full")
    slopes = level.slopes
    level.prepare(q)

    def store(v, t, s, tile):
        out_ref[v, SUB * s : SUB * (s + 1), LANES * t : LANES * (t + 1)] = tile

    level.finish(q, store)
    half = LANES // 2
    low_lane = (plan.start - 1) * depth
    high_lane = plan.end * depth - LANES
    at_low = (lane >= low_lane) & (lane < low_lane + depth)
    at_high = (lane >= high_lane) & (lane < high_lane + depth)
    for x in range(plan.start, plan.end, SUB):
        here, padded = slice(x, x + SUB), slice(PAD + x, PAD + x + SUB)
        cells = [[q[v, t + 1, padded] for v in range(NVAR)] for t in range(2)]
        slope = [[level.slope[v, t + 1, here] for v in range(NVAR)] for t in range(2)]
        left = [[c + d for c, d in zip(cells[t], slope[t])] for t in range(2)]
        right = [[c - d for c, d in zip(cells[t], slope[t])] for t in range(2)]
        last, first = level.last, level.first
        ahead = [
            jnp.where(last, roll(b, -depth), roll(a, -depth)) for a, b in zip(right[0], right[1])
        ]
        behind = [
            jnp.where(first, roll(a, depth), roll(b, depth)) for a, b in zip(left[0], left[1])
        ]
        low = flux_of(left[0], ahead, 1)
        high = flux_of(behind, right[1], 1)
        for v in range(NVAR):
            out_ref[v, here, 0:LANES] = out_ref[v, here, 0:LANES] + jnp.where(at_low, weight * low[v], 0.0)
            out_ref[v, here, LANES : 2 * LANES] = out_ref[v, here, LANES : 2 * LANES] - jnp.where(
                at_high, weight * high[v], 0.0
            )
    for side, x in enumerate((plan.start - 1, plan.end)):
        face = x if side == 0 else x - 1
        for t in range(2):
            left = [q[v, t + 1, PAD + face : PAD + face + 1] + slopes[v, t, face + 1 : face + 2] for v in range(NVAR)]
            right = [
                q[v, t + 1, PAD + face + 1 : PAD + face + 2] - slopes[v, t, face + 2 : face + 3]
                for v in range(NVAR)
            ]
            flux = flux_of(left, right, 0)
            inner = single >= half if t == 0 else single < half
            signed = weight if side == 0 else -weight
            for v in range(NVAR):
                at = (v, slice(x, x + 1), slice(LANES * t, LANES * (t + 1)))
                out_ref[at] = out_ref[at] + jnp.where(inner, signed * flux[v], 0.0)
    put.wait()


def patch_kernel(plan, others, live_ref, ids_ref, c_ref, *refs):
    payloads = refs[: others + 1]
    out_ref, pay = refs[others + 1 :]
    depth = plan.depth
    lane, single = lanes_of(), lanes_of(1)
    mine = ids_ref[SUB : 2 * SUB]
    owners = [
        jnp.broadcast_to(ref[plan.owner_at : plan.owner_at + 1], (SUB, LANES)) == mine for ref in payloads
    ]
    for at in range(0, plan.payload_rows, SUB):
        chosen = payloads[0][at : at + SUB]
        for k in range(1, others + 1):
            chosen = jnp.where(owners[k], payloads[k][at : at + SUB], chosen)
        pay[at : at + SUB] = chosen
    live = jnp.zeros((SUB, LANES), jnp.float32) + live_ref[0].astype(jnp.float32)
    weight = courant * live
    present = live > 0
    half = LANES // 2
    low_lane = (plan.start - 1) * depth
    high_lane = plan.end * depth - LANES
    at_low = (lane >= low_lane) & (lane < low_lane + depth)
    at_high = (lane >= high_lane) & (lane < high_lane + depth)
    under = (present & (lane >= half), present & (lane < half))
    for v in range(NVAR):
        for x in range(0, plan.rows, SUB):
            here = slice(x, x + SUB)
            tiles = [c_ref[v, here, LANES * t : LANES * (t + 1)] for t in range(plan.count)]
            if plan.start <= x < plan.end:
                base = plan.side_at + x - plan.start
                side = pay[base : base + SUB]
                low = roll(side, low_lane - v * 2 * depth)
                high = roll(side, high_lane - v * 2 * depth - depth)
                tiles[0] = tiles[0] - jnp.where(at_low, weight * low, 0.0)
                tiles[1] = tiles[1] + jnp.where(at_high, weight * high, 0.0)
                base = v * plan.patch + x - plan.start
                average = roll(pay[base : base + SUB], half)
                for t in range(2):
                    tiles[t] = jnp.where(under[t], average, tiles[t])
            for t in range(plan.count):
                out_ref[v, here, LANES * t : LANES * (t + 1)] = tiles[t]
        for side, x in enumerate((plan.start - 1, plan.end)):
            at = plan.face_at + 5 * side + v
            register = roll(pay[at : at + 1], half)
            signed = -weight[0:1] if side == 0 else weight[0:1]
            for t in range(2):
                inner = single >= half if t == 0 else single < half
                at = (v, slice(x, x + 1), slice(LANES * t, LANES * (t + 1)))
                out_ref[at] = c_ref[at] + jnp.where(inner, signed * register, 0.0)


def call(body, out_shape, scratch, flops, moved, spaces, out_spaces=None):
    if out_spaces is None:
        out_spaces = jax.tree.map(lambda _: VMEM, out_shape)
    return pl.pallas_call(
        body,
        out_shape=out_shape,
        in_specs=[pl.BlockSpec(memory_space=space) for space in spaces],
        out_specs=jax.tree.map(lambda space: pl.BlockSpec(memory_space=space), out_spaces),
        scratch_shapes=scratch,
        cost_estimate=pl.CostEstimate(flops=flops, bytes_accessed=moved, transcendentals=0),
        compiler_params=pltpu.CompilerParams(vmem_limit_bytes=16 << 20),
    )


def step(coarse_state, fine_state, slot_site, box_live):
    size = lax.axis_size("gy")
    plan = Plan(coarse_state.shape, fine_state.shape, size)
    f32 = jnp.float32
    shape = jax.ShapeDtypeStruct
    smem = pltpu.SMEM
    cells = VMEM((NVAR, plan.count + 2, plan.rows + 2 * PAD, LANES), f32)
    copying = pltpu.SemaphoreType.DMA
    sent = shape((plan.sent_rows, LANES), f32)
    edge = shape((2 * plan.edge_rows, LANES), f32)
    held_shape = shape(fine_state.shape, f32)
    coarse_shape = shape(coarse_state.shape, f32)
    near = plan.near
    mid, edges, ids, held, coarse, *edged = call(
        partial(coarse_kernel, plan),
        (shape((plan.ring_rows, LANES), f32), edge, shape((4 * SUB, LANES), f32), held_shape, coarse_shape)
        + (sent,) * len(near),
        [cells, VMEM((NVAR, plan.count, plan.rows, LANES), f32), smem((1, 2), jnp.int32), copying((3,))]
        + Level.work(plan.count, plan.rows),
        4_000_000,
        400_000,
        [pltpu.HBM] * 3,
    )(*[pltpu.with_memory_space_constraint(x, pltpu.HBM) for x in (slot_site, coarse_state, fine_state)])
    buffers = dict(zip(near, edged))
    pairs = {k: [(i, plan.target(i, k)) for i in range(size)] for k in plan.exchanges}
    rings = {k: lax.ppermute(buffers.get(k, mid), "gy", pairs[k]) for k in plan.exchanges}
    length = lax.axis_size("gx")
    rise = [(i, (i + 1) % length) for i in range(length)]
    fall = [(j, i) for i, j in rise]
    before = lax.ppermute(edges, "gx", rise)
    after = lax.ppermute(edges, "gx", fall)
    fine_cells = VMEM((NVAR, plan.fine_count + 2, plan.fine_rows + 2 * PAD, LANES), f32)
    second, payload = call(
        partial(fine_kernel, plan, size - 1),
        (held_shape, shape((plan.payload_rows, LANES), f32)),
        [
            fine_cells,
            fine_cells,
            VMEM((plan.fine_count, plan.line_rows, LANES), f32),
            VMEM((plan.fine_count, 2 * SUB, LANES), f32),
            VMEM((NVAR, plan.fine_rows, LANES), f32),
        ]
        + Level.work(plan.fine_count, plan.fine_rows),
        16_000_000,
        1_000_000,
        [VMEM, VMEM] + [VMEM] * size,
    )(ids, held, mid, *[rings[k] for k in plan.exchanges])
    payloads = [payload] + [lax.ppermute(payload, "gy", pairs[k]) for k in plan.exchanges]
    coarse_new, fine_out = call(
        partial(outer_kernel, plan),
        (coarse_shape, held_shape),
        [cells, copying] + Level.work(plan.count, plan.rows),
        4_000_000,
        400_000,
        [smem] + [VMEM] * (5 + len(near)),
        (VMEM, pltpu.HBM),
    )(box_live, ids, coarse, second, before, after, *[rings[k] for k in near])
    coarse_out = call(
        partial(patch_kernel, plan, size - 1),
        coarse_shape,
        [VMEM((plan.payload_rows, LANES), f32)],
        400_000,
        400_000,
        [smem, VMEM, VMEM] + [VMEM] * size,
    )(box_live, ids, coarse_new, *payloads)
    return (coarse_out, fine_out)


def solution(mesh):
    return jax.shard_map(
        step,
        mesh=mesh,
        in_specs=(
            P(None, "gx", "gy"),
            P(("gx", "gy"), None, None, None),
            P(("gx", "gy"), None),
            P(("gx", "gy")),
        ),
        out_specs=(P(None, "gx", "gy"), P(("gx", "gy"), None, None, None)),
        check_vma=False,
    )
```

```python
from functools import partial

import jax
import jax.numpy as jnp
import numpy as np
from jax import lax
from jax.experimental import pallas as pl
from jax.experimental.pallas import tpu as pltpu
from jax.sharding import PartitionSpec as P


LANES = 128
SUB = 8
PAD = 8

courant = 0.2
drift = (0.5, 0.3, 0.2)
signal = (1.5, 1.3, 1.2)
PLUS = tuple(0.5 * (a + s) for a, s in zip(drift, signal))
MINUS = tuple(0.5 * (a - s) for a, s in zip(drift, signal))

NVAR = 5
VMEM = pltpu.VMEM


def minmod(first, second):
    return jnp.maximum(jnp.minimum(first, second), jnp.minimum(jnp.maximum(first, second), 0.0))


def lanes_of(rows=SUB):
    return lax.broadcasted_iota(jnp.int32, (rows, LANES), 1)


def roll(values, step):
    step = step % LANES
    return values if step == 0 else pltpu.roll(values, step, 1)


def take(values, index):
    return jnp.take_along_axis(values, index, axis=1, mode="promise_in_bounds")


def coupled(direction):
    return {0: 1 + direction, 1 + direction: 4, 4: 1 + direction}


def flux_of(left, right, direction):
    couples = coupled(direction)
    out = []
    for v in range(NVAR):
        flux = PLUS[direction] * left[v] + MINUS[direction] * right[v]
        if v in couples:
            w = couples[v]
            flux = flux + 0.5 * (left[w] + right[w])
        out.append(flux)
    return out


class Level:
    def __init__(self, work, count, rows, depth, ghosts, matrix=None):
        self.slopes, self.low, self.slope, self.left, self.right = work[:5]
        self.matrix = matrix
        if matrix is None:
            self.zlow, self.zslope, self.zleft, self.zright = work[5:]
        else:
            self.parts, self.steps, self.rises = work[5:]
        self.count, self.rows, self.depth, self.ghosts = count, rows, depth, ghosts
        lane = lanes_of()
        self.first = lane < depth
        self.last = lane >= LANES - depth
        place = lane % depth
        self.behind = jnp.where(place == 0, lane + depth - 1, lane - 1)
        self.ahead = jnp.where(place == depth - 1, lane - depth + 1, lane + 1)

    @staticmethod
    def work(count, rows, matrix=False):
        f32 = jnp.float32
        wide = VMEM((NVAR, count + 2, rows, LANES), f32)
        narrow = VMEM((NVAR, count, rows, LANES), f32)
        cells = NVAR * count * rows
        along_z = [narrow] * 4
        if matrix:
            along_z = [VMEM((cells, 2 * LANES), jnp.bfloat16)] + [VMEM((cells, 2 * LANES), f32)] * 2
        return [VMEM((NVAR, count, rows + SUB, LANES), f32)] + [wide] * 4 + along_z

    def place(self, v, t, row):
        return (v * self.count + t) * self.rows + row

    def split(self, at, values):
        high = values.astype(jnp.bfloat16)
        rest = (values - high.astype(jnp.float32)).astype(jnp.bfloat16)
        self.parts[at : at + 2 * SUB, 0:LANES] = high
        self.parts[at : at + 2 * SUB, LANES : 2 * LANES] = rest

    def differences(self):
        return jnp.dot(self.parts[...], self.matrix[...], preferred_element_type=jnp.float32)

    def columns(self):
        for v in range(NVAR):
            for s in range(self.rows // SUB):
                yield v, slice(SUB * s, SUB * (s + 1)), slice(PAD + SUB * s, PAD + SUB * (s + 1))

    def tiles(self):
        for v, here, padded in self.columns():
            for t in range(self.count):
                yield v, t, here, padded

    def prepare(self, q):
        count, depth = self.count, self.depth
        full, flat = self.ghosts == "full", self.ghosts == "flat"
        inner = range(1, count + 1)
        for v, here, padded in self.columns():
            cells = {t: q[v, t, padded] for t in range(count + 2)}
            moved = {t: roll(cells[t], depth) for t in inner}
            moved[0] = roll(cells[0], depth) if full else cells[0] if flat else moved[1]
            for t in inner:
                self.low[v, t, here] = cells[t] - jnp.where(self.first, moved[t - 1], moved[t])
            if full:
                top = roll(cells[count + 1], depth)
                self.low[v, 0, here] = cells[0] - moved[0]
                self.low[v, count + 1, here] = cells[count + 1] - jnp.where(self.first, moved[count], top)
            if flat:
                self.low[v, count + 1, here] = cells[count + 1] - moved[count]
        if self.matrix is None:
            for v, t, here, padded in self.tiles():
                cell = q[v, t + 1, padded]
                self.zlow[v, t, here] = cell - take(cell, self.behind)
        else:
            for v in range(NVAR):
                for t in range(count):
                    for row in range(0, self.rows, 2 * SUB):
                        self.split(self.place(v, t, row), q[v, t + 1, PAD + row : PAD + row + 2 * SUB])
            self.steps[...] = self.differences()
        for v in range(NVAR):
            for t in range(count):
                for b in range((self.rows + 2 + SUB - 1) // SUB):
                    row = PAD - 1 + SUB * b
                    cell = q[v, t + 1, row : row + SUB]
                    low = cell - q[v, t + 1, row - 1 : row - 1 + SUB]
                    high = q[v, t + 1, row + 1 : row + 1 + SUB] - cell
                    self.slopes[v, t, SUB * b : SUB * (b + 1)] = 0.5 * minmod(low, high)
        for v, here, padded in self.columns():
            low = {t: self.low[v, t, here] for t in inner}
            moved = {t: roll(low[t], -depth) for t in inner}
            if full or flat:
                low[count + 1] = self.low[v, count + 1, here]
                moved[count + 1] = roll(low[count + 1], -depth)
            else:
                moved[count + 1] = moved[count]
            for t in inner:
                high = jnp.where(self.last, moved[t + 1], moved[t])
                self.slope[v, t, here] = 0.5 * minmod(low[t], high)
            if full:
                low[0] = self.low[v, 0, here]
                high = jnp.where(self.last, moved[1], roll(low[0], -depth))
                self.slope[v, 0, here] = 0.5 * minmod(low[0], high)
                self.slope[v, count + 1, here] = 0.5 * minmod(low[count + 1], moved[count + 1])
        if self.matrix is None:
            for v, t, here, padded in self.tiles():
                low = self.zlow[v, t, here]
                self.zslope[v, t, here] = 0.5 * minmod(low, take(low, self.ahead))
        else:
            for at in range(0, NVAR * count * self.rows, 2 * SUB):
                both = slice(at, at + 2 * SUB)
                self.split(at, 0.5 * minmod(self.steps[both, 0:LANES], self.steps[both, LANES : 2 * LANES]))
            self.rises[...] = self.differences()

    def finish(self, q, store):
        count, depth = self.count, self.depth
        full, flat = self.ghosts == "full", self.ghosts == "flat"
        inner = range(1, count + 1)
        for v, t, here, padded in self.tiles() if self.matrix is None else ():
            slope = self.zslope[v, t, here]
            rise = slope - take(slope, self.behind)
            low = self.zlow[v, t, here]
            self.zleft[v, t, here] = low + rise
            self.zright[v, t, here] = low - rise
        for v, here, padded in self.columns():
            slope = {t: self.slope[v, t, here] for t in inner}
            moved = {t: roll(slope[t], depth) for t in inner}
            if full:
                moved[0] = roll(self.slope[v, 0, here], depth)
            else:
                moved[0] = jnp.zeros((SUB, LANES), jnp.float32) if flat else moved[1]
            for t in inner:
                rise = slope[t] - jnp.where(self.first, moved[t - 1], moved[t])
                low = self.low[v, t, here]
                self.left[v, t, here] = low + rise
                self.right[v, t, here] = low - rise
            if full:
                rise = self.slope[v, count + 1, here] - moved[count]
                self.right[v, count + 1, here] = self.low[v, count + 1, here] - rise
            if flat:
                self.right[v, count + 1, here] = self.low[v, count + 1, here] + moved[count]
        for v, t, here, padded in self.tiles() if self.matrix is None else ():
            self.zright[v, t, here] = take(self.zright[v, t, here], self.ahead)
        for v, here, padded in self.columns():
            moved = {t: roll(self.right[v, t, here], -depth) for t in inner}
            if full or flat:
                moved[count + 1] = roll(self.right[v, count + 1, here], -depth)
            else:
                moved[count + 1] = moved[count]
            for t in inner:
                self.right[v, t, here] = jnp.where(self.last, moved[t + 1], moved[t])
        for s in range(self.rows // SUB):
            for t in range(count):
                self.gather(q, s, t, store)

    def gather(self, q, s, t, store):
        here = slice(SUB * s, SUB * (s + 1))
        row = PAD + SUB * s
        cell = [q[v, t + 1, row : row + SUB] for v in range(NVAR)]
        acc = [None] * NVAR

        def add(v, term):
            acc[v] = term if acc[v] is None else acc[v] + term

        for direction in range(3):
            couples = coupled(direction)
            for v in range(NVAR):
                if direction == 0:
                    low = cell[v] - q[v, t + 1, row - 1 : row - 1 + SUB]
                    high = q[v, t + 1, row + 1 : row + 1 + SUB] - cell[v]
                    slope = self.slopes[v, t, SUB * s + 1 : SUB * s + 1 + SUB]
                    left = low + (slope - self.slopes[v, t, SUB * s : SUB * s + SUB])
                    right = high - (self.slopes[v, t, SUB * s + 2 : SUB * s + 2 + SUB] - slope)
                elif direction == 1:
                    left, right = self.left[v, t + 1, here], self.right[v, t + 1, here]
                elif self.matrix is None:
                    left, right = self.zleft[v, t, here], self.zright[v, t, here]
                else:
                    at = self.place(v, t, SUB * s)
                    at = slice(at, at + SUB)
                    left = self.steps[at, 0:LANES] + self.rises[at, 0:LANES]
                    right = self.steps[at, LANES : 2 * LANES] - self.rises[at, LANES : 2 * LANES]
                add(v, (courant * PLUS[direction]) * left + (courant * MINUS[direction]) * right)
                targets = [w for w in couples if couples[w] == v]
                if targets:
                    shared = (0.5 * courant) * (left + right)
                    for w in targets:
                        add(w, shared)
        for v in range(NVAR):
            store(v, t, s, cell[v] - acc[v])


def z_matrix(depth):
    lane = np.arange(LANES)
    base = lane - lane % depth
    below, above = base + (lane - 1) % depth, base + (lane + 1) % depth
    one = np.eye(LANES, dtype=np.float32)
    half = np.concatenate([one - one[:, below], one[:, above] - one], axis=1)
    return jnp.asarray(np.concatenate([half, half]), jnp.bfloat16)


class Plan:
    def __init__(self, coarse, fine, size):
        self.rows = coarse[1]
        self.depth = 8
        self.count = coarse[2] // LANES
        self.fine_rows = fine[2]
        self.fine_depth = 2 * self.depth
        self.fine_count = fine[3] // LANES
        self.patch = self.fine_rows // 2
        self.start = (self.rows - self.patch) // 2
        self.end = self.start + self.patch
        self.size = size
        self.paired = size & (size - 1) == 0
        self.exchanges = list(range(size // 2, size)) + list(range(1, size // 2))
        near = {1, size - 1}
        self.near = [k for k in self.exchanges if any((self.target(i, k) - i) % size in near for i in range(size))]
        self.line_rows = 24
        self.source_at = 20
        self.ring_rows = 48
        self.sent_rows = 72
        self.edge_rows = 24
        self.average_rows = NVAR * self.patch
        self.side_at = self.average_rows
        self.face_at = self.side_at + self.patch
        self.owner_at = self.face_at + 10
        self.payload_rows = self.owner_at + 6


    def target(self, i, k):
        return i ^ k if self.paired else (i + k) % self.size


def split(plan, c_ref, q):
    for v in range(NVAR):
        for t in range(plan.count):
            q[v, t + 1, PAD : PAD + plan.rows] = c_ref[v, :, LANES * t : LANES * (t + 1)]


def window_row(tiles, lane):
    low, high = (roll(tile, LANES // 2) for tile in tiles)
    return jnp.where(lane < LANES // 2, low, high)


def coarse_kernel(
    plan, site_hbm, c_hbm, f_hbm, mid_ref, rows_ref, ids_ref, held_ref, c_ref, *refs
):
    near_refs = refs[: len(plan.near)]
    q, fresh, site_ref, sems = refs[len(plan.near) : len(plan.near) + 4]
    work = refs[len(plan.near) + 4 :]
    me = lax.axis_index("gy")
    loads = [
        pltpu.make_async_copy(source, target, sems.at[index])
        for index, (source, target) in enumerate(
            ((c_hbm, c_ref), (f_hbm, held_ref), (site_hbm, site_ref))
        )
    ]
    for load in loads:
        load.start()
    loads[0].wait()
    split(plan, c_ref, q)
    for v in range(NVAR):
        for t in range(plan.count):
            for edge in (0, PAD + plan.rows):
                q[v, t + 1, edge : edge + PAD] = jnp.zeros((PAD, LANES), jnp.float32)
        for t in (0, plan.count + 1):
            q[v, t, PAD : PAD + plan.rows] = jnp.zeros((plan.rows, LANES), jnp.float32)
    level = Level(work, plan.count, plan.rows, plan.depth, "none")
    level.prepare(q)

    def store(v, t, s, tile):
        row = PAD + SUB * s
        fresh[v, t, SUB * s : SUB * (s + 1)] = 0.5 * (q[v, t + 1, row : row + SUB] + tile)

    level.finish(q, store)
    lane, single = lanes_of(), lanes_of(1)
    sent = (mid_ref, *near_refs)
    blank = jnp.zeros((SUB, LANES), jnp.float32)
    mine = blank + me.astype(jnp.float32)
    for ref in sent:
        ref[16:24] = mine
    for level_id in range(2):
        for side, x in enumerate((plan.start - 1, plan.end)):
            for v in range(NVAR):
                if level_id == 0:
                    tiles = [q[v, t + 1, PAD + x : PAD + x + 1] for t in range(2)]
                else:
                    tiles = [fresh[v, t, x : x + 1] for t in range(2)]
                line = window_row(tiles, single)
                at = 10 * level_id + 5 * side + v
                for ref in sent:
                    ref[at : at + 1] = line
    depth = plan.depth
    low_lane = (plan.start - 1) * depth
    high_lane = plan.end * depth - LANES
    packed = [None] * 3
    for level_id in range(2):
        for side, (t, at) in enumerate(((0, low_lane), (1, high_lane))):
            for v in range(NVAR):
                for half in range(plan.patch // SUB):
                    x = plan.start + SUB * half
                    if level_id == 0:
                        tile = q[v, t + 1, PAD + x : PAD + x + SUB]
                    else:
                        tile = fresh[v, t, x : x + SUB]
                    piece = ((level_id * 2 + side) * NVAR + v) * 2 + half
                    slot = piece % 16
                    moved = roll(tile, slot * depth - at)
                    where, old = piece // 16, packed[piece // 16]
                    packed[where] = moved if old is None else jnp.where(lane // depth == slot, moved, old)
    for index, tile in enumerate(packed):
        for ref in sent:
            ref[plan.line_rows + SUB * index : plan.line_rows + SUB * (index + 1)] = tile
    wide = 2 * depth
    edges = []
    for t, at in ((plan.count - 1, LANES - wide), (0, 0)):
        packed = [None] * 3
        for v in range(NVAR):
            for s in range(plan.rows // SUB):
                piece = v * (plan.rows // SUB) + s
                slot = piece % 8
                moved = roll(q[v, t + 1, PAD + SUB * s : PAD + SUB * (s + 1)], slot * wide - at)
                where, old = piece // 8, packed[piece // 8]
                packed[where] = moved if old is None else jnp.where(lane // wide == slot, moved, old)
        edges.append(packed)
    for k, ref in zip(plan.near, near_refs):
        upward = plan.target(me, k) == (me + 1) % plan.size
        for index in range(3):
            ref[plan.ring_rows + SUB * index : plan.ring_rows + SUB * (index + 1)] = jnp.where(
                upward, edges[0][index], edges[1][index]
            )
    for base, x in ((0, plan.rows - 2), (plan.edge_rows, 0)):
        rows_ref[base + 16 : base + 24] = blank
        for v in range(NVAR):
            for t in range(plan.count):
                at = base + (v * plan.count + t) * 2
                rows_ref[at : at + 2] = q[v, t + 1, PAD + x : PAD + x + 2]
    for load in loads[1:]:
        load.wait()
    zero = jnp.zeros((SUB, LANES), jnp.float32)
    for index, number in enumerate((site_ref[0, 0], me, (me + 1) % plan.size, (me + plan.size - 1) % plan.size)):
        ids_ref[SUB * index : SUB * (index + 1)] = zero + number.astype(jnp.float32)


def fine_kernel(plan, others, ids_ref, matrix_ref, f_ref, *refs):
    rings = refs[: others + 1]
    out_ref, pay_ref, q, q_later, lines, faces, sides = refs[others + 1 : others + 8]
    work = refs[others + 8 :]
    owner = ids_ref[0:SUB]
    sources = [jnp.broadcast_to(ref[plan.source_at : plan.source_at + 1], (SUB, LANES)) == owner for ref in rings]
    count, depth, rows = plan.fine_count, plan.fine_depth, plan.fine_rows
    lane = lanes_of()
    ring = []
    for at in range(0, plan.ring_rows, SUB):
        chosen = rings[0][at : at + SUB]
        for k in range(1, others + 1):
            chosen = jnp.where(sources[k], rings[k][at : at + SUB], chosen)
        ring.append(chosen)
    for t in range(count):
        cells = (lane // depth + t * (LANES // depth)) // 2
        index = cells * plan.depth + (lane % depth) // 2
        for at in range(plan.line_rows // SUB):
            lines[t, SUB * at : SUB * (at + 1)] = take(ring[at], index)
    spread = (lane % depth) // 2

    def ghosts(q, level_id):
        for v in range(NVAR):
            for side, row in enumerate((PAD - 2, PAD + rows)):
                at = 10 * level_id + 5 * side + v
                for t in range(count):
                    q[v, t + 1, row : row + 2] = jnp.broadcast_to(lines[t, at : at + 1], (2, LANES))
        places = [
            (v, side, half) for v in range(NVAR) for side in range(2) for half in range(plan.patch // SUB)
        ]
        moved = []
        for v, side, half in places:
            piece = ((level_id * 2 + side) * NVAR + v) * 2 + half
            tile = ring[plan.line_rows // SUB + piece // 16]
            moved.append(roll(tile, -(piece % 16) * plan.depth))
        moved = [take(tile, spread) for tile in moved]
        for (v, side, half), column in zip(places, moved):
            row = PAD + 2 * SUB * half
            q[v, (count + 1) * side, pl.ds(row, SUB, stride=2)] = column
            q[v, (count + 1) * side, pl.ds(row + 1, SUB, stride=2)] = column

    for v in range(NVAR):
        for t in range(count):
            q[v, t + 1, PAD : PAD + rows] = f_ref[0, v, :, LANES * t : LANES * (t + 1)]
    level = Level(work, count, rows, depth, "flat", matrix_ref)
    slopes = level.slopes
    second = (lane >= depth) & (lane < 2 * depth)
    ghosts(q, 0)
    ghosts(q_later, 1)
    for step, (now, later) in enumerate(((q, q_later), (q_later, q))):

        def add(ref, index, value, step=step):
            ref[index] = value if step == 0 else ref[index] + value

        level.prepare(now)
        for side in range(2):
            for t in range(count):
                edge = PAD if side == 0 else PAD + rows
                left = [now[v, t + 1, edge - 1 : edge] for v in range(NVAR)]
                right = [now[v, t + 1, edge : edge + 1] for v in range(NVAR)]
                for v in range(NVAR):
                    if side == 0:
                        right[v] = right[v] - slopes[v, t, 1:2]
                    else:
                        left[v] = left[v] + slopes[v, t, rows : rows + 1]
                flux = flux_of(left, right, 0)
                for v in range(NVAR):
                    add(faces, (t, slice(5 * side + v, 5 * side + v + 1)), flux[v])
        for s in range(rows // SUB):
            here = slice(SUB * s, SUB * (s + 1))
            padded = slice(PAD + SUB * s, PAD + SUB * (s + 1))
            left, right = [], []
            for v in range(NVAR):
                inner = roll(now[v, count, padded] + level.slope[v, count, here], 2 * depth)
                left.append(jnp.where(second, inner, now[v, 0, padded]))
                right.append(jnp.where(second, now[v, count + 1, padded], now[v, 1, padded] - level.slope[v, 1, here]))
            flux = flux_of(left, right, 1)
            for v in range(NVAR):
                add(sides, (v, here), flux[v])

        def store(v, t, s, tile, step=step, later=later):
            later[v, t + 1, PAD + SUB * s : PAD + SUB * (s + 1)] = tile
            if step == 1:
                out_ref[0, v, SUB * s : SUB * (s + 1), LANES * t : LANES * (t + 1)] = tile

        level.finish(now, store)

    within = ((lane % 32) // plan.depth) * (2 * depth) + (lane % plan.depth) * 2

    groups = []
    for v in range(NVAR):
        for half in range(plan.patch // SUB):
            row = PAD + 2 * SUB * half
            groups.append(
                [
                    q[v, t + 1, pl.ds(row, SUB, stride=2)] + q[v, t + 1, pl.ds(row + 1, SUB, stride=2)]
                    for t in range(count)
                ]
            )
    for part in range(2):
        groups.append([faces[t, SUB * part : SUB * (part + 1)] for t in range(count)])
    beside = []
    for v in range(NVAR):
        for half in range(plan.patch // SUB):
            row = 2 * SUB * half
            beside.append(sides[v, pl.ds(row, SUB, stride=2)] + sides[v, pl.ds(row + 1, SUB, stride=2)])
    groups = [[tile + roll(tile, -1) for tile in tiles] for tiles in groups]
    beside = [tile + roll(tile, -1) for tile in beside]
    groups = [[tile + roll(tile, -depth) for tile in tiles] for tiles in groups]
    pair = ((lane // plan.depth) % 2) * depth + (lane % plan.depth) * 2
    beside = [take(tile, pair) for tile in beside]
    groups = [[take(tile, within) for tile in tiles] for tiles in groups]
    packed = []
    for tiles in groups:
        out = tiles[0]
        for t in range(1, count):
            out = jnp.where(lane // 32 == t, tiles[t], out)
        packed.append(0.125 * out)
    halves = plan.patch // SUB
    for at in range(NVAR * halves):
        pay_ref[SUB * at : SUB * (at + 1)] = packed[at]
    for half in range(halves):
        out = beside[half]
        for v in range(1, NVAR):
            out = jnp.where(lane // depth == v, beside[v * halves + half], out)
        at = plan.side_at + SUB * half
        pay_ref[at : at + SUB] = 0.125 * out
    pay_ref[plan.payload_rows - SUB : plan.payload_rows] = owner
    pay_ref[plan.face_at : plan.face_at + SUB] = packed[-2]
    pay_ref[plan.face_at + SUB : plan.face_at + SUB + 2] = packed[-1][0:2]


def outer_kernel(plan, live_ref, ids_ref, c_ref, held_ref, before_ref, after_ref, *refs):
    near_refs = refs[: len(plan.near)]
    out_ref, fine_ref, q, sem = refs[len(plan.near) : len(plan.near) + 4]
    work = refs[len(plan.near) + 4 :]
    put = pltpu.make_async_copy(held_ref, fine_ref, sem)
    put.start()
    count, depth, rows = plan.count, plan.depth, plan.rows
    lane, single = lanes_of(), lanes_of(1)
    split(plan, c_ref, q)
    wide = 2 * depth
    blank = jnp.zeros((PAD, LANES), jnp.float32)
    for v in range(NVAR):
        for t in range(count):
            at = (v * count + t) * 2
            q[v, t + 1, 0:PAD] = blank
            q[v, t + 1, PAD + rows : 2 * PAD + rows] = blank
            q[v, t + 1, PAD - 2 : PAD] = before_ref[at : at + 2]
            q[v, t + 1, PAD + rows : PAD + rows + 2] = after_ref[plan.edge_rows + at : plan.edge_rows + at + 2]
    columns = []
    for side in range(2):
        wanted = ids_ref[SUB * (3 - side) : SUB * (4 - side)]
        chosen = [blank] * 3
        for ref in near_refs:
            found = jnp.broadcast_to(ref[plan.source_at : plan.source_at + 1], (SUB, LANES)) == wanted
            for index in range(3):
                at = plan.ring_rows + SUB * index
                chosen[index] = jnp.where(found, ref[at : at + SUB], chosen[index])
        columns.append(chosen)
    for v in range(NVAR):
        for s in range(rows // SUB):
            piece = v * (rows // SUB) + s
            slot = piece % 8
            row = PAD + SUB * s
            q[v, 0, row : row + SUB] = roll(columns[0][piece // 8], LANES - wide - slot * wide)
            q[v, count + 1, row : row + SUB] = roll(columns[1][piece // 8], -slot * wide)
    weight = courant * live_ref[0].astype(jnp.float32)
    level = Level(work, count, rows, depth, "full")
    slopes = level.slopes
    level.prepare(q)

    def store(v, t, s, tile):
        out_ref[v, SUB * s : SUB * (s + 1), LANES * t : LANES * (t + 1)] = tile

    level.finish(q, store)
    half = LANES // 2
    low_lane = (plan.start - 1) * depth
    high_lane = plan.end * depth - LANES
    at_low = (lane >= low_lane) & (lane < low_lane + depth)
    at_high = (lane >= high_lane) & (lane < high_lane + depth)
    for x in range(plan.start, plan.end, SUB):
        here, padded = slice(x, x + SUB), slice(PAD + x, PAD + x + SUB)
        cells = [[q[v, t + 1, padded] for v in range(NVAR)] for t in range(2)]
        slope = [[level.slope[v, t + 1, here] for v in range(NVAR)] for t in range(2)]
        left = [[c + d for c, d in zip(cells[t], slope[t])] for t in range(2)]
        right = [[c - d for c, d in zip(cells[t], slope[t])] for t in range(2)]
        last, first = level.last, level.first
        ahead = [
            jnp.where(last, roll(b, -depth), roll(a, -depth)) for a, b in zip(right[0], right[1])
        ]
        behind = [
            jnp.where(first, roll(a, depth), roll(b, depth)) for a, b in zip(left[0], left[1])
        ]
        low = flux_of(left[0], ahead, 1)
        high = flux_of(behind, right[1], 1)
        for v in range(NVAR):
            out_ref[v, here, 0:LANES] = out_ref[v, here, 0:LANES] + jnp.where(at_low, weight * low[v], 0.0)
            out_ref[v, here, LANES : 2 * LANES] = out_ref[v, here, LANES : 2 * LANES] - jnp.where(
                at_high, weight * high[v], 0.0
            )
    for side, x in enumerate((plan.start - 1, plan.end)):
        face = x if side == 0 else x - 1
        for t in range(2):
            left = [q[v, t + 1, PAD + face : PAD + face + 1] + slopes[v, t, face + 1 : face + 2] for v in range(NVAR)]
            right = [
                q[v, t + 1, PAD + face + 1 : PAD + face + 2] - slopes[v, t, face + 2 : face + 3]
                for v in range(NVAR)
            ]
            flux = flux_of(left, right, 0)
            inner = single >= half if t == 0 else single < half
            signed = weight if side == 0 else -weight
            for v in range(NVAR):
                at = (v, slice(x, x + 1), slice(LANES * t, LANES * (t + 1)))
                out_ref[at] = out_ref[at] + jnp.where(inner, signed * flux[v], 0.0)
    put.wait()


def patch_kernel(plan, others, live_ref, ids_ref, c_ref, *refs):
    payloads = refs[: others + 1]
    out_ref, pay = refs[others + 1 :]
    depth = plan.depth
    lane, single = lanes_of(), lanes_of(1)
    mine = ids_ref[SUB : 2 * SUB]
    owners = [
        jnp.broadcast_to(ref[plan.owner_at : plan.owner_at + 1], (SUB, LANES)) == mine for ref in payloads
    ]
    for at in range(0, plan.payload_rows, SUB):
        chosen = payloads[0][at : at + SUB]
        for k in range(1, others + 1):
            chosen = jnp.where(owners[k], payloads[k][at : at + SUB], chosen)
        pay[at : at + SUB] = chosen
    live = jnp.zeros((SUB, LANES), jnp.float32) + live_ref[0].astype(jnp.float32)
    weight = courant * live
    present = live > 0
    half = LANES // 2
    low_lane = (plan.start - 1) * depth
    high_lane = plan.end * depth - LANES
    at_low = (lane >= low_lane) & (lane < low_lane + depth)
    at_high = (lane >= high_lane) & (lane < high_lane + depth)
    under = (present & (lane >= half), present & (lane < half))
    for v in range(NVAR):
        for x in range(0, plan.rows, SUB):
            here = slice(x, x + SUB)
            tiles = [c_ref[v, here, LANES * t : LANES * (t + 1)] for t in range(plan.count)]
            if plan.start <= x < plan.end:
                base = plan.side_at + x - plan.start
                side = pay[base : base + SUB]
                low = roll(side, low_lane - v * 2 * depth)
                high = roll(side, high_lane - v * 2 * depth - depth)
                tiles[0] = tiles[0] - jnp.where(at_low, weight * low, 0.0)
                tiles[1] = tiles[1] + jnp.where(at_high, weight * high, 0.0)
                base = v * plan.patch + x - plan.start
                average = roll(pay[base : base + SUB], half)
                for t in range(2):
                    tiles[t] = jnp.where(under[t], average, tiles[t])
            for t in range(plan.count):
                out_ref[v, here, LANES * t : LANES * (t + 1)] = tiles[t]
        for side, x in enumerate((plan.start - 1, plan.end)):
            at = plan.face_at + 5 * side + v
            register = roll(pay[at : at + 1], half)
            signed = -weight[0:1] if side == 0 else weight[0:1]
            for t in range(2):
                inner = single >= half if t == 0 else single < half
                at = (v, slice(x, x + 1), slice(LANES * t, LANES * (t + 1)))
                out_ref[at] = c_ref[at] + jnp.where(inner, signed * register, 0.0)


def call(body, out_shape, scratch, flops, moved, spaces, out_spaces=None):
    if out_spaces is None:
        out_spaces = jax.tree.map(lambda _: VMEM, out_shape)
    return pl.pallas_call(
        body,
        out_shape=out_shape,
        in_specs=[pl.BlockSpec(memory_space=space) for space in spaces],
        out_specs=jax.tree.map(lambda space: pl.BlockSpec(memory_space=space), out_spaces),
        scratch_shapes=scratch,
        cost_estimate=pl.CostEstimate(flops=flops, bytes_accessed=moved, transcendentals=0),
        compiler_params=pltpu.CompilerParams(vmem_limit_bytes=16 << 20),
    )


def step(coarse_state, fine_state, slot_site, box_live):
    size = lax.axis_size("gy")
    plan = Plan(coarse_state.shape, fine_state.shape, size)
    f32 = jnp.float32
    shape = jax.ShapeDtypeStruct
    smem = pltpu.SMEM
    cells = VMEM((NVAR, plan.count + 2, plan.rows + 2 * PAD, LANES), f32)
    copying = pltpu.SemaphoreType.DMA
    sent = shape((plan.sent_rows, LANES), f32)
    edge = shape((2 * plan.edge_rows, LANES), f32)
    held_shape = shape(fine_state.shape, f32)
    coarse_shape = shape(coarse_state.shape, f32)
    near = plan.near
    mid, edges, ids, held, coarse, *edged = call(
        partial(coarse_kernel, plan),
        (shape((plan.ring_rows, LANES), f32), edge, shape((4 * SUB, LANES), f32), held_shape, coarse_shape)
        + (sent,) * len(near),
        [cells, VMEM((NVAR, plan.count, plan.rows, LANES), f32), smem((1, 2), jnp.int32), copying((3,))]
        + Level.work(plan.count, plan.rows),
        4_000_000,
        400_000,
        [pltpu.HBM] * 3,
    )(*[pltpu.with_memory_space_constraint(x, pltpu.HBM) for x in (slot_site, coarse_state, fine_state)])
    buffers = dict(zip(near, edged))
    pairs = {k: [(i, plan.target(i, k)) for i in range(size)] for k in plan.exchanges}
    rings = {k: lax.ppermute(buffers.get(k, mid), "gy", pairs[k]) for k in plan.exchanges}
    length = lax.axis_size("gx")
    rise = [(i, (i + 1) % length) for i in range(length)]
    fall = [(j, i) for i, j in rise]
    before = lax.ppermute(edges, "gx", rise)
    after = lax.ppermute(edges, "gx", fall)
    fine_cells = VMEM((NVAR, plan.fine_count + 2, plan.fine_rows + 2 * PAD, LANES), f32)
    second, payload = call(
        partial(fine_kernel, plan, size - 1),
        (held_shape, shape((plan.payload_rows, LANES), f32)),
        [
            fine_cells,
            fine_cells,
            VMEM((plan.fine_count, plan.line_rows, LANES), f32),
            VMEM((plan.fine_count, 2 * SUB, LANES), f32),
            VMEM((NVAR, plan.fine_rows, LANES), f32),
        ]
        + Level.work(plan.fine_count, plan.fine_rows, True),
        16_000_000,
        1_000_000,
        [VMEM, VMEM, VMEM] + [VMEM] * size,
    )(ids, z_matrix(plan.fine_depth), held, mid, *[rings[k] for k in plan.exchanges])
    payloads = [payload] + [lax.ppermute(payload, "gy", pairs[k]) for k in plan.exchanges]
    coarse_new, fine_out = call(
        partial(outer_kernel, plan),
        (coarse_shape, held_shape),
        [cells, copying] + Level.work(plan.count, plan.rows),
        4_000_000,
        400_000,
        [smem] + [VMEM] * (5 + len(near)),
        (VMEM, pltpu.HBM),
    )(box_live, ids, coarse, second, before, after, *[rings[k] for k in near])
    coarse_out = call(
        partial(patch_kernel, plan, size - 1),
        coarse_shape,
        [VMEM((plan.payload_rows, LANES), f32)],
        400_000,
        400_000,
        [smem, VMEM, VMEM] + [VMEM] * size,
    )(box_live, ids, coarse_new, *payloads)
    return (coarse_out, fine_out)


def solution(mesh):
    return jax.shard_map(
        step,
        mesh=mesh,
        in_specs=(
            P(None, "gx", "gy"),
            P(("gx", "gy"), None, None, None),
            P(("gx", "gy"), None),
            P(("gx", "gy")),
        ),
        out_specs=(P(None, "gx", "gy"), P(("gx", "gy"), None, None, None)),
        check_vma=False,
    )
```

```python
from functools import partial

import jax
import jax.numpy as jnp
import numpy as np
from jax import lax
from jax.experimental import pallas as pl
from jax.experimental.pallas import tpu as pltpu
from jax.sharding import PartitionSpec as P


LANES = 128
SUB = 8
PAD = 8

courant = 0.2
drift = (0.5, 0.3, 0.2)
signal = (1.5, 1.3, 1.2)
PLUS = tuple(0.5 * (a + s) for a, s in zip(drift, signal))
MINUS = tuple(0.5 * (a - s) for a, s in zip(drift, signal))
assert all(abs(m + 0.5) < 1e-12 for m in MINUS)

NVAR = 5
VMEM = pltpu.VMEM


def minmod(first, second):
    return jnp.maximum(jnp.minimum(first, second), jnp.minimum(jnp.maximum(first, second), 0.0))


def lanes_of(rows=SUB):
    return lax.broadcasted_iota(jnp.int32, (rows, LANES), 1)


def roll(values, step):
    step = step % LANES
    return values if step == 0 else pltpu.roll(values, step, 1)


def take(values, index):
    return jnp.take_along_axis(values, index, axis=1, mode="promise_in_bounds")


def coupled(direction):
    return {0: 1 + direction, 1 + direction: 4, 4: 1 + direction}


def flux_of(left, right, direction):
    couples = coupled(direction)
    out = []
    for v in range(NVAR):
        flux = PLUS[direction] * left[v] + MINUS[direction] * right[v]
        if v in couples:
            w = couples[v]
            flux = flux + 0.5 * (left[w] + right[w])
        out.append(flux)
    return out


class Level:
    def __init__(self, work, count, rows, depth, ghosts, matrix=None):
        self.jumps, self.slopes, self.low, self.slope, self.left, self.right = work[:6]
        self.matrix = matrix
        if matrix is None:
            self.zlow, self.zslope, self.zleft, self.zright = work[6:]
        else:
            self.parts, self.steps, self.rises = work[6:]
        self.count, self.rows, self.depth, self.ghosts = count, rows, depth, ghosts
        lane = lanes_of()
        self.first = lane < depth
        self.last = lane >= LANES - depth
        place = lane % depth
        self.behind = jnp.where(place == 0, lane + depth - 1, lane - 1)
        self.ahead = jnp.where(place == depth - 1, lane - depth + 1, lane + 1)

    @staticmethod
    def work(count, rows, matrix=False):
        f32 = jnp.float32
        wide = VMEM((NVAR, count + 2, rows, LANES), f32)
        narrow = VMEM((NVAR, count, rows, LANES), f32)
        cells = NVAR * count * rows
        along_z = [narrow] * 4
        if matrix:
            along_z = [VMEM((cells, 2 * LANES), jnp.bfloat16)] + [VMEM((cells, 2 * LANES), f32)] * 2
        jumps = VMEM((NVAR, count, rows + 2 * SUB, LANES), f32)
        return [jumps, VMEM((NVAR, count, rows + SUB, LANES), f32)] + [wide] * 4 + along_z

    def place(self, v, t, row):
        return (v * self.count + t) * self.rows + row

    def split(self, at, values):
        high = values.astype(jnp.bfloat16)
        rest = (values - high.astype(jnp.float32)).astype(jnp.bfloat16)
        self.parts[at : at + 2 * SUB, 0:LANES] = high
        self.parts[at : at + 2 * SUB, LANES : 2 * LANES] = rest

    def differences(self, index):
        return jnp.dot(self.parts[...], self.matrix[index], preferred_element_type=jnp.float32)

    def columns(self):
        for v in range(NVAR):
            for s in range(self.rows // SUB):
                yield v, slice(SUB * s, SUB * (s + 1)), slice(PAD + SUB * s, PAD + SUB * (s + 1))

    def tiles(self):
        for v, here, padded in self.columns():
            for t in range(self.count):
                yield v, t, here, padded

    def prepare(self, q):
        count, depth = self.count, self.depth
        full, flat = self.ghosts == "full", self.ghosts == "flat"
        inner = range(1, count + 1)
        for v, here, padded in self.columns():
            cells = {t: q[v, t, padded] for t in range(count + 2)}
            moved = {t: roll(cells[t], depth) for t in inner}
            moved[0] = roll(cells[0], depth) if full else cells[0] if flat else moved[1]
            for t in inner:
                self.low[v, t, here] = cells[t] - jnp.where(self.first, moved[t - 1], moved[t])
            if full:
                top = roll(cells[count + 1], depth)
                self.low[v, 0, here] = cells[0] - moved[0]
                self.low[v, count + 1, here] = cells[count + 1] - jnp.where(self.first, moved[count], top)
            if flat:
                self.low[v, count + 1, here] = cells[count + 1] - moved[count]
        if self.matrix is None:
            for v, t, here, padded in self.tiles():
                cell = q[v, t + 1, padded]
                self.zlow[v, t, here] = cell - take(cell, self.behind)
        else:
            for v in range(NVAR):
                for t in range(count):
                    for row in range(0, self.rows, 2 * SUB):
                        self.split(self.place(v, t, row), q[v, t + 1, PAD + row : PAD + row + 2 * SUB])
            self.steps[...] = self.differences(0)
        for v in range(NVAR):
            for t in range(count):
                for at in range(0, self.rows + 3, SUB):
                    row = PAD - 2 + at
                    self.jumps[v, t, at : at + SUB] = (
                        q[v, t + 1, row + 1 : row + 1 + SUB] - q[v, t + 1, row : row + SUB]
                    )
        for v in range(NVAR):
            for t in range(count):
                for at in range(0, self.rows + 2, SUB):
                    low, high = self.jumps[v, t, at : at + SUB], self.jumps[v, t, at + 1 : at + 1 + SUB]
                    self.slopes[v, t, at : at + SUB] = 0.5 * minmod(low, high)
        for v, here, padded in self.columns():
            low = {t: self.low[v, t, here] for t in inner}
            moved = {t: roll(low[t], -depth) for t in inner}
            if full or flat:
                low[count + 1] = self.low[v, count + 1, here]
                moved[count + 1] = roll(low[count + 1], -depth)
            else:
                moved[count + 1] = moved[count]
            for t in inner:
                high = jnp.where(self.last, moved[t + 1], moved[t])
                self.slope[v, t, here] = 0.5 * minmod(low[t], high)
            if full:
                low[0] = self.low[v, 0, here]
                high = jnp.where(self.last, moved[1], roll(low[0], -depth))
                self.slope[v, 0, here] = 0.5 * minmod(low[0], high)
                self.slope[v, count + 1, here] = 0.5 * minmod(low[count + 1], moved[count + 1])
        if self.matrix is None:
            for v, t, here, padded in self.tiles():
                low = self.zlow[v, t, here]
                self.zslope[v, t, here] = 0.5 * minmod(low, take(low, self.ahead))
        else:
            for at in range(0, NVAR * count * self.rows, 2 * SUB):
                both = slice(at, at + 2 * SUB)
                self.split(at, minmod(self.steps[both, 0:LANES], self.steps[both, LANES : 2 * LANES]))
            self.rises[...] = self.differences(1)

    def finish(self, q, store):
        count, depth = self.count, self.depth
        full, flat = self.ghosts == "full", self.ghosts == "flat"
        inner = range(1, count + 1)
        for v, t, here, padded in self.tiles() if self.matrix is None else ():
            slope = self.zslope[v, t, here]
            rise = slope - take(slope, self.behind)
            low = self.zlow[v, t, here]
            self.zleft[v, t, here] = low + rise
            self.zright[v, t, here] = low - rise
        for v, here, padded in self.columns():
            slope = {t: self.slope[v, t, here] for t in inner}
            moved = {t: roll(slope[t], depth) for t in inner}
            if full:
                moved[0] = roll(self.slope[v, 0, here], depth)
            else:
                moved[0] = jnp.zeros((SUB, LANES), jnp.float32) if flat else moved[1]
            for t in inner:
                rise = slope[t] - jnp.where(self.first, moved[t - 1], moved[t])
                low = self.low[v, t, here]
                self.left[v, t, here] = low + rise
                self.right[v, t, here] = low - rise
            if full:
                rise = self.slope[v, count + 1, here] - moved[count]
                self.right[v, count + 1, here] = self.low[v, count + 1, here] - rise
            if flat:
                self.right[v, count + 1, here] = self.low[v, count + 1, here] + moved[count]
        for v, t, here, padded in self.tiles() if self.matrix is None else ():
            self.zright[v, t, here] = take(self.zright[v, t, here], self.ahead)
        for v, here, padded in self.columns():
            moved = {t: roll(self.right[v, t, here], -depth) for t in inner}
            if full or flat:
                moved[count + 1] = roll(self.right[v, count + 1, here], -depth)
            else:
                moved[count + 1] = moved[count]
            for t in inner:
                self.right[v, t, here] = jnp.where(self.last, moved[t + 1], moved[t])
        for s in range(self.rows // SUB):
            for t in range(count):
                self.gather(q, s, t, store)

    def gather(self, q, s, t, store):
        here = slice(SUB * s, SUB * (s + 1))
        row = PAD + SUB * s
        cell = [q[v, t + 1, row : row + SUB] for v in range(NVAR)]
        lefts, rights = [None] * NVAR, [None] * NVAR

        def add(acc, v, term):
            acc[v] = term if acc[v] is None else acc[v] + term

        for direction in range(3):
            couples = coupled(direction)
            for v in range(NVAR):
                if direction == 0:
                    slope = self.slopes[v, t, SUB * s + 1 : SUB * s + 1 + SUB]
                    rise = slope - self.slopes[v, t, SUB * s : SUB * s + SUB]
                    fall = self.slopes[v, t, SUB * s + 2 : SUB * s + 2 + SUB] - slope
                    left = self.jumps[v, t, SUB * s + 1 : SUB * s + 1 + SUB] + rise
                    right = self.jumps[v, t, SUB * s + 2 : SUB * s + 2 + SUB] - fall
                elif direction == 1:
                    left, right = self.left[v, t + 1, here], self.right[v, t + 1, here]
                elif self.matrix is None:
                    left, right = self.zleft[v, t, here], self.zright[v, t, here]
                else:
                    at = self.place(v, t, SUB * s)
                    at = slice(at, at + SUB)
                    left = self.steps[at, 0:LANES] + self.rises[at, 0:LANES]
                    right = self.steps[at, LANES : 2 * LANES] - self.rises[at, LANES : 2 * LANES]
                add(lefts, v, 2.0 * PLUS[direction] * left)
                add(rights, v, right)
                targets = [w for w in couples if couples[w] == v]
                if targets:
                    shared = left + right
                    for w in targets:
                        add(lefts, w, shared)
        for v in range(NVAR):
            store(v, t, s, cell[v] - (0.5 * courant) * (lefts[v] - rights[v]))


def z_matrix(depth):
    lane = np.arange(LANES)
    base = lane - lane % depth
    below, above = base + (lane - 1) % depth, base + (lane + 1) % depth
    one = np.eye(LANES, dtype=np.float32)
    half = np.concatenate([one - one[:, below], one[:, above] - one], axis=1)
    whole = np.concatenate([half, half])
    return jnp.asarray(np.stack([whole, 0.5 * whole]), jnp.bfloat16)


class Plan:
    def __init__(self, coarse, fine, size):
        self.rows = coarse[1]
        self.depth = 8
        self.count = coarse[2] // LANES
        self.fine_rows = fine[2]
        self.fine_depth = 2 * self.depth
        self.fine_count = fine[3] // LANES
        self.patch = self.fine_rows // 2
        self.start = (self.rows - self.patch) // 2
        self.end = self.start + self.patch
        self.size = size
        self.paired = size & (size - 1) == 0
        self.exchanges = list(range(size // 2, size)) + list(range(1, size // 2))
        near = {1, size - 1}
        self.near = [k for k in self.exchanges if any((self.target(i, k) - i) % size in near for i in range(size))]
        self.line_rows = 24
        self.source_at = 20
        self.ring_rows = 48
        self.sent_rows = 72
        self.edge_rows = 24
        self.average_rows = NVAR * self.patch
        self.side_at = self.average_rows
        self.face_at = self.side_at + self.patch
        self.owner_at = self.face_at + 10
        self.payload_rows = self.owner_at + 6


    def target(self, i, k):
        return i ^ k if self.paired else (i + k) % self.size


def split(plan, c_ref, q):
    for v in range(NVAR):
        for t in range(plan.count):
            q[v, t + 1, PAD : PAD + plan.rows] = c_ref[v, :, LANES * t : LANES * (t + 1)]


def window_row(tiles, lane):
    low, high = (roll(tile, LANES // 2) for tile in tiles)
    return jnp.where(lane < LANES // 2, low, high)


def coarse_kernel(
    plan, site_hbm, c_hbm, f_hbm, matrix_hbm, mid_ref, rows_ref, ids_ref, held_ref, c_ref, *refs
):
    near_refs = refs[: len(plan.near)]
    q, fresh, site_ref, matrix_ref, sems = refs[len(plan.near) : len(plan.near) + 5]
    work = refs[len(plan.near) + 5 :]
    me = lax.axis_index("gy")
    loads = [
        pltpu.make_async_copy(source, target, sems.at[index])
        for index, (source, target) in enumerate(
            ((c_hbm, c_ref), (matrix_hbm, matrix_ref), (f_hbm, held_ref), (site_hbm, site_ref))
        )
    ]
    for load in loads:
        load.start()
    loads[0].wait()
    split(plan, c_ref, q)
    for v in range(NVAR):
        for t in range(plan.count):
            for edge in (0, PAD + plan.rows):
                q[v, t + 1, edge : edge + PAD] = jnp.zeros((PAD, LANES), jnp.float32)
        for t in (0, plan.count + 1):
            q[v, t, PAD : PAD + plan.rows] = jnp.zeros((plan.rows, LANES), jnp.float32)
    level = Level(work, plan.count, plan.rows, plan.depth, "none", matrix_ref)
    loads[1].wait()
    level.prepare(q)

    def store(v, t, s, tile):
        row = PAD + SUB * s
        fresh[v, t, SUB * s : SUB * (s + 1)] = 0.5 * (q[v, t + 1, row : row + SUB] + tile)

    level.finish(q, store)
    lane, single = lanes_of(), lanes_of(1)
    sent = (mid_ref, *near_refs)
    blank = jnp.zeros((SUB, LANES), jnp.float32)
    mine = blank + me.astype(jnp.float32)
    for ref in sent:
        ref[16:24] = mine
    for level_id in range(2):
        for side, x in enumerate((plan.start - 1, plan.end)):
            for v in range(NVAR):
                if level_id == 0:
                    tiles = [q[v, t + 1, PAD + x : PAD + x + 1] for t in range(2)]
                else:
                    tiles = [fresh[v, t, x : x + 1] for t in range(2)]
                line = window_row(tiles, single)
                at = 10 * level_id + 5 * side + v
                for ref in sent:
                    ref[at : at + 1] = line
    depth = plan.depth
    low_lane = (plan.start - 1) * depth
    high_lane = plan.end * depth - LANES
    packed = [None] * 3
    for level_id in range(2):
        for side, (t, at) in enumerate(((0, low_lane), (1, high_lane))):
            for v in range(NVAR):
                for half in range(plan.patch // SUB):
                    x = plan.start + SUB * half
                    if level_id == 0:
                        tile = q[v, t + 1, PAD + x : PAD + x + SUB]
                    else:
                        tile = fresh[v, t, x : x + SUB]
                    piece = ((level_id * 2 + side) * NVAR + v) * 2 + half
                    slot = piece % 16
                    moved = roll(tile, slot * depth - at)
                    where, old = piece // 16, packed[piece // 16]
                    packed[where] = moved if old is None else jnp.where(lane // depth == slot, moved, old)
    for index, tile in enumerate(packed):
        for ref in sent:
            ref[plan.line_rows + SUB * index : plan.line_rows + SUB * (index + 1)] = tile
    wide = 2 * depth
    edges = []
    for t, at in ((plan.count - 1, LANES - wide), (0, 0)):
        packed = [None] * 3
        for v in range(NVAR):
            for s in range(plan.rows // SUB):
                piece = v * (plan.rows // SUB) + s
                slot = piece % 8
                moved = roll(q[v, t + 1, PAD + SUB * s : PAD + SUB * (s + 1)], slot * wide - at)
                where, old = piece // 8, packed[piece // 8]
                packed[where] = moved if old is None else jnp.where(lane // wide == slot, moved, old)
        edges.append(packed)
    for k, ref in zip(plan.near, near_refs):
        upward = plan.target(me, k) == (me + 1) % plan.size
        for index in range(3):
            ref[plan.ring_rows + SUB * index : plan.ring_rows + SUB * (index + 1)] = jnp.where(
                upward, edges[0][index], edges[1][index]
            )
    for base, x in ((0, plan.rows - 2), (plan.edge_rows, 0)):
        rows_ref[base + 16 : base + 24] = blank
        for v in range(NVAR):
            for t in range(plan.count):
                at = base + (v * plan.count + t) * 2
                rows_ref[at : at + 2] = q[v, t + 1, PAD + x : PAD + x + 2]
    for load in loads[2:]:
        load.wait()
    zero = jnp.zeros((SUB, LANES), jnp.float32)
    for index, number in enumerate((site_ref[0, 0], me, (me + 1) % plan.size, (me + plan.size - 1) % plan.size)):
        ids_ref[SUB * index : SUB * (index + 1)] = zero + number.astype(jnp.float32)


def fine_kernel(plan, others, ids_ref, matrix_ref, f_ref, *refs):
    rings = refs[: others + 1]
    out_ref, pay_ref, q, q_later, lines, faces, sides = refs[others + 1 : others + 8]
    work = refs[others + 8 :]
    owner = ids_ref[0:SUB]
    sources = [jnp.broadcast_to(ref[plan.source_at : plan.source_at + 1], (SUB, LANES)) == owner for ref in rings]
    count, depth, rows = plan.fine_count, plan.fine_depth, plan.fine_rows
    lane = lanes_of()
    ring = []
    for at in range(0, plan.ring_rows, SUB):
        chosen = rings[0][at : at + SUB]
        for k in range(1, others + 1):
            chosen = jnp.where(sources[k], rings[k][at : at + SUB], chosen)
        ring.append(chosen)
    for t in range(count):
        cells = (lane // depth + t * (LANES // depth)) // 2
        index = cells * plan.depth + (lane % depth) // 2
        for at in range(plan.line_rows // SUB):
            lines[t, SUB * at : SUB * (at + 1)] = take(ring[at], index)
    spread = (lane % depth) // 2

    def ghosts(q, level_id):
        for v in range(NVAR):
            for side, row in enumerate((PAD - 2, PAD + rows)):
                at = 10 * level_id + 5 * side + v
                for t in range(count):
                    q[v, t + 1, row : row + 2] = jnp.broadcast_to(lines[t, at : at + 1], (2, LANES))
        places = [
            (v, side, half) for v in range(NVAR) for side in range(2) for half in range(plan.patch // SUB)
        ]
        moved = []
        for v, side, half in places:
            piece = ((level_id * 2 + side) * NVAR + v) * 2 + half
            tile = ring[plan.line_rows // SUB + piece // 16]
            moved.append(roll(tile, -(piece % 16) * plan.depth))
        moved = [take(tile, spread) for tile in moved]
        for (v, side, half), column in zip(places, moved):
            row = PAD + 2 * SUB * half
            q[v, (count + 1) * side, pl.ds(row, SUB, stride=2)] = column
            q[v, (count + 1) * side, pl.ds(row + 1, SUB, stride=2)] = column

    for v in range(NVAR):
        for t in range(count):
            q[v, t + 1, PAD : PAD + rows] = f_ref[0, v, :, LANES * t : LANES * (t + 1)]
    level = Level(work, count, rows, depth, "flat", matrix_ref)
    slopes = level.slopes
    second = (lane >= depth) & (lane < 2 * depth)
    ghosts(q, 0)
    ghosts(q_later, 1)
    for step, (now, later) in enumerate(((q, q_later), (q_later, q))):

        def add(ref, index, value, step=step):
            ref[index] = value if step == 0 else ref[index] + value

        level.prepare(now)
        for side in range(2):
            for t in range(count):
                edge = PAD if side == 0 else PAD + rows
                left = [now[v, t + 1, edge - 1 : edge] for v in range(NVAR)]
                right = [now[v, t + 1, edge : edge + 1] for v in range(NVAR)]
                for v in range(NVAR):
                    if side == 0:
                        right[v] = right[v] - slopes[v, t, 1:2]
                    else:
                        left[v] = left[v] + slopes[v, t, rows : rows + 1]
                flux = flux_of(left, right, 0)
                for v in range(NVAR):
                    add(faces, (t, slice(5 * side + v, 5 * side + v + 1)), flux[v])
        for s in range(rows // SUB):
            here = slice(SUB * s, SUB * (s + 1))
            padded = slice(PAD + SUB * s, PAD + SUB * (s + 1))
            left, right = [], []
            for v in range(NVAR):
                inner = roll(now[v, count, padded] + level.slope[v, count, here], 2 * depth)
                left.append(jnp.where(second, inner, now[v, 0, padded]))
                right.append(jnp.where(second, now[v, count + 1, padded], now[v, 1, padded] - level.slope[v, 1, here]))
            flux = flux_of(left, right, 1)
            for v in range(NVAR):
                add(sides, (v, here), flux[v])

        def store(v, t, s, tile, step=step, later=later):
            later[v, t + 1, PAD + SUB * s : PAD + SUB * (s + 1)] = tile
            if step == 1:
                out_ref[0, v, SUB * s : SUB * (s + 1), LANES * t : LANES * (t + 1)] = tile

        level.finish(now, store)

    within = ((lane % 32) // plan.depth) * (2 * depth) + (lane % plan.depth) * 2

    groups = []
    for v in range(NVAR):
        for half in range(plan.patch // SUB):
            row = PAD + 2 * SUB * half
            groups.append(
                [
                    q[v, t + 1, pl.ds(row, SUB, stride=2)] + q[v, t + 1, pl.ds(row + 1, SUB, stride=2)]
                    for t in range(count)
                ]
            )
    for part in range(2):
        groups.append([faces[t, SUB * part : SUB * (part + 1)] for t in range(count)])
    beside = []
    for v in range(NVAR):
        for half in range(plan.patch // SUB):
            row = 2 * SUB * half
            beside.append(sides[v, pl.ds(row, SUB, stride=2)] + sides[v, pl.ds(row + 1, SUB, stride=2)])
    groups = [[tile + roll(tile, -1) for tile in tiles] for tiles in groups]
    beside = [tile + roll(tile, -1) for tile in beside]
    groups = [[tile + roll(tile, -depth) for tile in tiles] for tiles in groups]
    pair = ((lane // plan.depth) % 2) * depth + (lane % plan.depth) * 2
    beside = [take(tile, pair) for tile in beside]
    groups = [[take(tile, within) for tile in tiles] for tiles in groups]
    packed = []
    for tiles in groups:
        out = tiles[0]
        for t in range(1, count):
            out = jnp.where(lane // 32 == t, tiles[t], out)
        packed.append(0.125 * out)
    halves = plan.patch // SUB
    for at in range(NVAR * halves):
        pay_ref[SUB * at : SUB * (at + 1)] = packed[at]
    for half in range(halves):
        out = beside[half]
        for v in range(1, NVAR):
            out = jnp.where(lane // depth == v, beside[v * halves + half], out)
        at = plan.side_at + SUB * half
        pay_ref[at : at + SUB] = 0.125 * out
    pay_ref[plan.payload_rows - SUB : plan.payload_rows] = owner
    pay_ref[plan.face_at : plan.face_at + SUB] = packed[-2]
    pay_ref[plan.face_at + SUB : plan.face_at + SUB + 2] = packed[-1][0:2]


def outer_kernel(plan, live_ref, ids_ref, c_ref, held_ref, before_ref, after_ref, *refs):
    near_refs = refs[: len(plan.near)]
    out_ref, fine_ref, q, sem = refs[len(plan.near) : len(plan.near) + 4]
    work = refs[len(plan.near) + 4 :]
    put = pltpu.make_async_copy(held_ref, fine_ref, sem)
    put.start()
    count, depth, rows = plan.count, plan.depth, plan.rows
    lane, single = lanes_of(), lanes_of(1)
    split(plan, c_ref, q)
    wide = 2 * depth
    blank = jnp.zeros((PAD, LANES), jnp.float32)
    for v in range(NVAR):
        for t in range(count):
            at = (v * count + t) * 2
            q[v, t + 1, 0:PAD] = blank
            q[v, t + 1, PAD + rows : 2 * PAD + rows] = blank
            q[v, t + 1, PAD - 2 : PAD] = before_ref[at : at + 2]
            q[v, t + 1, PAD + rows : PAD + rows + 2] = after_ref[plan.edge_rows + at : plan.edge_rows + at + 2]
    columns = []
    for side in range(2):
        wanted = ids_ref[SUB * (3 - side) : SUB * (4 - side)]
        chosen = [blank] * 3
        for ref in near_refs:
            found = jnp.broadcast_to(ref[plan.source_at : plan.source_at + 1], (SUB, LANES)) == wanted
            for index in range(3):
                at = plan.ring_rows + SUB * index
                chosen[index] = jnp.where(found, ref[at : at + SUB], chosen[index])
        columns.append(chosen)
    for v in range(NVAR):
        for s in range(rows // SUB):
            piece = v * (rows // SUB) + s
            slot = piece % 8
            row = PAD + SUB * s
            q[v, 0, row : row + SUB] = roll(columns[0][piece // 8], LANES - wide - slot * wide)
            q[v, count + 1, row : row + SUB] = roll(columns[1][piece // 8], -slot * wide)
    weight = courant * live_ref[0].astype(jnp.float32)
    level = Level(work, count, rows, depth, "full")
    slopes = level.slopes
    level.prepare(q)

    def store(v, t, s, tile):
        out_ref[v, SUB * s : SUB * (s + 1), LANES * t : LANES * (t + 1)] = tile

    level.finish(q, store)
    half = LANES // 2
    low_lane = (plan.start - 1) * depth
    high_lane = plan.end * depth - LANES
    at_low = (lane >= low_lane) & (lane < low_lane + depth)
    at_high = (lane >= high_lane) & (lane < high_lane + depth)
    for x in range(plan.start, plan.end, SUB):
        here, padded = slice(x, x + SUB), slice(PAD + x, PAD + x + SUB)
        cells = [[q[v, t + 1, padded] for v in range(NVAR)] for t in range(2)]
        slope = [[level.slope[v, t + 1, here] for v in range(NVAR)] for t in range(2)]
        left = [[c + d for c, d in zip(cells[t], slope[t])] for t in range(2)]
        right = [[c - d for c, d in zip(cells[t], slope[t])] for t in range(2)]
        last, first = level.last, level.first
        ahead = [
            jnp.where(last, roll(b, -depth), roll(a, -depth)) for a, b in zip(right[0], right[1])
        ]
        behind = [
            jnp.where(first, roll(a, depth), roll(b, depth)) for a, b in zip(left[0], left[1])
        ]
        low = flux_of(left[0], ahead, 1)
        high = flux_of(behind, right[1], 1)
        for v in range(NVAR):
            out_ref[v, here, 0:LANES] = out_ref[v, here, 0:LANES] + jnp.where(at_low, weight * low[v], 0.0)
            out_ref[v, here, LANES : 2 * LANES] = out_ref[v, here, LANES : 2 * LANES] - jnp.where(
                at_high, weight * high[v], 0.0
            )
    for side, x in enumerate((plan.start - 1, plan.end)):
        face = x if side == 0 else x - 1
        for t in range(2):
            left = [q[v, t + 1, PAD + face : PAD + face + 1] + slopes[v, t, face + 1 : face + 2] for v in range(NVAR)]
            right = [
                q[v, t + 1, PAD + face + 1 : PAD + face + 2] - slopes[v, t, face + 2 : face + 3]
                for v in range(NVAR)
            ]
            flux = flux_of(left, right, 0)
            inner = single >= half if t == 0 else single < half
            signed = weight if side == 0 else -weight
            for v in range(NVAR):
                at = (v, slice(x, x + 1), slice(LANES * t, LANES * (t + 1)))
                out_ref[at] = out_ref[at] + jnp.where(inner, signed * flux[v], 0.0)
    put.wait()


def patch_kernel(plan, others, live_ref, ids_ref, c_ref, *refs):
    payloads = refs[: others + 1]
    out_ref, pay = refs[others + 1 :]
    depth = plan.depth
    lane, single = lanes_of(), lanes_of(1)
    mine = ids_ref[SUB : 2 * SUB]
    owners = [
        jnp.broadcast_to(ref[plan.owner_at : plan.owner_at + 1], (SUB, LANES)) == mine for ref in payloads
    ]
    for at in range(0, plan.payload_rows, SUB):
        chosen = payloads[0][at : at + SUB]
        for k in range(1, others + 1):
            chosen = jnp.where(owners[k], payloads[k][at : at + SUB], chosen)
        pay[at : at + SUB] = chosen
    live = jnp.zeros((SUB, LANES), jnp.float32) + live_ref[0].astype(jnp.float32)
    weight = courant * live
    present = live > 0
    half = LANES // 2
    low_lane = (plan.start - 1) * depth
    high_lane = plan.end * depth - LANES
    at_low = (lane >= low_lane) & (lane < low_lane + depth)
    at_high = (lane >= high_lane) & (lane < high_lane + depth)
    under = (present & (lane >= half), present & (lane < half))
    for v in range(NVAR):
        for x in range(0, plan.rows, SUB):
            here = slice(x, x + SUB)
            tiles = [c_ref[v, here, LANES * t : LANES * (t + 1)] for t in range(plan.count)]
            if plan.start <= x < plan.end:
                base = plan.side_at + x - plan.start
                side = pay[base : base + SUB]
                low = roll(side, low_lane - v * 2 * depth)
                high = roll(side, high_lane - v * 2 * depth - depth)
                tiles[0] = tiles[0] - jnp.where(at_low, weight * low, 0.0)
                tiles[1] = tiles[1] + jnp.where(at_high, weight * high, 0.0)
                base = v * plan.patch + x - plan.start
                average = roll(pay[base : base + SUB], half)
                for t in range(2):
                    tiles[t] = jnp.where(under[t], average, tiles[t])
            for t in range(plan.count):
                out_ref[v, here, LANES * t : LANES * (t + 1)] = tiles[t]
        for side, x in enumerate((plan.start - 1, plan.end)):
            at = plan.face_at + 5 * side + v
            register = roll(pay[at : at + 1], half)
            signed = -weight[0:1] if side == 0 else weight[0:1]
            for t in range(2):
                inner = single >= half if t == 0 else single < half
                at = (v, slice(x, x + 1), slice(LANES * t, LANES * (t + 1)))
                out_ref[at] = c_ref[at] + jnp.where(inner, signed * register, 0.0)


def call(body, out_shape, scratch, flops, moved, spaces, out_spaces=None):
    if out_spaces is None:
        out_spaces = jax.tree.map(lambda _: VMEM, out_shape)
    return pl.pallas_call(
        body,
        out_shape=out_shape,
        in_specs=[pl.BlockSpec(memory_space=space) for space in spaces],
        out_specs=jax.tree.map(lambda space: pl.BlockSpec(memory_space=space), out_spaces),
        scratch_shapes=scratch,
        cost_estimate=pl.CostEstimate(flops=flops, bytes_accessed=moved, transcendentals=0),
        compiler_params=pltpu.CompilerParams(vmem_limit_bytes=16 << 20),
    )


def step(coarse_state, fine_state, slot_site, box_live):
    size = lax.axis_size("gy")
    plan = Plan(coarse_state.shape, fine_state.shape, size)
    f32 = jnp.float32
    shape = jax.ShapeDtypeStruct
    smem = pltpu.SMEM
    cells = VMEM((NVAR, plan.count + 2, plan.rows + 2 * PAD, LANES), f32)
    copying = pltpu.SemaphoreType.DMA
    sent = shape((plan.sent_rows, LANES), f32)
    edge = shape((2 * plan.edge_rows, LANES), f32)
    held_shape = shape(fine_state.shape, f32)
    coarse_shape = shape(coarse_state.shape, f32)
    near = plan.near
    matrix = z_matrix(plan.depth)
    mid, edges, ids, held, coarse, *edged = call(
        partial(coarse_kernel, plan),
        (shape((plan.ring_rows, LANES), f32), edge, shape((4 * SUB, LANES), f32), held_shape, coarse_shape)
        + (sent,) * len(near),
        [cells, VMEM((NVAR, plan.count, plan.rows, LANES), f32), smem((1, 2), jnp.int32)]
        + [VMEM(matrix.shape, matrix.dtype), copying((4,))]
        + Level.work(plan.count, plan.rows, True),
        4_000_000,
        400_000,
        [pltpu.HBM] * 4,
    )(*[pltpu.with_memory_space_constraint(x, pltpu.HBM) for x in (slot_site, coarse_state, fine_state, matrix)])
    buffers = dict(zip(near, edged))
    pairs = {k: [(i, plan.target(i, k)) for i in range(size)] for k in plan.exchanges}
    rings = {k: lax.ppermute(buffers.get(k, mid), "gy", pairs[k]) for k in plan.exchanges}
    length = lax.axis_size("gx")
    rise = [(i, (i + 1) % length) for i in range(length)]
    fall = [(j, i) for i, j in rise]
    before = lax.ppermute(edges, "gx", rise)
    after = lax.ppermute(edges, "gx", fall)
    fine_cells = VMEM((NVAR, plan.fine_count + 2, plan.fine_rows + 2 * PAD, LANES), f32)
    second, payload = call(
        partial(fine_kernel, plan, size - 1),
        (held_shape, shape((plan.payload_rows, LANES), f32)),
        [
            fine_cells,
            fine_cells,
            VMEM((plan.fine_count, plan.line_rows, LANES), f32),
            VMEM((plan.fine_count, 2 * SUB, LANES), f32),
            VMEM((NVAR, plan.fine_rows, LANES), f32),
        ]
        + Level.work(plan.fine_count, plan.fine_rows, True),
        16_000_000,
        1_000_000,
        [VMEM, VMEM, VMEM] + [VMEM] * size,
    )(ids, z_matrix(plan.fine_depth), held, mid, *[rings[k] for k in plan.exchanges])
    payloads = [payload] + [lax.ppermute(payload, "gy", pairs[k]) for k in plan.exchanges]
    coarse_new, fine_out = call(
        partial(outer_kernel, plan),
        (coarse_shape, held_shape),
        [cells, copying] + Level.work(plan.count, plan.rows),
        4_000_000,
        400_000,
        [smem] + [VMEM] * (5 + len(near)),
        (VMEM, pltpu.HBM),
    )(box_live, ids, coarse, second, before, after, *[rings[k] for k in near])
    coarse_out = call(
        partial(patch_kernel, plan, size - 1),
        coarse_shape,
        [VMEM((plan.payload_rows, LANES), f32)],
        400_000,
        400_000,
        [smem, VMEM, VMEM] + [VMEM] * size,
    )(box_live, ids, coarse_new, *payloads)
    return (coarse_out, fine_out)


def solution(mesh):
    return jax.shard_map(
        step,
        mesh=mesh,
        in_specs=(
            P(None, "gx", "gy"),
            P(("gx", "gy"), None, None, None),
            P(("gx", "gy"), None),
            P(("gx", "gy")),
        ),
        out_specs=(P(None, "gx", "gy"), P(("gx", "gy"), None, None, None)),
        check_vma=False,
    )
```

```python
from functools import partial

import jax
import jax.numpy as jnp
import numpy as np
from jax import lax
from jax.experimental import pallas as pl
from jax.experimental.pallas import tpu as pltpu
from jax.sharding import PartitionSpec as P


LANES = 128
SUB = 8
PAD = 8

courant = 0.2
drift = (0.5, 0.3, 0.2)
signal = (1.5, 1.3, 1.2)
PLUS = tuple(0.5 * (a + s) for a, s in zip(drift, signal))
MINUS = tuple(0.5 * (a - s) for a, s in zip(drift, signal))
assert all(abs(m + 0.5) < 1e-12 for m in MINUS)

NVAR = 5
VMEM = pltpu.VMEM


def minmod(first, second):
    return jnp.maximum(jnp.minimum(first, second), jnp.minimum(jnp.maximum(first, second), 0.0))


def lanes_of(rows=SUB):
    return lax.broadcasted_iota(jnp.int32, (rows, LANES), 1)


def roll(values, step):
    step = step % LANES
    return values if step == 0 else pltpu.roll(values, step, 1)


def take(values, index):
    return jnp.take_along_axis(values, index, axis=1, mode="promise_in_bounds")


def coupled(direction):
    return {0: 1 + direction, 1 + direction: 4, 4: 1 + direction}


def flux_of(left, right, direction):
    couples = coupled(direction)
    out = []
    for v in range(NVAR):
        flux = PLUS[direction] * left[v] + MINUS[direction] * right[v]
        if v in couples:
            w = couples[v]
            flux = flux + 0.5 * (left[w] + right[w])
        out.append(flux)
    return out


class Level:
    def __init__(self, work, count, rows, depth, ghosts, matrix=None):
        self.jumps, self.slopes, self.low, self.slope, self.left, self.right = work[:6]
        self.matrix = matrix
        if matrix is None:
            self.zlow, self.zslope, self.zleft, self.zright = work[6:]
        else:
            self.parts, self.steps, self.rises = work[6:]
        self.count, self.rows, self.depth, self.ghosts = count, rows, depth, ghosts
        lane = lanes_of()
        self.first = lane < depth
        self.last = lane >= LANES - depth
        place = lane % depth
        self.behind = jnp.where(place == 0, lane + depth - 1, lane - 1)
        self.ahead = jnp.where(place == depth - 1, lane - depth + 1, lane + 1)

    @staticmethod
    def work(count, rows, matrix=False):
        f32 = jnp.float32
        wide = VMEM((NVAR, count + 2, rows, LANES), f32)
        narrow = VMEM((NVAR, count, rows, LANES), f32)
        cells = NVAR * count * rows
        along_z = [narrow] * 4
        if matrix:
            along_z = [VMEM((cells, 2 * LANES), jnp.bfloat16)] + [VMEM((cells, 2 * LANES), f32)] * 2
        jumps = VMEM((NVAR, count, rows + 2 * SUB, LANES), f32)
        return [jumps, VMEM((NVAR, count, rows + SUB, LANES), f32)] + [wide] * 4 + along_z

    def place(self, v, t, row):
        return (v * self.count + t) * self.rows + row

    def split(self, at, values):
        high, rest = parts_of(values)
        self.parts[at : at + 2 * SUB, 0:LANES] = high
        self.parts[at : at + 2 * SUB, LANES : 2 * LANES] = rest

    def differences(self, index):
        return jnp.dot(self.parts[...], self.matrix[index], preferred_element_type=jnp.float32)

    def columns(self):
        for v in range(NVAR):
            for s in range(self.rows // SUB):
                yield v, slice(SUB * s, SUB * (s + 1)), slice(PAD + SUB * s, PAD + SUB * (s + 1))

    def tiles(self):
        for v, here, padded in self.columns():
            for t in range(self.count):
                yield v, t, here, padded

    def prepare(self, q):
        count, depth = self.count, self.depth
        full, flat = self.ghosts == "full", self.ghosts == "flat"
        inner = range(1, count + 1)
        for v, here, padded in self.columns():
            cells = {t: q[v, t, padded] for t in range(count + 2)}
            moved = {t: roll(cells[t], depth) for t in inner}
            moved[0] = roll(cells[0], depth) if full else cells[0] if flat else moved[1]
            for t in inner:
                self.low[v, t, here] = cells[t] - jnp.where(self.first, moved[t - 1], moved[t])
            if full:
                top = roll(cells[count + 1], depth)
                self.low[v, 0, here] = cells[0] - moved[0]
                self.low[v, count + 1, here] = cells[count + 1] - jnp.where(self.first, moved[count], top)
            if flat:
                self.low[v, count + 1, here] = cells[count + 1] - moved[count]
        if self.matrix is None:
            for v, t, here, padded in self.tiles():
                cell = q[v, t + 1, padded]
                self.zlow[v, t, here] = cell - take(cell, self.behind)
        else:
            for v in range(NVAR):
                for t in range(count):
                    for row in range(0, self.rows, 2 * SUB):
                        self.split(self.place(v, t, row), q[v, t + 1, PAD + row : PAD + row + 2 * SUB])
            self.steps[...] = self.differences(0)
        for v in range(NVAR):
            for t in range(count):
                for at in range(0, self.rows + 3, SUB):
                    row = PAD - 2 + at
                    self.jumps[v, t, at : at + SUB] = (
                        q[v, t + 1, row + 1 : row + 1 + SUB] - q[v, t + 1, row : row + SUB]
                    )
        for v in range(NVAR):
            for t in range(count):
                for at in range(0, self.rows + 2, SUB):
                    low, high = self.jumps[v, t, at : at + SUB], self.jumps[v, t, at + 1 : at + 1 + SUB]
                    self.slopes[v, t, at : at + SUB] = 0.5 * minmod(low, high)
        for v, here, padded in self.columns():
            low = {t: self.low[v, t, here] for t in inner}
            moved = {t: roll(low[t], -depth) for t in inner}
            if full or flat:
                low[count + 1] = self.low[v, count + 1, here]
                moved[count + 1] = roll(low[count + 1], -depth)
            else:
                moved[count + 1] = moved[count]
            for t in inner:
                high = jnp.where(self.last, moved[t + 1], moved[t])
                self.slope[v, t, here] = 0.5 * minmod(low[t], high)
            if full:
                low[0] = self.low[v, 0, here]
                high = jnp.where(self.last, moved[1], roll(low[0], -depth))
                self.slope[v, 0, here] = 0.5 * minmod(low[0], high)
                self.slope[v, count + 1, here] = 0.5 * minmod(low[count + 1], moved[count + 1])
        if self.matrix is None:
            for v, t, here, padded in self.tiles():
                low = self.zlow[v, t, here]
                self.zslope[v, t, here] = 0.5 * minmod(low, take(low, self.ahead))
        else:
            for at in range(0, NVAR * count * self.rows, 2 * SUB):
                both = slice(at, at + 2 * SUB)
                self.split(at, minmod(self.steps[both, 0:LANES], self.steps[both, LANES : 2 * LANES]))
            self.rises[...] = self.differences(1)

    def finish(self, q, store):
        count, depth = self.count, self.depth
        full, flat = self.ghosts == "full", self.ghosts == "flat"
        inner = range(1, count + 1)
        for v, t, here, padded in self.tiles() if self.matrix is None else ():
            slope = self.zslope[v, t, here]
            rise = slope - take(slope, self.behind)
            low = self.zlow[v, t, here]
            self.zleft[v, t, here] = low + rise
            self.zright[v, t, here] = low - rise
        for v, here, padded in self.columns():
            slope = {t: self.slope[v, t, here] for t in inner}
            moved = {t: roll(slope[t], depth) for t in inner}
            if full:
                moved[0] = roll(self.slope[v, 0, here], depth)
            else:
                moved[0] = jnp.zeros((SUB, LANES), jnp.float32) if flat else moved[1]
            for t in inner:
                rise = slope[t] - jnp.where(self.first, moved[t - 1], moved[t])
                low = self.low[v, t, here]
                self.left[v, t, here] = low + rise
                self.right[v, t, here] = low - rise
            if full:
                rise = self.slope[v, count + 1, here] - moved[count]
                self.right[v, count + 1, here] = self.low[v, count + 1, here] - rise
            if flat:
                self.right[v, count + 1, here] = self.low[v, count + 1, here] + moved[count]
        for v, t, here, padded in self.tiles() if self.matrix is None else ():
            self.zright[v, t, here] = take(self.zright[v, t, here], self.ahead)
        for v, here, padded in self.columns():
            moved = {t: roll(self.right[v, t, here], -depth) for t in inner}
            if full or flat:
                moved[count + 1] = roll(self.right[v, count + 1, here], -depth)
            else:
                moved[count + 1] = moved[count]
            for t in inner:
                self.right[v, t, here] = jnp.where(self.last, moved[t + 1], moved[t])
        for s in range(self.rows // SUB):
            for t in range(count):
                self.gather(q, s, t, store)

    def gather(self, q, s, t, store):
        here = slice(SUB * s, SUB * (s + 1))
        row = PAD + SUB * s
        cell = [q[v, t + 1, row : row + SUB] for v in range(NVAR)]
        lefts, rights = [None] * NVAR, [None] * NVAR

        def add(acc, v, term):
            acc[v] = term if acc[v] is None else acc[v] + term

        for direction in range(3):
            couples = coupled(direction)
            for v in range(NVAR):
                if direction == 0:
                    slope = self.slopes[v, t, SUB * s + 1 : SUB * s + 1 + SUB]
                    rise = slope - self.slopes[v, t, SUB * s : SUB * s + SUB]
                    fall = self.slopes[v, t, SUB * s + 2 : SUB * s + 2 + SUB] - slope
                    left = self.jumps[v, t, SUB * s + 1 : SUB * s + 1 + SUB] + rise
                    right = self.jumps[v, t, SUB * s + 2 : SUB * s + 2 + SUB] - fall
                elif direction == 1:
                    left, right = self.left[v, t + 1, here], self.right[v, t + 1, here]
                elif self.matrix is None:
                    left, right = self.zleft[v, t, here], self.zright[v, t, here]
                else:
                    at = self.place(v, t, SUB * s)
                    at = slice(at, at + SUB)
                    left = self.steps[at, 0:LANES] + self.rises[at, 0:LANES]
                    right = self.steps[at, LANES : 2 * LANES] - self.rises[at, LANES : 2 * LANES]
                add(lefts, v, 2.0 * PLUS[direction] * left)
                add(rights, v, right)
                targets = [w for w in couples if couples[w] == v]
                if targets:
                    shared = left + right
                    for w in targets:
                        add(lefts, w, shared)
        for v in range(NVAR):
            store(v, t, s, cell[v] - (0.5 * courant) * (lefts[v] - rights[v]))


def z_matrix(depth):
    lane = np.arange(LANES)
    base = lane - lane % depth
    below, above = base + (lane - 1) % depth, base + (lane + 1) % depth
    one = np.eye(LANES, dtype=np.float32)
    half = np.concatenate([one - one[:, below], one[:, above] - one], axis=1)
    whole = np.concatenate([half, half])
    return jnp.asarray(np.stack([whole, 0.5 * whole]), jnp.bfloat16)


def mean_matrix(depth, count):
    lane = np.arange(LANES)
    place = (lane // depth // 2) * (depth // 2) + lane % depth // 2
    out = np.zeros((count, 2, LANES, LANES), np.float32)
    for t in range(count):
        out[t, :, lane, LANES // 4 * t + place] = 0.125
    return jnp.asarray(out.reshape(-1, LANES), jnp.bfloat16)


def parts_of(values):
    high = values.astype(jnp.bfloat16)
    return high, (values - high.astype(jnp.float32)).astype(jnp.bfloat16)


class Plan:
    def __init__(self, coarse, fine, size):
        self.rows = coarse[1]
        self.depth = 8
        self.count = coarse[2] // LANES
        self.fine_rows = fine[2]
        self.fine_depth = 2 * self.depth
        self.fine_count = fine[3] // LANES
        self.patch = self.fine_rows // 2
        self.start = (self.rows - self.patch) // 2
        self.end = self.start + self.patch
        self.size = size
        self.paired = size & (size - 1) == 0
        self.exchanges = list(range(size // 2, size)) + list(range(1, size // 2))
        near = {1, size - 1}
        self.near = [k for k in self.exchanges if any((self.target(i, k) - i) % size in near for i in range(size))]
        self.line_rows = 24
        self.source_at = 20
        self.ring_rows = 48
        self.sent_rows = 72
        self.edge_rows = 24
        self.average_rows = NVAR * self.patch
        self.side_at = self.average_rows
        self.face_at = self.side_at + self.patch
        self.owner_at = self.face_at + 10
        self.payload_rows = self.owner_at + 6


    def target(self, i, k):
        return i ^ k if self.paired else (i + k) % self.size


def split(plan, c_ref, q):
    for v in range(NVAR):
        for t in range(plan.count):
            q[v, t + 1, PAD : PAD + plan.rows] = c_ref[v, :, LANES * t : LANES * (t + 1)]


def window_row(tiles, lane):
    low, high = (roll(tile, LANES // 2) for tile in tiles)
    return jnp.where(lane < LANES // 2, low, high)


def coarse_kernel(
    plan, site_hbm, c_hbm, f_hbm, matrix_hbm, mid_ref, rows_ref, ids_ref, held_ref, c_ref, *refs
):
    near_refs = refs[: len(plan.near)]
    q, fresh, site_ref, matrix_ref, sems = refs[len(plan.near) : len(plan.near) + 5]
    work = refs[len(plan.near) + 5 :]
    me = lax.axis_index("gy")
    loads = [
        pltpu.make_async_copy(source, target, sems.at[index])
        for index, (source, target) in enumerate(
            ((c_hbm, c_ref), (matrix_hbm, matrix_ref), (f_hbm, held_ref), (site_hbm, site_ref))
        )
    ]
    for load in loads:
        load.start()
    loads[0].wait()
    split(plan, c_ref, q)
    for v in range(NVAR):
        for t in range(plan.count):
            for edge in (0, PAD + plan.rows):
                q[v, t + 1, edge : edge + PAD] = jnp.zeros((PAD, LANES), jnp.float32)
        for t in (0, plan.count + 1):
            q[v, t, PAD : PAD + plan.rows] = jnp.zeros((plan.rows, LANES), jnp.float32)
    level = Level(work, plan.count, plan.rows, plan.depth, "none", matrix_ref)
    loads[1].wait()
    level.prepare(q)

    def store(v, t, s, tile):
        row = PAD + SUB * s
        fresh[v, t, SUB * s : SUB * (s + 1)] = 0.5 * (q[v, t + 1, row : row + SUB] + tile)

    level.finish(q, store)
    lane, single = lanes_of(), lanes_of(1)
    sent = (mid_ref, *near_refs)
    blank = jnp.zeros((SUB, LANES), jnp.float32)
    mine = blank + me.astype(jnp.float32)
    for ref in sent:
        ref[16:24] = mine
    for level_id in range(2):
        for side, x in enumerate((plan.start - 1, plan.end)):
            for v in range(NVAR):
                if level_id == 0:
                    tiles = [q[v, t + 1, PAD + x : PAD + x + 1] for t in range(2)]
                else:
                    tiles = [fresh[v, t, x : x + 1] for t in range(2)]
                line = window_row(tiles, single)
                at = 10 * level_id + 5 * side + v
                for ref in sent:
                    ref[at : at + 1] = line
    depth = plan.depth
    low_lane = (plan.start - 1) * depth
    high_lane = plan.end * depth - LANES
    packed = [None] * 3
    for level_id in range(2):
        for side, (t, at) in enumerate(((0, low_lane), (1, high_lane))):
            for v in range(NVAR):
                for half in range(plan.patch // SUB):
                    x = plan.start + SUB * half
                    if level_id == 0:
                        tile = q[v, t + 1, PAD + x : PAD + x + SUB]
                    else:
                        tile = fresh[v, t, x : x + SUB]
                    piece = ((level_id * 2 + side) * NVAR + v) * 2 + half
                    slot = piece % 16
                    moved = roll(tile, slot * depth - at)
                    where, old = piece // 16, packed[piece // 16]
                    packed[where] = moved if old is None else jnp.where(lane // depth == slot, moved, old)
    for index, tile in enumerate(packed):
        for ref in sent:
            ref[plan.line_rows + SUB * index : plan.line_rows + SUB * (index + 1)] = tile
    wide = 2 * depth
    edges = []
    for t, at in ((plan.count - 1, LANES - wide), (0, 0)):
        packed = [None] * 3
        for v in range(NVAR):
            for s in range(plan.rows // SUB):
                piece = v * (plan.rows // SUB) + s
                slot = piece % 8
                moved = roll(q[v, t + 1, PAD + SUB * s : PAD + SUB * (s + 1)], slot * wide - at)
                where, old = piece // 8, packed[piece // 8]
                packed[where] = moved if old is None else jnp.where(lane // wide == slot, moved, old)
        edges.append(packed)
    for k, ref in zip(plan.near, near_refs):
        upward = plan.target(me, k) == (me + 1) % plan.size
        for index in range(3):
            ref[plan.ring_rows + SUB * index : plan.ring_rows + SUB * (index + 1)] = jnp.where(
                upward, edges[0][index], edges[1][index]
            )
    for base, x in ((0, plan.rows - 2), (plan.edge_rows, 0)):
        rows_ref[base + 16 : base + 24] = blank
        for v in range(NVAR):
            for t in range(plan.count):
                at = base + (v * plan.count + t) * 2
                rows_ref[at : at + 2] = q[v, t + 1, PAD + x : PAD + x + 2]
    for load in loads[2:]:
        load.wait()
    zero = jnp.zeros((SUB, LANES), jnp.float32)
    for index, number in enumerate((site_ref[0, 0], me, (me + 1) % plan.size, (me + plan.size - 1) % plan.size)):
        ids_ref[SUB * index : SUB * (index + 1)] = zero + number.astype(jnp.float32)


def fine_kernel(plan, others, ids_ref, matrix_ref, mean_ref, f_ref, *refs):
    rings = refs[: others + 1]
    out_ref, pay_ref, q, q_later, lines, faces, sides, sums = refs[others + 1 : others + 9]
    work = refs[others + 9 :]
    owner = ids_ref[0:SUB]
    sources = [jnp.broadcast_to(ref[plan.source_at : plan.source_at + 1], (SUB, LANES)) == owner for ref in rings]
    count, depth, rows = plan.fine_count, plan.fine_depth, plan.fine_rows
    lane = lanes_of()
    ring = []
    for at in range(0, plan.ring_rows, SUB):
        chosen = rings[0][at : at + SUB]
        for k in range(1, others + 1):
            chosen = jnp.where(sources[k], rings[k][at : at + SUB], chosen)
        ring.append(chosen)
    for t in range(count):
        cells = (lane // depth + t * (LANES // depth)) // 2
        index = cells * plan.depth + (lane % depth) // 2
        for at in range(plan.line_rows // SUB):
            lines[t, SUB * at : SUB * (at + 1)] = take(ring[at], index)
    spread = (lane % depth) // 2

    def ghosts(q, level_id):
        for v in range(NVAR):
            for side, row in enumerate((PAD - 2, PAD + rows)):
                at = 10 * level_id + 5 * side + v
                for t in range(count):
                    q[v, t + 1, row : row + 2] = jnp.broadcast_to(lines[t, at : at + 1], (2, LANES))
        places = [
            (v, side, half) for v in range(NVAR) for side in range(2) for half in range(plan.patch // SUB)
        ]
        moved = []
        for v, side, half in places:
            piece = ((level_id * 2 + side) * NVAR + v) * 2 + half
            tile = ring[plan.line_rows // SUB + piece // 16]
            moved.append(roll(tile, -(piece % 16) * plan.depth))
        moved = [take(tile, spread) for tile in moved]
        for (v, side, half), column in zip(places, moved):
            row = PAD + 2 * SUB * half
            q[v, (count + 1) * side, pl.ds(row, SUB, stride=2)] = column
            q[v, (count + 1) * side, pl.ds(row + 1, SUB, stride=2)] = column

    for v in range(NVAR):
        for t in range(count):
            q[v, t + 1, PAD : PAD + rows] = f_ref[0, v, :, LANES * t : LANES * (t + 1)]
    level = Level(work, count, rows, depth, "flat", matrix_ref)
    slopes = level.slopes
    second = (lane >= depth) & (lane < 2 * depth)
    ghosts(q, 0)
    ghosts(q_later, 1)

    def put_sums(rows_of, t, values):
        for part, piece in enumerate(parts_of(values)):
            at = (2 * t + part) * LANES
            sums[rows_of, at : at + LANES] = piece

    def pack_registers():
        pair = ((lane // plan.depth) % 2) * depth + (lane % plan.depth) * 2
        halves = plan.patch // SUB
        beside = []
        for v in range(NVAR):
            for half in range(halves):
                row = 2 * SUB * half
                beside.append(sides[v, pl.ds(row, SUB, stride=2)] + sides[v, pl.ds(row + 1, SUB, stride=2)])
        beside = [tile + roll(tile, -1) for tile in beside]
        beside = [take(tile, pair) for tile in beside]
        for half in range(halves):
            out = beside[half]
            for v in range(1, NVAR):
                out = jnp.where(lane // depth == v, beside[v * halves + half], out)
            at = plan.side_at + SUB * half
            pay_ref[at : at + SUB] = 0.125 * out
        for t in range(count):
            put_sums(slice(plan.average_rows, plan.average_rows + 2 * SUB), t, faces[t])

    for step, (now, later) in enumerate(((q, q_later), (q_later, q))):

        def add(ref, index, value, step=step):
            ref[index] = value if step == 0 else ref[index] + value

        level.prepare(now)
        for side in range(2):
            for t in range(count):
                edge = PAD if side == 0 else PAD + rows
                left = [now[v, t + 1, edge - 1 : edge] for v in range(NVAR)]
                right = [now[v, t + 1, edge : edge + 1] for v in range(NVAR)]
                for v in range(NVAR):
                    if side == 0:
                        right[v] = right[v] - slopes[v, t, 1:2]
                    else:
                        left[v] = left[v] + slopes[v, t, rows : rows + 1]
                flux = flux_of(left, right, 0)
                for v in range(NVAR):
                    add(faces, (t, slice(5 * side + v, 5 * side + v + 1)), flux[v])
        for s in range(rows // SUB):
            here = slice(SUB * s, SUB * (s + 1))
            padded = slice(PAD + SUB * s, PAD + SUB * (s + 1))
            left, right = [], []
            for v in range(NVAR):
                inner = roll(now[v, count, padded] + level.slope[v, count, here], 2 * depth)
                left.append(jnp.where(second, inner, now[v, 0, padded]))
                right.append(jnp.where(second, now[v, count + 1, padded], now[v, 1, padded] - level.slope[v, 1, here]))
            flux = flux_of(left, right, 1)
            for v in range(NVAR):
                add(sides, (v, here), flux[v])

        def store(v, t, s, tile, step=step, later=later):
            later[v, t + 1, PAD + SUB * s : PAD + SUB * (s + 1)] = tile
            if step == 1:
                out_ref[0, v, SUB * s : SUB * (s + 1), LANES * t : LANES * (t + 1)] = tile

        if step == 1:
            pack_registers()
        level.finish(now, store)

    for v in range(NVAR):
        rows_of = slice(v * plan.patch, (v + 1) * plan.patch)
        for t in range(count):
            pairs = q[v, t + 1, pl.ds(PAD, plan.patch, stride=2)] + q[v, t + 1, pl.ds(PAD + 1, plan.patch, stride=2)]
            put_sums(rows_of, t, pairs)
    means = jnp.dot(sums[...], mean_ref[...], preferred_element_type=jnp.float32)
    pay_ref[0 : plan.average_rows] = means[0 : plan.average_rows]
    pay_ref[plan.payload_rows - SUB : plan.payload_rows] = owner
    pay_ref[plan.face_at : plan.face_at + 2 * NVAR] = means[plan.average_rows : plan.average_rows + 2 * NVAR]


def outer_kernel(plan, live_ref, ids_ref, c_ref, held_ref, before_ref, after_ref, *refs):
    near_refs = refs[: len(plan.near)]
    out_ref, fine_ref, q, sem = refs[len(plan.near) : len(plan.near) + 4]
    work = refs[len(plan.near) + 4 :]
    put = pltpu.make_async_copy(held_ref, fine_ref, sem)
    put.start()
    count, depth, rows = plan.count, plan.depth, plan.rows
    lane, single = lanes_of(), lanes_of(1)
    split(plan, c_ref, q)
    wide = 2 * depth
    blank = jnp.zeros((PAD, LANES), jnp.float32)
    for v in range(NVAR):
        for t in range(count):
            at = (v * count + t) * 2
            q[v, t + 1, 0:PAD] = blank
            q[v, t + 1, PAD + rows : 2 * PAD + rows] = blank
            q[v, t + 1, PAD - 2 : PAD] = before_ref[at : at + 2]
            q[v, t + 1, PAD + rows : PAD + rows + 2] = after_ref[plan.edge_rows + at : plan.edge_rows + at + 2]
    columns = []
    for side in range(2):
        wanted = ids_ref[SUB * (3 - side) : SUB * (4 - side)]
        chosen = [blank] * 3
        for ref in near_refs:
            found = jnp.broadcast_to(ref[plan.source_at : plan.source_at + 1], (SUB, LANES)) == wanted
            for index in range(3):
                at = plan.ring_rows + SUB * index
                chosen[index] = jnp.where(found, ref[at : at + SUB], chosen[index])
        columns.append(chosen)
    for v in range(NVAR):
        for s in range(rows // SUB):
            piece = v * (rows // SUB) + s
            slot = piece % 8
            row = PAD + SUB * s
            q[v, 0, row : row + SUB] = roll(columns[0][piece // 8], LANES - wide - slot * wide)
            q[v, count + 1, row : row + SUB] = roll(columns[1][piece // 8], -slot * wide)
    weight = courant * live_ref[0].astype(jnp.float32)
    level = Level(work, count, rows, depth, "full")
    slopes = level.slopes
    level.prepare(q)

    def store(v, t, s, tile):
        out_ref[v, SUB * s : SUB * (s + 1), LANES * t : LANES * (t + 1)] = tile

    level.finish(q, store)
    half = LANES // 2
    low_lane = (plan.start - 1) * depth
    high_lane = plan.end * depth - LANES
    at_low = (lane >= low_lane) & (lane < low_lane + depth)
    at_high = (lane >= high_lane) & (lane < high_lane + depth)
    for x in range(plan.start, plan.end, SUB):
        here, padded = slice(x, x + SUB), slice(PAD + x, PAD + x + SUB)
        cells = [[q[v, t + 1, padded] for v in range(NVAR)] for t in range(2)]
        slope = [[level.slope[v, t + 1, here] for v in range(NVAR)] for t in range(2)]
        left = [[c + d for c, d in zip(cells[t], slope[t])] for t in range(2)]
        right = [[c - d for c, d in zip(cells[t], slope[t])] for t in range(2)]
        last, first = level.last, level.first
        ahead = [
            jnp.where(last, roll(b, -depth), roll(a, -depth)) for a, b in zip(right[0], right[1])
        ]
        behind = [
            jnp.where(first, roll(a, depth), roll(b, depth)) for a, b in zip(left[0], left[1])
        ]
        low = flux_of(left[0], ahead, 1)
        high = flux_of(behind, right[1], 1)
        for v in range(NVAR):
            out_ref[v, here, 0:LANES] = out_ref[v, here, 0:LANES] + jnp.where(at_low, weight * low[v], 0.0)
            out_ref[v, here, LANES : 2 * LANES] = out_ref[v, here, LANES : 2 * LANES] - jnp.where(
                at_high, weight * high[v], 0.0
            )
    for side, x in enumerate((plan.start - 1, plan.end)):
        face = x if side == 0 else x - 1
        for t in range(2):
            left = [q[v, t + 1, PAD + face : PAD + face + 1] + slopes[v, t, face + 1 : face + 2] for v in range(NVAR)]
            right = [
                q[v, t + 1, PAD + face + 1 : PAD + face + 2] - slopes[v, t, face + 2 : face + 3]
                for v in range(NVAR)
            ]
            flux = flux_of(left, right, 0)
            inner = single >= half if t == 0 else single < half
            signed = weight if side == 0 else -weight
            for v in range(NVAR):
                at = (v, slice(x, x + 1), slice(LANES * t, LANES * (t + 1)))
                out_ref[at] = out_ref[at] + jnp.where(inner, signed * flux[v], 0.0)
    put.wait()


def patch_kernel(plan, others, live_ref, ids_ref, c_ref, *refs):
    payloads = refs[: others + 1]
    out_ref, pay = refs[others + 1 :]
    depth = plan.depth
    lane, single = lanes_of(), lanes_of(1)
    mine = ids_ref[SUB : 2 * SUB]
    owners = [
        jnp.broadcast_to(ref[plan.owner_at : plan.owner_at + 1], (SUB, LANES)) == mine for ref in payloads
    ]
    for at in range(0, plan.payload_rows, SUB):
        chosen = payloads[0][at : at + SUB]
        for k in range(1, others + 1):
            chosen = jnp.where(owners[k], payloads[k][at : at + SUB], chosen)
        pay[at : at + SUB] = chosen
    live = jnp.zeros((SUB, LANES), jnp.float32) + live_ref[0].astype(jnp.float32)
    weight = courant * live
    present = live > 0
    half = LANES // 2
    low_lane = (plan.start - 1) * depth
    high_lane = plan.end * depth - LANES
    at_low = (lane >= low_lane) & (lane < low_lane + depth)
    at_high = (lane >= high_lane) & (lane < high_lane + depth)
    under = (present & (lane >= half), present & (lane < half))
    for v in range(NVAR):
        for x in range(0, plan.rows, SUB):
            here = slice(x, x + SUB)
            tiles = [c_ref[v, here, LANES * t : LANES * (t + 1)] for t in range(plan.count)]
            if plan.start <= x < plan.end:
                base = plan.side_at + x - plan.start
                side = pay[base : base + SUB]
                low = roll(side, low_lane - v * 2 * depth)
                high = roll(side, high_lane - v * 2 * depth - depth)
                tiles[0] = tiles[0] - jnp.where(at_low, weight * low, 0.0)
                tiles[1] = tiles[1] + jnp.where(at_high, weight * high, 0.0)
                base = v * plan.patch + x - plan.start
                average = roll(pay[base : base + SUB], half)
                for t in range(2):
                    tiles[t] = jnp.where(under[t], average, tiles[t])
            for t in range(plan.count):
                out_ref[v, here, LANES * t : LANES * (t + 1)] = tiles[t]
        for side, x in enumerate((plan.start - 1, plan.end)):
            at = plan.face_at + 5 * side + v
            register = roll(pay[at : at + 1], half)
            signed = -weight[0:1] if side == 0 else weight[0:1]
            for t in range(2):
                inner = single >= half if t == 0 else single < half
                at = (v, slice(x, x + 1), slice(LANES * t, LANES * (t + 1)))
                out_ref[at] = c_ref[at] + jnp.where(inner, signed * register, 0.0)


def call(body, out_shape, scratch, flops, moved, spaces, out_spaces=None):
    if out_spaces is None:
        out_spaces = jax.tree.map(lambda _: VMEM, out_shape)
    return pl.pallas_call(
        body,
        out_shape=out_shape,
        in_specs=[pl.BlockSpec(memory_space=space) for space in spaces],
        out_specs=jax.tree.map(lambda space: pl.BlockSpec(memory_space=space), out_spaces),
        scratch_shapes=scratch,
        cost_estimate=pl.CostEstimate(flops=flops, bytes_accessed=moved, transcendentals=0),
        compiler_params=pltpu.CompilerParams(vmem_limit_bytes=16 << 20),
    )


def step(coarse_state, fine_state, slot_site, box_live):
    size = lax.axis_size("gy")
    plan = Plan(coarse_state.shape, fine_state.shape, size)
    f32 = jnp.float32
    shape = jax.ShapeDtypeStruct
    smem = pltpu.SMEM
    cells = VMEM((NVAR, plan.count + 2, plan.rows + 2 * PAD, LANES), f32)
    copying = pltpu.SemaphoreType.DMA
    sent = shape((plan.sent_rows, LANES), f32)
    edge = shape((2 * plan.edge_rows, LANES), f32)
    held_shape = shape(fine_state.shape, f32)
    coarse_shape = shape(coarse_state.shape, f32)
    near = plan.near
    matrix = z_matrix(plan.depth)
    mid, edges, ids, held, coarse, *edged = call(
        partial(coarse_kernel, plan),
        (shape((plan.ring_rows, LANES), f32), edge, shape((4 * SUB, LANES), f32), held_shape, coarse_shape)
        + (sent,) * len(near),
        [cells, VMEM((NVAR, plan.count, plan.rows, LANES), f32), smem((1, 2), jnp.int32)]
        + [VMEM(matrix.shape, matrix.dtype), copying((4,))]
        + Level.work(plan.count, plan.rows, True),
        4_000_000,
        400_000,
        [pltpu.HBM] * 4,
    )(*[pltpu.with_memory_space_constraint(x, pltpu.HBM) for x in (slot_site, coarse_state, fine_state, matrix)])
    buffers = dict(zip(near, edged))
    pairs = {k: [(i, plan.target(i, k)) for i in range(size)] for k in plan.exchanges}
    rings = {k: lax.ppermute(buffers.get(k, mid), "gy", pairs[k]) for k in plan.exchanges}
    length = lax.axis_size("gx")
    rise = [(i, (i + 1) % length) for i in range(length)]
    fall = [(j, i) for i, j in rise]
    before = lax.ppermute(edges, "gx", rise)
    after = lax.ppermute(edges, "gx", fall)
    fine_cells = VMEM((NVAR, plan.fine_count + 2, plan.fine_rows + 2 * PAD, LANES), f32)
    second, payload = call(
        partial(fine_kernel, plan, size - 1),
        (held_shape, shape((plan.payload_rows, LANES), f32)),
        [
            fine_cells,
            fine_cells,
            VMEM((plan.fine_count, plan.line_rows, LANES), f32),
            VMEM((plan.fine_count, 2 * SUB, LANES), f32),
            VMEM((NVAR, plan.fine_rows, LANES), f32),
            VMEM((plan.average_rows + 2 * SUB, 2 * plan.fine_count * LANES), jnp.bfloat16),
        ]
        + Level.work(plan.fine_count, plan.fine_rows, True),
        16_000_000,
        1_000_000,
        [VMEM, VMEM, VMEM, VMEM] + [VMEM] * size,
    )(ids, z_matrix(plan.fine_depth), mean_matrix(plan.fine_depth, plan.fine_count), held, mid, *[rings[k] for k in plan.exchanges])
    payloads = [payload] + [lax.ppermute(payload, "gy", pairs[k]) for k in plan.exchanges]
    coarse_new, fine_out = call(
        partial(outer_kernel, plan),
        (coarse_shape, held_shape),
        [cells, copying] + Level.work(plan.count, plan.rows),
        4_000_000,
        400_000,
        [smem] + [VMEM] * (5 + len(near)),
        (VMEM, pltpu.HBM),
    )(box_live, ids, coarse, second, before, after, *[rings[k] for k in near])
    coarse_out = call(
        partial(patch_kernel, plan, size - 1),
        coarse_shape,
        [VMEM((plan.payload_rows, LANES), f32)],
        400_000,
        400_000,
        [smem, VMEM, VMEM] + [VMEM] * size,
    )(box_live, ids, coarse_new, *payloads)
    return (coarse_out, fine_out)


def solution(mesh):
    return jax.shard_map(
        step,
        mesh=mesh,
        in_specs=(
            P(None, "gx", "gy"),
            P(("gx", "gy"), None, None, None),
            P(("gx", "gy"), None),
            P(("gx", "gy")),
        ),
        out_specs=(P(None, "gx", "gy"), P(("gx", "gy"), None, None, None)),
        check_vma=False,
    )
```

```python
from functools import partial

import jax
import jax.numpy as jnp
import numpy as np
from jax import lax
from jax.experimental import pallas as pl
from jax.experimental.pallas import tpu as pltpu
from jax.sharding import PartitionSpec as P


LANES = 128
SUB = 8
PAD = 8

courant = 0.2
drift = (0.5, 0.3, 0.2)
signal = (1.5, 1.3, 1.2)
PLUS = tuple(0.5 * (a + s) for a, s in zip(drift, signal))
MINUS = tuple(0.5 * (a - s) for a, s in zip(drift, signal))
assert all(abs(m + 0.5) < 1e-12 for m in MINUS)

NVAR = 5
VMEM = pltpu.VMEM


def minmod(first, second):
    return jnp.maximum(jnp.minimum(first, second), jnp.minimum(jnp.maximum(first, second), 0.0))


def lanes_of(rows=SUB):
    return lax.broadcasted_iota(jnp.int32, (rows, LANES), 1)


def roll(values, step):
    step = step % LANES
    return values if step == 0 else pltpu.roll(values, step, 1)


def take(values, index):
    return jnp.take_along_axis(values, index, axis=1, mode="promise_in_bounds")


def coupled(direction):
    return {0: 1 + direction, 1 + direction: 4, 4: 1 + direction}


def flux_of(left, right, direction):
    couples = coupled(direction)
    out = []
    for v in range(NVAR):
        flux = PLUS[direction] * left[v] + MINUS[direction] * right[v]
        if v in couples:
            w = couples[v]
            flux = flux + 0.5 * (left[w] + right[w])
        out.append(flux)
    return out


class Level:
    def __init__(self, work, count, rows, depth, ghosts, matrix=None):
        self.jumps, self.slopes, self.low, self.slope, self.left, self.right = work[:6]
        self.matrix = matrix
        if matrix is None:
            self.zlow, self.zslope, self.zleft, self.zright = work[6:]
        else:
            self.parts, self.steps, self.rises = work[6:]
        self.count, self.rows, self.depth, self.ghosts = count, rows, depth, ghosts
        lane = lanes_of()
        self.first = lane < depth
        self.last = lane >= LANES - depth
        place = lane % depth
        self.behind = jnp.where(place == 0, lane + depth - 1, lane - 1)
        self.ahead = jnp.where(place == depth - 1, lane - depth + 1, lane + 1)

    @staticmethod
    def work(count, rows, matrix=False):
        f32 = jnp.float32
        wide = VMEM((NVAR, count + 2, rows, LANES), f32)
        narrow = VMEM((NVAR, count, rows, LANES), f32)
        cells = NVAR * count * rows
        along_z = [narrow] * 4
        if matrix:
            along_z = [VMEM((cells, 2 * LANES), jnp.bfloat16)] + [VMEM((cells, 2 * LANES), f32)] * 2
        jumps = VMEM((NVAR, count, rows + 2 * SUB, LANES), f32)
        return [jumps, VMEM((NVAR, count, rows + SUB, LANES), f32)] + [wide] * 4 + along_z

    def place(self, v, t, row):
        return (v * self.count + t) * self.rows + row

    def split(self, at, values):
        high, rest = parts_of(values)
        self.parts[at : at + 2 * SUB, 0:LANES] = high
        self.parts[at : at + 2 * SUB, LANES : 2 * LANES] = rest

    def differences(self, index):
        return jnp.dot(self.parts[...], self.matrix[index], preferred_element_type=jnp.float32)

    def columns(self):
        for v in range(NVAR):
            for s in range(self.rows // SUB):
                yield v, slice(SUB * s, SUB * (s + 1)), slice(PAD + SUB * s, PAD + SUB * (s + 1))

    def tiles(self):
        for v, here, padded in self.columns():
            for t in range(self.count):
                yield v, t, here, padded

    def prepare(self, q):
        count, depth = self.count, self.depth
        full, flat = self.ghosts == "full", self.ghosts == "flat"
        inner = range(1, count + 1)
        for v, here, padded in self.columns():
            cells = {t: q[v, t, padded] for t in range(count + 2)}
            moved = {t: roll(cells[t], depth) for t in inner}
            moved[0] = roll(cells[0], depth) if full else cells[0] if flat else moved[1]
            for t in inner:
                self.low[v, t, here] = cells[t] - jnp.where(self.first, moved[t - 1], moved[t])
            if full:
                top = roll(cells[count + 1], depth)
                self.low[v, 0, here] = cells[0] - moved[0]
                self.low[v, count + 1, here] = cells[count + 1] - jnp.where(self.first, moved[count], top)
            if flat:
                self.low[v, count + 1, here] = cells[count + 1] - moved[count]
        if self.matrix is None:
            for v, t, here, padded in self.tiles():
                cell = q[v, t + 1, padded]
                self.zlow[v, t, here] = cell - take(cell, self.behind)
        else:
            for v in range(NVAR):
                for t in range(count):
                    for row in range(0, self.rows, 2 * SUB):
                        self.split(self.place(v, t, row), q[v, t + 1, PAD + row : PAD + row + 2 * SUB])
            self.steps[...] = self.differences(0)
        for v in range(NVAR):
            for t in range(count):
                for at in range(0, self.rows + 3, SUB):
                    row = PAD - 2 + at
                    self.jumps[v, t, at : at + SUB] = (
                        q[v, t + 1, row + 1 : row + 1 + SUB] - q[v, t + 1, row : row + SUB]
                    )
        for v in range(NVAR):
            for t in range(count):
                for at in range(0, self.rows + 2, SUB):
                    low, high = self.jumps[v, t, at : at + SUB], self.jumps[v, t, at + 1 : at + 1 + SUB]
                    self.slopes[v, t, at : at + SUB] = 0.5 * minmod(low, high)
        for v, here, padded in self.columns():
            low = {t: self.low[v, t, here] for t in inner}
            moved = {t: roll(low[t], -depth) for t in inner}
            if full or flat:
                low[count + 1] = self.low[v, count + 1, here]
                moved[count + 1] = roll(low[count + 1], -depth)
            else:
                moved[count + 1] = moved[count]
            for t in inner:
                high = jnp.where(self.last, moved[t + 1], moved[t])
                self.slope[v, t, here] = 0.5 * minmod(low[t], high)
            if full:
                low[0] = self.low[v, 0, here]
                high = jnp.where(self.last, moved[1], roll(low[0], -depth))
                self.slope[v, 0, here] = 0.5 * minmod(low[0], high)
                self.slope[v, count + 1, here] = 0.5 * minmod(low[count + 1], moved[count + 1])
        if self.matrix is None:
            for v, t, here, padded in self.tiles():
                low = self.zlow[v, t, here]
                self.zslope[v, t, here] = 0.5 * minmod(low, take(low, self.ahead))
        else:
            for at in range(0, NVAR * count * self.rows, 2 * SUB):
                both = slice(at, at + 2 * SUB)
                self.split(at, minmod(self.steps[both, 0:LANES], self.steps[both, LANES : 2 * LANES]))
            self.rises[...] = self.differences(1)

    def finish(self, q, store):
        count, depth = self.count, self.depth
        full, flat = self.ghosts == "full", self.ghosts == "flat"
        inner = range(1, count + 1)
        for v, t, here, padded in self.tiles() if self.matrix is None else ():
            slope = self.zslope[v, t, here]
            rise = slope - take(slope, self.behind)
            low = self.zlow[v, t, here]
            self.zleft[v, t, here] = low + rise
            self.zright[v, t, here] = low - rise
        for v, here, padded in self.columns():
            slope = {t: self.slope[v, t, here] for t in inner}
            moved = {t: roll(slope[t], depth) for t in inner}
            if full:
                moved[0] = roll(self.slope[v, 0, here], depth)
            else:
                moved[0] = jnp.zeros((SUB, LANES), jnp.float32) if flat else moved[1]
            for t in inner:
                rise = slope[t] - jnp.where(self.first, moved[t - 1], moved[t])
                low = self.low[v, t, here]
                self.left[v, t, here] = low + rise
                self.right[v, t, here] = low - rise
            if full:
                rise = self.slope[v, count + 1, here] - moved[count]
                self.right[v, count + 1, here] = self.low[v, count + 1, here] - rise
            if flat:
                self.right[v, count + 1, here] = self.low[v, count + 1, here] + moved[count]
        for v, t, here, padded in self.tiles() if self.matrix is None else ():
            self.zright[v, t, here] = take(self.zright[v, t, here], self.ahead)
        for v, here, padded in self.columns():
            moved = {t: roll(self.right[v, t, here], -depth) for t in inner}
            if full or flat:
                moved[count + 1] = roll(self.right[v, count + 1, here], -depth)
            else:
                moved[count + 1] = moved[count]
            for t in inner:
                self.right[v, t, here] = jnp.where(self.last, moved[t + 1], moved[t])
        for s in range(self.rows // SUB):
            for t in range(count):
                self.gather(q, s, t, store)

    def gather(self, q, s, t, store):
        here = slice(SUB * s, SUB * (s + 1))
        row = PAD + SUB * s
        cell = [q[v, t + 1, row : row + SUB] for v in range(NVAR)]
        lefts, rights = [None] * NVAR, [None] * NVAR

        def add(acc, v, term):
            acc[v] = term if acc[v] is None else acc[v] + term

        for direction in range(3):
            couples = coupled(direction)
            for v in range(NVAR):
                if direction == 0:
                    slope = self.slopes[v, t, SUB * s + 1 : SUB * s + 1 + SUB]
                    rise = slope - self.slopes[v, t, SUB * s : SUB * s + SUB]
                    fall = self.slopes[v, t, SUB * s + 2 : SUB * s + 2 + SUB] - slope
                    left = self.jumps[v, t, SUB * s + 1 : SUB * s + 1 + SUB] + rise
                    right = self.jumps[v, t, SUB * s + 2 : SUB * s + 2 + SUB] - fall
                elif direction == 1:
                    left, right = self.left[v, t + 1, here], self.right[v, t + 1, here]
                elif self.matrix is None:
                    left, right = self.zleft[v, t, here], self.zright[v, t, here]
                else:
                    at = self.place(v, t, SUB * s)
                    at = slice(at, at + SUB)
                    left = self.steps[at, 0:LANES] + self.rises[at, 0:LANES]
                    right = self.steps[at, LANES : 2 * LANES] - self.rises[at, LANES : 2 * LANES]
                add(lefts, v, 2.0 * PLUS[direction] * left)
                add(rights, v, right)
                targets = [w for w in couples if couples[w] == v]
                if targets:
                    shared = left + right
                    for w in targets:
                        add(lefts, w, shared)
        for v in range(NVAR):
            store(v, t, s, cell[v] - (0.5 * courant) * (lefts[v] - rights[v]))


def z_matrix(depth):
    lane = np.arange(LANES)
    base = lane - lane % depth
    below, above = base + (lane - 1) % depth, base + (lane + 1) % depth
    one = np.eye(LANES, dtype=np.float32)
    half = np.concatenate([one - one[:, below], one[:, above] - one], axis=1)
    whole = np.concatenate([half, half])
    return jnp.asarray(np.stack([whole, 0.5 * whole]), jnp.bfloat16)


def mean_matrix(depth, count):
    lane = np.arange(LANES)
    place = (lane // depth // 2) * (depth // 2) + lane % depth // 2
    out = np.zeros((count, 2, LANES, LANES), np.float32)
    for t in range(count):
        out[t, :, lane, LANES // 4 * t + place] = 0.125
    return jnp.asarray(out.reshape(-1, LANES), jnp.bfloat16)


def parts_of(values):
    high = values.astype(jnp.bfloat16)
    return high, (values - high.astype(jnp.float32)).astype(jnp.bfloat16)


class Plan:
    def __init__(self, coarse, fine, size):
        self.rows = coarse[1]
        self.depth = 8
        self.count = coarse[2] // LANES
        self.fine_rows = fine[2]
        self.fine_depth = 2 * self.depth
        self.fine_count = fine[3] // LANES
        self.patch = self.fine_rows // 2
        self.start = (self.rows - self.patch) // 2
        self.end = self.start + self.patch
        self.size = size
        self.paired = size & (size - 1) == 0
        self.exchanges = list(range(size // 2, size)) + list(range(1, size // 2))
        self.passed = size == 2 * 2
        self.direct = [k for k in self.exchanges if not (self.passed and k == size - 1)]
        near = {1, size - 1}
        self.near = [k for k in self.exchanges if any((self.target(i, k) - i) % size in near for i in range(size))]
        self.line_rows = 24
        self.source_at = 20
        self.ring_rows = 48
        self.sent_rows = 72
        self.edge_rows = 24
        self.average_rows = NVAR * self.patch
        self.side_at = self.average_rows
        self.face_at = self.side_at + self.patch
        self.owner_at = self.face_at + 10
        self.payload_rows = self.owner_at + 6


    def target(self, i, k):
        return i ^ k if self.paired else (i + k) % self.size


def split(plan, c_ref, q):
    for v in range(NVAR):
        for t in range(plan.count):
            q[v, t + 1, PAD : PAD + plan.rows] = c_ref[v, :, LANES * t : LANES * (t + 1)]


def window_row(tiles, lane):
    low, high = (roll(tile, LANES // 2) for tile in tiles)
    return jnp.where(lane < LANES // 2, low, high)


def coarse_kernel(
    plan, site_hbm, c_hbm, f_hbm, matrix_hbm, mid_ref, rows_ref, ids_ref, held_ref, c_ref, *refs
):
    near_refs = refs[: len(plan.near)]
    q, fresh, site_ref, matrix_ref, sems = refs[len(plan.near) : len(plan.near) + 5]
    work = refs[len(plan.near) + 5 :]
    me = lax.axis_index("gy")
    loads = [
        pltpu.make_async_copy(source, target, sems.at[index])
        for index, (source, target) in enumerate(
            ((c_hbm, c_ref), (matrix_hbm, matrix_ref), (f_hbm, held_ref), (site_hbm, site_ref))
        )
    ]
    for load in loads:
        load.start()
    loads[0].wait()
    split(plan, c_ref, q)
    for v in range(NVAR):
        for t in range(plan.count):
            for edge in (0, PAD + plan.rows):
                q[v, t + 1, edge : edge + PAD] = jnp.zeros((PAD, LANES), jnp.float32)
        for t in (0, plan.count + 1):
            q[v, t, PAD : PAD + plan.rows] = jnp.zeros((plan.rows, LANES), jnp.float32)
    level = Level(work, plan.count, plan.rows, plan.depth, "none", matrix_ref)
    loads[1].wait()
    level.prepare(q)

    def store(v, t, s, tile):
        row = PAD + SUB * s
        fresh[v, t, SUB * s : SUB * (s + 1)] = 0.5 * (q[v, t + 1, row : row + SUB] + tile)

    level.finish(q, store)
    lane, single = lanes_of(), lanes_of(1)
    sent = (mid_ref, *near_refs)
    blank = jnp.zeros((SUB, LANES), jnp.float32)
    mine = blank + me.astype(jnp.float32)
    for ref in sent:
        ref[16:24] = mine
    for level_id in range(2):
        for side, x in enumerate((plan.start - 1, plan.end)):
            for v in range(NVAR):
                if level_id == 0:
                    tiles = [q[v, t + 1, PAD + x : PAD + x + 1] for t in range(2)]
                else:
                    tiles = [fresh[v, t, x : x + 1] for t in range(2)]
                line = window_row(tiles, single)
                at = 10 * level_id + 5 * side + v
                for ref in sent:
                    ref[at : at + 1] = line
    depth = plan.depth
    low_lane = (plan.start - 1) * depth
    high_lane = plan.end * depth - LANES
    packed = [None] * 3
    for level_id in range(2):
        for side, (t, at) in enumerate(((0, low_lane), (1, high_lane))):
            for v in range(NVAR):
                for half in range(plan.patch // SUB):
                    x = plan.start + SUB * half
                    if level_id == 0:
                        tile = q[v, t + 1, PAD + x : PAD + x + SUB]
                    else:
                        tile = fresh[v, t, x : x + SUB]
                    piece = ((level_id * 2 + side) * NVAR + v) * 2 + half
                    slot = piece % 16
                    moved = roll(tile, slot * depth - at)
                    where, old = piece // 16, packed[piece // 16]
                    packed[where] = moved if old is None else jnp.where(lane // depth == slot, moved, old)
    for index, tile in enumerate(packed):
        for ref in sent:
            ref[plan.line_rows + SUB * index : plan.line_rows + SUB * (index + 1)] = tile
    wide = 2 * depth
    edges = []
    for t, at in ((plan.count - 1, LANES - wide), (0, 0)):
        packed = [None] * 3
        for v in range(NVAR):
            for s in range(plan.rows // SUB):
                piece = v * (plan.rows // SUB) + s
                slot = piece % 8
                moved = roll(q[v, t + 1, PAD + SUB * s : PAD + SUB * (s + 1)], slot * wide - at)
                where, old = piece // 8, packed[piece // 8]
                packed[where] = moved if old is None else jnp.where(lane // wide == slot, moved, old)
        edges.append(packed)
    for k, ref in zip(plan.near, near_refs):
        upward = plan.target(me, k) == (me + 1) % plan.size
        for index in range(3):
            ref[plan.ring_rows + SUB * index : plan.ring_rows + SUB * (index + 1)] = jnp.where(
                upward, edges[0][index], edges[1][index]
            )
    for base, x in ((0, plan.rows - 2), (plan.edge_rows, 0)):
        rows_ref[base + 16 : base + 24] = blank
        for v in range(NVAR):
            for t in range(plan.count):
                at = base + (v * plan.count + t) * 2
                rows_ref[at : at + 2] = q[v, t + 1, PAD + x : PAD + x + 2]
    for load in loads[2:]:
        load.wait()
    zero = jnp.zeros((SUB, LANES), jnp.float32)
    for index, number in enumerate((site_ref[0, 0], me, (me + 1) % plan.size, (me + plan.size - 1) % plan.size)):
        ids_ref[SUB * index : SUB * (index + 1)] = zero + number.astype(jnp.float32)


def fine_kernel(plan, others, ids_ref, matrix_ref, mean_ref, f_ref, *refs):
    rings = refs[: others + 1]
    out_ref, pay_ref, q, q_later, lines, faces, sides, sums = refs[others + 1 : others + 9]
    work = refs[others + 9 :]
    owner = ids_ref[0:SUB]
    sources = [jnp.broadcast_to(ref[plan.source_at : plan.source_at + 1], (SUB, LANES)) == owner for ref in rings]
    count, depth, rows = plan.fine_count, plan.fine_depth, plan.fine_rows
    lane = lanes_of()
    ring = []
    for at in range(0, plan.ring_rows, SUB):
        chosen = rings[0][at : at + SUB]
        for k in range(1, others + 1):
            chosen = jnp.where(sources[k], rings[k][at : at + SUB], chosen)
        ring.append(chosen)
    for t in range(count):
        cells = (lane // depth + t * (LANES // depth)) // 2
        index = cells * plan.depth + (lane % depth) // 2
        for at in range(plan.line_rows // SUB):
            lines[t, SUB * at : SUB * (at + 1)] = take(ring[at], index)
    spread = (lane % depth) // 2

    def ghosts(q, level_id):
        for v in range(NVAR):
            for side, row in enumerate((PAD - 2, PAD + rows)):
                at = 10 * level_id + 5 * side + v
                for t in range(count):
                    q[v, t + 1, row : row + 2] = jnp.broadcast_to(lines[t, at : at + 1], (2, LANES))
        places = [
            (v, side, half) for v in range(NVAR) for side in range(2) for half in range(plan.patch // SUB)
        ]
        moved = []
        for v, side, half in places:
            piece = ((level_id * 2 + side) * NVAR + v) * 2 + half
            tile = ring[plan.line_rows // SUB + piece // 16]
            moved.append(roll(tile, -(piece % 16) * plan.depth))
        moved = [take(tile, spread) for tile in moved]
        for (v, side, half), column in zip(places, moved):
            row = PAD + 2 * SUB * half
            q[v, (count + 1) * side, pl.ds(row, SUB, stride=2)] = column
            q[v, (count + 1) * side, pl.ds(row + 1, SUB, stride=2)] = column

    for v in range(NVAR):
        for t in range(count):
            q[v, t + 1, PAD : PAD + rows] = f_ref[0, v, :, LANES * t : LANES * (t + 1)]
    level = Level(work, count, rows, depth, "flat", matrix_ref)
    slopes = level.slopes
    second = (lane >= depth) & (lane < 2 * depth)
    ghosts(q, 0)
    ghosts(q_later, 1)

    def put_sums(rows_of, t, values):
        for part, piece in enumerate(parts_of(values)):
            at = (2 * t + part) * LANES
            sums[rows_of, at : at + LANES] = piece

    def pack_registers():
        pair = ((lane // plan.depth) % 2) * depth + (lane % plan.depth) * 2
        halves = plan.patch // SUB
        beside = []
        for v in range(NVAR):
            for half in range(halves):
                row = 2 * SUB * half
                beside.append(sides[v, pl.ds(row, SUB, stride=2)] + sides[v, pl.ds(row + 1, SUB, stride=2)])
        beside = [tile + roll(tile, -1) for tile in beside]
        beside = [take(tile, pair) for tile in beside]
        for half in range(halves):
            out = beside[half]
            for v in range(1, NVAR):
                out = jnp.where(lane // depth == v, beside[v * halves + half], out)
            at = plan.side_at + SUB * half
            pay_ref[at : at + SUB] = 0.125 * out
        for t in range(count):
            put_sums(slice(plan.average_rows, plan.average_rows + 2 * SUB), t, faces[t])

    for step, (now, later) in enumerate(((q, q_later), (q_later, q))):

        def add(ref, index, value, step=step):
            ref[index] = value if step == 0 else ref[index] + value

        level.prepare(now)
        for side in range(2):
            for t in range(count):
                edge = PAD if side == 0 else PAD + rows
                left = [now[v, t + 1, edge - 1 : edge] for v in range(NVAR)]
                right = [now[v, t + 1, edge : edge + 1] for v in range(NVAR)]
                for v in range(NVAR):
                    if side == 0:
                        right[v] = right[v] - slopes[v, t, 1:2]
                    else:
                        left[v] = left[v] + slopes[v, t, rows : rows + 1]
                flux = flux_of(left, right, 0)
                for v in range(NVAR):
                    add(faces, (t, slice(5 * side + v, 5 * side + v + 1)), flux[v])
        for s in range(rows // SUB):
            here = slice(SUB * s, SUB * (s + 1))
            padded = slice(PAD + SUB * s, PAD + SUB * (s + 1))
            left, right = [], []
            for v in range(NVAR):
                inner = roll(now[v, count, padded] + level.slope[v, count, here], 2 * depth)
                left.append(jnp.where(second, inner, now[v, 0, padded]))
                right.append(jnp.where(second, now[v, count + 1, padded], now[v, 1, padded] - level.slope[v, 1, here]))
            flux = flux_of(left, right, 1)
            for v in range(NVAR):
                add(sides, (v, here), flux[v])

        def store(v, t, s, tile, step=step, later=later):
            later[v, t + 1, PAD + SUB * s : PAD + SUB * (s + 1)] = tile
            if step == 1:
                out_ref[0, v, SUB * s : SUB * (s + 1), LANES * t : LANES * (t + 1)] = tile

        if step == 1:
            pack_registers()
        level.finish(now, store)

    for v in range(NVAR):
        rows_of = slice(v * plan.patch, (v + 1) * plan.patch)
        for t in range(count):
            pairs = q[v, t + 1, pl.ds(PAD, plan.patch, stride=2)] + q[v, t + 1, pl.ds(PAD + 1, plan.patch, stride=2)]
            put_sums(rows_of, t, pairs)
    means = jnp.dot(sums[...], mean_ref[...], preferred_element_type=jnp.float32)
    pay_ref[0 : plan.average_rows] = means[0 : plan.average_rows]
    pay_ref[plan.payload_rows - SUB : plan.payload_rows] = owner
    pay_ref[plan.face_at : plan.face_at + 2 * NVAR] = means[plan.average_rows : plan.average_rows + 2 * NVAR]


def outer_kernel(plan, live_ref, ids_ref, c_ref, held_ref, before_ref, after_ref, *refs):
    near_refs = refs[: len(plan.near)]
    out_ref, fine_ref, q, sem = refs[len(plan.near) : len(plan.near) + 4]
    work = refs[len(plan.near) + 4 :]
    put = pltpu.make_async_copy(held_ref, fine_ref, sem)
    put.start()
    count, depth, rows = plan.count, plan.depth, plan.rows
    lane, single = lanes_of(), lanes_of(1)
    split(plan, c_ref, q)
    wide = 2 * depth
    blank = jnp.zeros((PAD, LANES), jnp.float32)
    for v in range(NVAR):
        for t in range(count):
            at = (v * count + t) * 2
            q[v, t + 1, 0:PAD] = blank
            q[v, t + 1, PAD + rows : 2 * PAD + rows] = blank
            q[v, t + 1, PAD - 2 : PAD] = before_ref[at : at + 2]
            q[v, t + 1, PAD + rows : PAD + rows + 2] = after_ref[plan.edge_rows + at : plan.edge_rows + at + 2]
    columns = []
    for side in range(2):
        wanted = ids_ref[SUB * (3 - side) : SUB * (4 - side)]
        chosen = [blank] * 3
        for ref in near_refs:
            found = jnp.broadcast_to(ref[plan.source_at : plan.source_at + 1], (SUB, LANES)) == wanted
            for index in range(3):
                at = plan.ring_rows + SUB * index
                chosen[index] = jnp.where(found, ref[at : at + SUB], chosen[index])
        columns.append(chosen)
    for v in range(NVAR):
        for s in range(rows // SUB):
            piece = v * (rows // SUB) + s
            slot = piece % 8
            row = PAD + SUB * s
            q[v, 0, row : row + SUB] = roll(columns[0][piece // 8], LANES - wide - slot * wide)
            q[v, count + 1, row : row + SUB] = roll(columns[1][piece // 8], -slot * wide)
    weight = courant * live_ref[0].astype(jnp.float32)
    level = Level(work, count, rows, depth, "full")
    slopes = level.slopes
    level.prepare(q)

    def store(v, t, s, tile):
        out_ref[v, SUB * s : SUB * (s + 1), LANES * t : LANES * (t + 1)] = tile

    level.finish(q, store)
    half = LANES // 2
    low_lane = (plan.start - 1) * depth
    high_lane = plan.end * depth - LANES
    at_low = (lane >= low_lane) & (lane < low_lane + depth)
    at_high = (lane >= high_lane) & (lane < high_lane + depth)
    for x in range(plan.start, plan.end, SUB):
        here, padded = slice(x, x + SUB), slice(PAD + x, PAD + x + SUB)
        cells = [[q[v, t + 1, padded] for v in range(NVAR)] for t in range(2)]
        slope = [[level.slope[v, t + 1, here] for v in range(NVAR)] for t in range(2)]
        left = [[c + d for c, d in zip(cells[t], slope[t])] for t in range(2)]
        right = [[c - d for c, d in zip(cells[t], slope[t])] for t in range(2)]
        last, first = level.last, level.first
        ahead = [
            jnp.where(last, roll(b, -depth), roll(a, -depth)) for a, b in zip(right[0], right[1])
        ]
        behind = [
            jnp.where(first, roll(a, depth), roll(b, depth)) for a, b in zip(left[0], left[1])
        ]
        low = flux_of(left[0], ahead, 1)
        high = flux_of(behind, right[1], 1)
        for v in range(NVAR):
            out_ref[v, here, 0:LANES] = out_ref[v, here, 0:LANES] + jnp.where(at_low, weight * low[v], 0.0)
            out_ref[v, here, LANES : 2 * LANES] = out_ref[v, here, LANES : 2 * LANES] - jnp.where(
                at_high, weight * high[v], 0.0
            )
    for side, x in enumerate((plan.start - 1, plan.end)):
        face = x if side == 0 else x - 1
        for t in range(2):
            left = [q[v, t + 1, PAD + face : PAD + face + 1] + slopes[v, t, face + 1 : face + 2] for v in range(NVAR)]
            right = [
                q[v, t + 1, PAD + face + 1 : PAD + face + 2] - slopes[v, t, face + 2 : face + 3]
                for v in range(NVAR)
            ]
            flux = flux_of(left, right, 0)
            inner = single >= half if t == 0 else single < half
            signed = weight if side == 0 else -weight
            for v in range(NVAR):
                at = (v, slice(x, x + 1), slice(LANES * t, LANES * (t + 1)))
                out_ref[at] = out_ref[at] + jnp.where(inner, signed * flux[v], 0.0)
    put.wait()


def patch_kernel(plan, others, live_ref, ids_ref, c_ref, *refs):
    payloads = refs[: others + 1]
    out_ref, pay = refs[others + 1 :]
    depth = plan.depth
    lane, single = lanes_of(), lanes_of(1)
    mine = ids_ref[SUB : 2 * SUB]
    owners = [
        jnp.broadcast_to(ref[plan.owner_at : plan.owner_at + 1], (SUB, LANES)) == mine for ref in payloads
    ]
    for at in range(0, plan.payload_rows, SUB):
        chosen = payloads[0][at : at + SUB]
        for k in range(1, others + 1):
            chosen = jnp.where(owners[k], payloads[k][at : at + SUB], chosen)
        pay[at : at + SUB] = chosen
    live = jnp.zeros((SUB, LANES), jnp.float32) + live_ref[0].astype(jnp.float32)
    weight = courant * live
    present = live > 0
    half = LANES // 2
    low_lane = (plan.start - 1) * depth
    high_lane = plan.end * depth - LANES
    at_low = (lane >= low_lane) & (lane < low_lane + depth)
    at_high = (lane >= high_lane) & (lane < high_lane + depth)
    under = (present & (lane >= half), present & (lane < half))
    for v in range(NVAR):
        for x in range(0, plan.rows, SUB):
            here = slice(x, x + SUB)
            tiles = [c_ref[v, here, LANES * t : LANES * (t + 1)] for t in range(plan.count)]
            if plan.start <= x < plan.end:
                base = plan.side_at + x - plan.start
                side = pay[base : base + SUB]
                low = roll(side, low_lane - v * 2 * depth)
                high = roll(side, high_lane - v * 2 * depth - depth)
                tiles[0] = tiles[0] - jnp.where(at_low, weight * low, 0.0)
                tiles[1] = tiles[1] + jnp.where(at_high, weight * high, 0.0)
                base = v * plan.patch + x - plan.start
                average = roll(pay[base : base + SUB], half)
                for t in range(2):
                    tiles[t] = jnp.where(under[t], average, tiles[t])
            for t in range(plan.count):
                out_ref[v, here, LANES * t : LANES * (t + 1)] = tiles[t]
        for side, x in enumerate((plan.start - 1, plan.end)):
            at = plan.face_at + 5 * side + v
            register = roll(pay[at : at + 1], half)
            signed = -weight[0:1] if side == 0 else weight[0:1]
            for t in range(2):
                inner = single >= half if t == 0 else single < half
                at = (v, slice(x, x + 1), slice(LANES * t, LANES * (t + 1)))
                out_ref[at] = c_ref[at] + jnp.where(inner, signed * register, 0.0)


def call(body, out_shape, scratch, flops, moved, spaces, out_spaces=None):
    if out_spaces is None:
        out_spaces = jax.tree.map(lambda _: VMEM, out_shape)
    return pl.pallas_call(
        body,
        out_shape=out_shape,
        in_specs=[pl.BlockSpec(memory_space=space) for space in spaces],
        out_specs=jax.tree.map(lambda space: pl.BlockSpec(memory_space=space), out_spaces),
        scratch_shapes=scratch,
        cost_estimate=pl.CostEstimate(flops=flops, bytes_accessed=moved, transcendentals=0),
        compiler_params=pltpu.CompilerParams(vmem_limit_bytes=16 << 20),
    )


def step(coarse_state, fine_state, slot_site, box_live):
    size = lax.axis_size("gy")
    plan = Plan(coarse_state.shape, fine_state.shape, size)
    f32 = jnp.float32
    shape = jax.ShapeDtypeStruct
    smem = pltpu.SMEM
    cells = VMEM((NVAR, plan.count + 2, plan.rows + 2 * PAD, LANES), f32)
    copying = pltpu.SemaphoreType.DMA
    sent = shape((plan.sent_rows, LANES), f32)
    edge = shape((2 * plan.edge_rows, LANES), f32)
    held_shape = shape(fine_state.shape, f32)
    coarse_shape = shape(coarse_state.shape, f32)
    near = plan.near
    matrix = z_matrix(plan.depth)
    mid, edges, ids, held, coarse, *edged = call(
        partial(coarse_kernel, plan),
        (shape((plan.ring_rows, LANES), f32), edge, shape((4 * SUB, LANES), f32), held_shape, coarse_shape)
        + (sent,) * len(near),
        [cells, VMEM((NVAR, plan.count, plan.rows, LANES), f32), smem((1, 2), jnp.int32)]
        + [VMEM(matrix.shape, matrix.dtype), copying((4,))]
        + Level.work(plan.count, plan.rows, True),
        4_000_000,
        400_000,
        [pltpu.HBM] * 4,
    )(*[pltpu.with_memory_space_constraint(x, pltpu.HBM) for x in (slot_site, coarse_state, fine_state, matrix)])
    buffers = dict(zip(near, edged))
    pairs = {k: [(i, plan.target(i, k)) for i in range(size)] for k in plan.exchanges}
    rings = {k: lax.ppermute(buffers.get(k, mid), "gy", pairs[k]) for k in plan.exchanges}
    length = lax.axis_size("gx")
    rise = [(i, (i + 1) % length) for i in range(length)]
    fall = [(j, i) for i, j in rise]
    before = lax.ppermute(edges, "gx", rise)
    after = lax.ppermute(edges, "gx", fall)
    fine_cells = VMEM((NVAR, plan.fine_count + 2, plan.fine_rows + 2 * PAD, LANES), f32)
    second, payload = call(
        partial(fine_kernel, plan, size - 1),
        (held_shape, shape((plan.payload_rows, LANES), f32)),
        [
            fine_cells,
            fine_cells,
            VMEM((plan.fine_count, plan.line_rows, LANES), f32),
            VMEM((plan.fine_count, 2 * SUB, LANES), f32),
            VMEM((NVAR, plan.fine_rows, LANES), f32),
            VMEM((plan.average_rows + 2 * SUB, 2 * plan.fine_count * LANES), jnp.bfloat16),
        ]
        + Level.work(plan.fine_count, plan.fine_rows, True),
        16_000_000,
        1_000_000,
        [VMEM, VMEM, VMEM, VMEM] + [VMEM] * size,
    )(ids, z_matrix(plan.fine_depth), mean_matrix(plan.fine_depth, plan.fine_count), held, mid, *[rings[k] for k in plan.exchanges])
    payloads = [payload] + [lax.ppermute(payload, "gy", pairs[k]) for k in plan.direct]
    if plan.passed:
        payloads.append(lax.ppermute(payloads[1], "gy", pairs[1]))
    coarse_new, fine_out = call(
        partial(outer_kernel, plan),
        (coarse_shape, held_shape),
        [cells, copying] + Level.work(plan.count, plan.rows),
        4_000_000,
        400_000,
        [smem] + [VMEM] * (5 + len(near)),
        (VMEM, pltpu.HBM),
    )(box_live, ids, coarse, second, before, after, *[rings[k] for k in near])
    coarse_out = call(
        partial(patch_kernel, plan, size - 1),
        coarse_shape,
        [VMEM((plan.payload_rows, LANES), f32)],
        400_000,
        400_000,
        [smem, VMEM, VMEM] + [VMEM] * size,
    )(box_live, ids, coarse_new, *payloads)
    return (coarse_out, fine_out)


def solution(mesh):
    return jax.shard_map(
        step,
        mesh=mesh,
        in_specs=(
            P(None, "gx", "gy"),
            P(("gx", "gy"), None, None, None),
            P(("gx", "gy"), None),
            P(("gx", "gy")),
        ),
        out_specs=(P(None, "gx", "gy"), P(("gx", "gy"), None, None, None)),
        check_vma=False,
    )
```
